32 devices in a mesh: seq: 16 (over z, y, x), head: 2 (over core).
Axes of the slice: x: 2, y: 2, z: 4, core: 2. Of those that a mesh axis runs over, the one named last changes fastest.
Arguments:
- raw_keys: bfloat16 [2, 16384, 8, 128], P(None, 'seq', 'head'), may hold values from -6 to 6
- raw_values: bfloat16 [2, 16384, 8, 128], P(None, 'seq', 'head'), may hold values from -6 to 6
- phase: int32 [2], replicated, may hold values from 0 to 255, as said below
- ratio: int32 [2, 16], replicated, may hold values from 8 to 32, as said below
- resident_len: int32 [2, 16], replicated, may hold values from 1 to 256, as said below
- beacon_queries: bfloat16 [2, 2048, 8, 8, 128], P(None, 'seq', 'head'), may hold values from -150 to 150
- beacon_wk: bfloat16 [8192, 1024], P('seq', 'head'), may hold values from -0.125 to 0.125
- beacon_wv: bfloat16 [8192, 1024], P('seq', 'head'), may hold values from -0.125 to 0.125
- resident_keys: bfloat16 [2, 4096, 8, 128], P(None, 'seq', 'head'), may hold values from -6 to 6
- resident_values: bfloat16 [2, 4096, 8, 128], P(None, 'seq', 'head'), may hold values from -6 to 6
- decode_queries: bfloat16 [4, 2, 8, 8, 128], P(None, None, 'head'), may hold values from -150 to 150
- out_weight: bfloat16 [8192, 8192], P('head', 'seq'), may hold values from -0.0625 to 0.0625
Outputs:
- beacon_keys: bfloat16 [2, 2048, 8, 128], P(None, 'seq', 'head')
- beacon_values: bfloat16 [2, 2048, 8, 128], P(None, 'seq', 'head')
- projected: bfloat16 [4, 2, 8192], P(None, None, 'seq')
The draws below stay inside these ranges and needn't reach their ends.
Inputs may be any that keep to these rules, and one draw needn't show every extreme that they name: `phase`: some request has 255. `ratio`: each value is 1024 // 128 times 1, 2 or 4; both ends occur. `resident_len`: some pair has 256.
All inputs are finite; a program needn't handle non-finite values.
Results may differ from the reference program's by a relative error of at most 0.025.
Values may be sent and summed in bfloat16 or wider, within the bound.
A program may use at most 64 MiB of HBM per device.

```python
import math
import jax
import jax.numpy as jnp
from jax import lax

KVH = 8
G = 8
HD = 128
D = 8192
INTERVAL = 1024
NB = 128
OFF = 256
REQ = 2
RES_DEV = 256
STEPS = 4
N_SEQ = 16


def draw_phase(key, part):
    base = jax.random.randint(key, (REQ,), 0, OFF)
    chosen = jax.random.randint(jax.random.fold_in(key, 7), (), 0, REQ)
    return jnp.where(jnp.arange(REQ) == chosen, OFF - 1, base).astype(jnp.int32)


def draw_ratio(key, part):
    power = jax.random.randint(key, (REQ, N_SEQ), 0, 3)
    flat_ids = jnp.arange(REQ * N_SEQ).reshape(REQ, N_SEQ)
    chosen = jax.random.randint(jax.random.fold_in(key, 3), (), 0, REQ * N_SEQ)
    power = jnp.where(flat_ids == chosen, 0, power)
    power = jnp.where(flat_ids == (chosen + 1) % (REQ * N_SEQ), 2, power)
    factor = jnp.where(power == 0, 1, jnp.where(power == 1, 2, 4))
    return (INTERVAL // NB * factor).astype(jnp.int32)


def draw_resident_len(key, part):
    base = jax.random.randint(key, (REQ, N_SEQ), 1, RES_DEV + 1)
    flat_ids = jnp.arange(REQ * N_SEQ).reshape(REQ, N_SEQ)
    chosen = jax.random.randint(jax.random.fold_in(key, 5), (), 0, REQ * N_SEQ)
    return jnp.where(flat_ids == chosen, RES_DEV, base).astype(jnp.int32)


def anchor_rows(key):
    anchors = jax.random.normal(jax.random.fold_in(key, 41), (REQ, N_SEQ, KVH, HD), jnp.float32)
    length = jnp.sqrt(jnp.sum(anchors * anchors, axis=-1, keepdims=True))
    anchors = anchors * (math.sqrt(HD) / length)
    return jnp.clip(anchors, -6.0, 6.0).astype(jnp.bfloat16).astype(jnp.float32)


def draw_resident_keys(key, part):
    whole = jax.random.normal(jax.random.fold_in(key, 42), (REQ, N_SEQ, RES_DEV, KVH, HD), jnp.float32)
    whole = jnp.clip(whole, -6.0, 6.0)
    whole = whole.at[:, :, 0].set(anchor_rows(key))
    return whole.reshape(REQ, N_SEQ * RES_DEV, KVH, HD).astype(jnp.bfloat16)


def draw_beacon_queries(key, part):
    inner = jax.random.fold_in(key, 21)
    shape = (REQ, N_SEQ * NB, KVH, G, HD)
    base = jax.random.normal(inner, shape, jnp.float32)
    return jnp.clip(2.0 * base, -12.0, 12.0).astype(jnp.bfloat16)


def draw_decode_queries(key, part):
    inner = jax.random.fold_in(key, 22)
    shape = (STEPS, REQ, KVH, G, HD)
    base = jax.random.normal(inner, shape, jnp.float32)
    return jnp.clip(2.5 * base, -12.0, 12.0).astype(jnp.bfloat16)


def steps_of(own_key, shape, split, smallest, high):
    level, own = 1.0, jax.random.fold_in(own_key, 6)
    for axis_at, shards_of in split:
        draws = jnp.exp(jax.random.uniform(jax.random.fold_in(own, axis_at), (shards_of,), jnp.float32, smallest / len(split), high / len(split)))
        level = level * jnp.repeat(draws, shape[axis_at] // shards_of).reshape([-1 if axis == axis_at else 1 for axis in range(len(shape))])
    return level


def noise(own_key, shape, spread, bound, pieces=(), kind=jnp.bfloat16):
    array = spread * jax.random.normal(own_key, shape, jnp.float32)
    if pieces:
        array = array * steps_of(own_key, shape, pieces, -0.22, 0.18)
    return jnp.clip(array, -bound, bound).astype(kind)


def setup_inputs(seed: int = 0) -> dict:
    key_list = jax.random.split(jax.random.key(seed), 13)
    raw_keys = noise(key_list[0], (REQ, INTERVAL * N_SEQ, KVH, HD), 1.0, 6.0, ((1, 16), (2, 2)))
    raw_values = noise(key_list[1], (REQ, INTERVAL * N_SEQ, KVH, HD), 1.0, 6.0, ((1, 16), (2, 2)))
    phase = draw_phase(jax.random.fold_in(key_list[12], 71), 0)
    ratio = draw_ratio(jax.random.fold_in(key_list[12], 71), 0)
    resident_len = draw_resident_len(jax.random.fold_in(key_list[12], 71), 0)
    beacon_queries = draw_beacon_queries(jax.random.fold_in(key_list[12], 71), 0)
    beacon_wk = noise(key_list[6], (D, KVH * HD), (D // 4) ** -0.5, 0.125, ((0, 16), (1, 2)))
    beacon_wv = noise(key_list[7], (D, KVH * HD), (D // 4) ** -0.5, 0.125, ((0, 16), (1, 2)))
    resident_keys = draw_resident_keys(jax.random.fold_in(key_list[12], 71), 0)
    resident_values = noise(key_list[9], (REQ, N_SEQ * RES_DEV, KVH, HD), 1.0, 6.0, ((1, 16), (2, 2)))
    decode_queries = draw_decode_queries(jax.random.fold_in(key_list[12], 71), 0)
    out_weight = noise(key_list[11], (D, D), D ** -0.5, 0.0625, ((0, 2), (1, 16)))
    return dict(raw_keys=raw_keys, raw_values=raw_values, phase=phase, ratio=ratio, resident_len=resident_len, beacon_queries=beacon_queries, beacon_wk=beacon_wk, beacon_wv=beacon_wv, resident_keys=resident_keys, resident_values=resident_values, decode_queries=decode_queries, out_weight=out_weight)


masked_score = -1e+30

def reference(raw_keys, raw_values, phase, ratio, resident_len, beacon_queries, beacon_wk, beacon_wv, resident_keys, resident_values, decode_queries, out_weight):
    requests = raw_keys.shape[0]
    heads = raw_keys.shape[2]
    inv_root = 1.0 / math.sqrt(HD)
    shaped_keys = raw_keys.reshape(requests, N_SEQ, INTERVAL, heads, HD)
    shaped_values = raw_values.reshape(requests, N_SEQ, INTERVAL, heads, HD)
    tails_k = shaped_keys[:, :, INTERVAL - OFF:]
    tails_v = shaped_values[:, :, INTERVAL - OFF:]
    near_keys = jnp.concatenate([jnp.zeros_like(tails_k[:, :1]), tails_k[:, :-1]], axis=1)
    near_values = jnp.concatenate([jnp.zeros_like(tails_v[:, :1]), tails_v[:, :-1]], axis=1)
    window_keys = jnp.moveaxis(jnp.concatenate([near_keys, shaped_keys], axis=2), 1, 0)
    window_values = jnp.moveaxis(jnp.concatenate([near_values, shaped_values], axis=2), 1, 0)
    queries = jnp.moveaxis(beacon_queries.reshape(requests, N_SEQ, NB, heads, G, HD), 1, 0)
    slot_ids = jnp.arange(NB, dtype=jnp.int32)
    row_ids = jnp.arange(OFF + INTERVAL, dtype=jnp.int32)
    key_map = beacon_wk.astype(jnp.float32)
    value_map = beacon_wv.astype(jnp.float32)

    def per_shard(members):
        shard_index, query_block, key_rows, value_rows, shard_ratio = members
        positions = row_ids[None, :] - OFF + phase[:, None]
        present = (shard_index > 0) | (positions >= phase[:, None])
        lead_in = jnp.where(shard_index == 0, phase, 0)
        reaches = (slot_ids[None, :] + 1) * shard_ratio[:, None] + lead_in[:, None]
        allowed = present[:, None, :] & (positions >= 0)[:, None, :] & (positions < INTERVAL)[:, None, :] & (positions[:, None, :] < reaches[:, :, None])
        scores = jnp.einsum('rjkgd,rikd->rjkgi', query_block.astype(jnp.float32), key_rows.astype(jnp.float32)) * inv_root
        cache_mask = allowed[:, :, None, None, :]
        row_peak = lax.optimization_barrier(jnp.max(jnp.where(cache_mask, scores, masked_score), axis=-1, keepdims=True))
        weights = jnp.where(cache_mask, jnp.exp(scores - row_peak), 0.0)
        weight_sum = lax.optimization_barrier(jnp.sum(weights, axis=-1))
        rounded = lax.optimization_barrier(weights.astype(jnp.bfloat16))
        weighted = jnp.einsum('rjkgi,rikd->rjkgd', rounded.astype(jnp.float32), value_rows.astype(jnp.float32))
        pooled = lax.optimization_barrier((weighted / weight_sum[..., None]).astype(jnp.bfloat16))
        pooled_flat = pooled.reshape(requests, NB, heads * G * HD).astype(jnp.float32)
        made_keys = jnp.einsum('rjx,xy->rjy', pooled_flat, key_map).reshape(requests, NB, heads, HD)
        made_values = jnp.einsum('rjx,xy->rjy', pooled_flat, value_map).reshape(requests, NB, heads, HD)
        slot_live = (slot_ids[None, :] < (INTERVAL // shard_ratio)[:, None])[:, :, None, None]
        return (jnp.where(slot_live, made_keys, 0.0).astype(jnp.bfloat16), jnp.where(slot_live, made_values, 0.0).astype(jnp.bfloat16))
    made_k, made_v = lax.map(per_shard, (jnp.arange(N_SEQ, dtype=jnp.int32), queries, window_keys, window_values, jnp.transpose(ratio)))
    beacon_keys = jnp.moveaxis(made_k, 0, 1).reshape(requests, N_SEQ * NB, heads, HD)
    beacon_values = jnp.moveaxis(made_v, 0, 1).reshape(requests, N_SEQ * NB, heads, HD)
    leftover_keys = shaped_keys[:, N_SEQ - 1, INTERVAL - OFF:]
    leftover_values = shaped_values[:, N_SEQ - 1, INTERVAL - OFF:]
    cache_keys = jnp.concatenate([resident_keys, beacon_keys, leftover_keys], axis=1)
    cache_values = jnp.concatenate([resident_values, beacon_values, leftover_values], axis=1)
    resident_ok = (jnp.arange(RES_DEV, dtype=jnp.int32)[None, None, :] < resident_len[:, :, None]).reshape(requests, N_SEQ * RES_DEV)
    beacon_ok = (slot_ids[None, None, :] < (INTERVAL // ratio)[:, :, None]).reshape(requests, N_SEQ * NB)
    leftover_ok = jnp.arange(OFF, dtype=jnp.int32)[None, :] >= OFF - phase[:, None]
    usable = jnp.concatenate([resident_ok, beacon_ok, leftover_ok], axis=1)
    scores = jnp.einsum('srkgd,rikd->rksgi', decode_queries.astype(jnp.float32), cache_keys.astype(jnp.float32)) * inv_root
    cache_mask = usable[:, None, None, None, :]
    row_peak = lax.optimization_barrier(jnp.max(jnp.where(cache_mask, scores, masked_score), axis=-1, keepdims=True))
    weights = jnp.where(cache_mask, jnp.exp(scores - row_peak), 0.0)
    weight_sum = lax.optimization_barrier(jnp.sum(weights, axis=-1))
    rounded = lax.optimization_barrier(weights.astype(jnp.bfloat16))
    weighted = jnp.einsum('rksgi,rikd->rksgd', rounded.astype(jnp.float32), cache_values.astype(jnp.float32))
    attended = (weighted / weight_sum[..., None]).astype(jnp.bfloat16)
    attended = jnp.transpose(attended, (2, 0, 1, 3, 4)).reshape(STEPS * requests, D)
    projected = jnp.dot(attended, out_weight, preferred_element_type=jnp.float32).astype(jnp.bfloat16)
    return (beacon_keys, beacon_values, projected.reshape(STEPS, requests, D))
```

```python
import contextlib
import functools
import math

import jax
import jax.numpy as jnp
from jax import lax
from jax.experimental import pallas as pl
from jax.experimental.pallas import tpu as pltpu
from jax.sharding import PartitionSpec as P

G = 8
INTERVAL = 1024
NB = 128
OFF = 256
STEPS = 4


masked_score = -1e30


def region(name):
    return contextlib.nullcontext()


def shifted(value, axis, steps):
    count = lax.axis_size(axis)
    first, last = (max(0, -steps), min(count, count - steps))
    return lax.ppermute(value, axis, [(source, source + steps) for source in range(first, last)])


def joined(shard, axis, combine):
    everything = jax.tree.map(lambda part: lax.all_gather(part, axis), shard)
    first = jax.tree.map(lambda part: part[0], everything)

    def hop(k, so_far):
        return combine(so_far, jax.tree.map(lambda part: part[k], everything))

    return lax.fori_loop(1, lax.axis_size(axis), hop, first)


def blend(former, latter):
    row_peak = jnp.maximum(former[0], latter[0])
    former_scale = jnp.exp(former[0] - row_peak)
    latter_scale = jnp.exp(latter[0] - row_peak)
    weight_sum = former[1] * former_scale + latter[1] * latter_scale
    weighted = former[2] * former_scale[..., None] + latter[2] * latter_scale[..., None]
    return (row_peak, weight_sum, weighted)


def pool_part(queries, key_rows, value_rows, positions, present, reaches):
    inv_root = 1.0 / math.sqrt(queries.shape[-1])

    def per_request(members):
        query_block, key_block, value_block, position_row, present_row, reach_row = members
        scores = (
            jnp.einsum("jkgd,ikd->jkgi", query_block, key_block, preferred_element_type=jnp.float32)
            * inv_root
        )
        allowed = (
            present_row[None, :]
            & (position_row[None, :] >= 0)
            & (position_row[None, :] < INTERVAL)
            & (position_row[None, :] < reach_row[:, None])
        )
        cache_mask = allowed[:, None, None, :]
        row_peak = jnp.max(jnp.where(cache_mask, scores, masked_score), axis=-1)
        weights = jnp.where(cache_mask, jnp.exp(scores - row_peak[..., None]), 0.0)
        weight_sum = jnp.sum(weights, axis=-1)
        weighted = jnp.einsum(
            "jkgi,ikd->jkgd",
            weights.astype(jnp.bfloat16),
            value_block,
            preferred_element_type=jnp.float32,
        )
        return (row_peak, weight_sum, weighted)

    return lax.map(per_request, (queries, key_rows, value_rows, positions, present, reaches))


def body(
    raw_keys,
    raw_values,
    phase,
    ratio,
    resident_len,
    beacon_queries,
    beacon_wk,
    beacon_wv,
    resident_keys,
    resident_values,
    decode_queries,
    out_weight,
):
    requests = raw_keys.shape[0]
    kv_local = raw_keys.shape[2]
    head_dim = raw_keys.shape[3]
    shard_index = lax.axis_index("seq")
    shard_count = lax.axis_size("seq")
    is_first = shard_index == 0
    is_last = shard_index == shard_count - 1
    own_ratio = lax.dynamic_index_in_dim(ratio, shard_index, 1, keepdims=False)
    slot_ids = jnp.arange(NB, dtype=jnp.int32)
    lead_in = jnp.where(is_first, phase, 0)
    reaches = (slot_ids[None, :] + 1) * own_ratio[:, None] + lead_in[:, None]
    tail_keys = raw_keys[:, INTERVAL - OFF :]
    tail_values = raw_values[:, INTERVAL - OFF :]
    own_positions = jnp.arange(INTERVAL, dtype=jnp.int32)[None, :] + phase[:, None]
    rim_ids = jnp.arange(OFF, dtype=jnp.int32)
    rim_positions = rim_ids[None, :] - OFF + phase[:, None]
    near_keys, near_values = shifted((tail_keys, tail_values), "seq", 1)
    key_rows = jnp.concatenate([near_keys, raw_keys], axis=1)
    value_rows = jnp.concatenate([near_values, raw_values], axis=1)
    positions = jnp.concatenate([rim_positions, own_positions], axis=1)
    present = jnp.logical_not(is_first) | (positions >= phase[:, None])
    pooled_parts = pool_part(beacon_queries, key_rows, value_rows, positions, present, reaches)
    pooled = (pooled_parts[2] / pooled_parts[1][..., None]).astype(jnp.bfloat16)
    pooled_flat = pooled.reshape(requests * NB, kv_local * G * head_dim)
    pooled_whole = lax.all_gather(pooled_flat, "head", axis=1, tiled=True)
    key_sum = jnp.dot(
        pooled_whole,
        lax.all_gather(beacon_wk, "seq", axis=0, tiled=True),
        preferred_element_type=jnp.float32,
    )
    value_sum = jnp.dot(
        pooled_whole,
        lax.all_gather(beacon_wv, "seq", axis=0, tiled=True),
        preferred_element_type=jnp.float32,
    )
    made_keys = key_sum
    made_values = value_sum
    made_keys = made_keys.reshape(requests, NB, kv_local, head_dim)
    made_values = made_values.reshape(requests, NB, kv_local, head_dim)
    slot_live = slot_ids[None, :] < (INTERVAL // own_ratio)[:, None]
    beacon_keys = jnp.where(slot_live[:, :, None, None], made_keys, 0.0).astype(jnp.bfloat16)
    beacon_values = jnp.where(slot_live[:, :, None, None], made_values, 0.0).astype(jnp.bfloat16)
    cache_keys = jnp.concatenate([resident_keys, beacon_keys, tail_keys], axis=1)
    cache_values = jnp.concatenate([resident_values, beacon_values, tail_values], axis=1)
    own_len = lax.dynamic_index_in_dim(resident_len, shard_index, 1, keepdims=False)
    resident_ok = jnp.arange(resident_keys.shape[1], dtype=jnp.int32)[None, :] < own_len[:, None]
    leftover_ok = (rim_ids[None, :] >= OFF - phase[:, None]) & is_last
    usable = jnp.concatenate([resident_ok, slot_live, leftover_ok], axis=1)
    inv_root = 1.0 / math.sqrt(head_dim)
    scores = (
        jnp.einsum(
            "srkgd,rikd->rksgi", decode_queries, cache_keys, preferred_element_type=jnp.float32
        )
        * inv_root
    )
    cache_mask = usable[:, None, None, None, :]
    row_peak = jnp.max(jnp.where(cache_mask, scores, masked_score), axis=-1)
    weights = jnp.where(cache_mask, jnp.exp(scores - row_peak[..., None]), 0.0)
    weight_sum = jnp.sum(weights, axis=-1)
    weighted = jnp.einsum(
        "rksgi,rikd->rksgd",
        weights.astype(jnp.bfloat16),
        cache_values,
        preferred_element_type=jnp.float32,
    )
    merged = joined((row_peak, weight_sum, weighted), "seq", blend)
    total_sum = merged[1]
    total_weighted = merged[2]
    attended = (total_weighted / total_sum[..., None]).astype(jnp.bfloat16)
    attended = jnp.transpose(attended, (2, 0, 1, 3, 4)).reshape(
        STEPS * requests, kv_local * G * head_dim
    )
    partial_value = jnp.dot(attended, out_weight, preferred_element_type=jnp.float32)
    summed = lax.psum(partial_value, "head")
    projected = summed.astype(jnp.bfloat16).reshape(STEPS, requests, out_weight.shape[1])
    return (beacon_keys, beacon_values, projected)


B = 4
CH = 4


def fused_kernel(
    shard_count,
    phase_ref,
    ratio_ref,
    rlen_ref,
    k_hbm,
    v_hbm,
    q_hbm,
    wk_hbm,
    wv_hbm,
    rk_hbm,
    rv_hbm,
    dq_hbm,
    ow_hbm,
    bk_out,
    bv_out,
    proj_ref,
    kraw,
    vraw,
    qraw,
    rkraw,
    rvraw,
    dqraw,
    rimraw,
    rimrel,
    kbuf,
    vbuf,
    qbuf,
    wbuf,
    act,
    stage,
    psend,
    precv,
    own,
    bias,
    owbuf,
    rk_ref,
    rv_ref,
    dq_ref,
    bk_ref,
    bv_ref,
    snd,
    snd_stats,
    rcv,
    rcv_stats,
    att,
    part,
    load_sem,
    rim_send,
    rim_recv,
    rel_send,
    rel_recv,
    w_send,
    w_recv,
    a_send,
    a_recv,
    a_loc,
    p_send,
    p_recv,
    s_send,
    s_recv,
    d_send,
    d_recv,
    e_send,
    e_recv,
    t_send,
    t_recv,
    h_send,
    h_recv,
):
    n = shard_count
    depth = n // B
    s = lax.axis_index("seq")
    h = lax.axis_index("head")
    z = s // B
    me = lax.rem(s, B)
    requests, interval, heads, hd = kraw.shape
    rows = interval + OFF
    nb = bias.shape[1]
    width = wbuf.shape[3]
    inv_root = 1.0 / math.sqrt(hd)
    f32 = jnp.float32
    bf16 = jnp.bfloat16

    def remote(src, dst, send, recv, seq=None):
        target = {"head": 1 - h} if seq is None else {"seq": seq}
        return pltpu.make_async_remote_copy(
            src_ref=src,
            dst_ref=dst,
            send_sem=send,
            recv_sem=recv,
            device_id=target,
            device_id_type=pl.DeviceIdType.MESH,
        )

    loads = []

    def load(source, target):
        loads.append(pltpu.make_async_copy(source, target, load_sem.at[len(loads)]))
        loads[-1].start()
        return loads[-1]

    half = wk_hbm.shape[1] // (CH // 2)
    w_load = []
    for c in range(CH):
        source = (wk_hbm, wv_hbm)[c // (CH // 2)]
        first = (c % (CH // 2)) * half
        w_load.append(load(source.at[:, first : first + half], wbuf.at[z, c]))
    kv_load = [
        load((k_hbm, v_hbm)[p % 2].at[p // 2], (kraw, vraw)[p % 2].at[p // 2])
        for p in range(2 * requests)
    ]
    q_load = load(q_hbm, qraw)
    rest_load = [load(rk_hbm, rkraw), load(rv_hbm, rvraw), load(dq_hbm, dqraw)]
    ow_load = load(ow_hbm, owbuf)

    with region("barrier"):
        barrier = pltpu.get_barrier_semaphore()
        for o in range(1, n):
            pl.semaphore_signal(
                barrier,
                inc=1,
                device_id={"seq": lax.rem(s + o, n)},
                device_id_type=pl.DeviceIdType.MESH,
            )
        pl.semaphore_signal(
            barrier, inc=1, device_id={"head": 1 - h}, device_id_type=pl.DeviceIdType.MESH
        )
        pl.semaphore_wait(barrier, n)

    crosses = (me == B - 1) & (z < depth - 1)
    relays = (me < B - 1) & (z < depth - 1)

    def rim_near(p):
        source = (k_hbm, v_hbm)[p % 2].at[p // 2, interval - OFF :]
        return remote(source, rimraw.at[p], rim_send.at[p], rim_recv.at[p], lax.rem(s + 1, n))

    def rim_far(p):
        source = (k_hbm, v_hbm)[p % 2].at[p // 2, interval - OFF :]
        return remote(source, rimrel, rim_send.at[p], rel_recv, z * B + B - 1 - p)

    def rim_pass():
        p = B - 1 - me
        return remote(rimrel, rimraw.at[p], rel_send, rim_recv.at[p], lax.rem((z + 1) * B, n))

    @pl.when(me < B - 1)
    def _():
        for p in range(2 * requests):
            rim_near(p).start()

    @pl.when(crosses)
    def _():
        rim_near(0).start()
        for p in range(1, 2 * requests):
            rim_far(p).start()

    def w_copy(way, d, c, shard, target):
        return remote(
            wbuf.at[shard, c],
            wbuf.at[shard, c],
            w_send.at[way, d, c],
            w_recv.at[way, d, c],
            target * B + me,
        )

    def w_out(way, d):
        if way == 0:
            return z - d, z + 1, (z - d >= 0) & (z + 1 < depth)
        return z + d, z - 1, (z + d < depth) & (z - 1 >= 0)

    def w_in(way, d):
        if way == 0:
            return z - 1 - d, z - 1 - d >= 0
        return z + 1 + d, z + 1 + d < depth

    def w_own(c):
        w_load[c].wait()
        for way in range(2):
            shard, target, there = w_out(way, 0)

            @pl.when(there)
            def _(way=way, shard=shard, target=target):
                w_copy(way, 0, c, shard, target).start()

    def w_relay(d, c):
        for way in range(2):
            shard, target, onward = w_out(way, d)

            @pl.when(onward)
            def _(way=way, shard=shard, target=target):
                w_copy(way, d - 1, c, shard, z).wait_recv()
                w_copy(way, d, c, shard, target).start()

    def w_wait(c):
        for way in range(2):
            for d in range(depth - 1):
                shard, there = w_in(way, d)
                if d < depth - 2:
                    there = there & ((z == depth - 1) if way == 0 else (z == 0))

                @pl.when(there)
                def _(way=way, d=d, shard=shard):
                    w_copy(way, d, c, shard, z).wait_recv()

    with region("w_own"):
        for c in range(CH):
            w_own(c)

    with region("prep"):
        for r in range(requests):
            slot = lax.broadcasted_iota(jnp.int32, (nb, rows), 0)
            position = lax.broadcasted_iota(jnp.int32, (nb, rows), 1) - OFF + phase_ref[r]
            lead = jnp.where(s == 0, phase_ref[r], 0)
            reach = (slot + 1) * ratio_ref[r, s] + lead
            allowed = (position >= lead) & (position < interval) & (position < reach)
            bias[r] = jnp.where(allowed, 0.0, masked_score).astype(f32)
        for p in range(2 * requests):
            kv_load[p].wait()
            (kbuf, vbuf)[p % 2][p // 2, :, OFF:] = jnp.swapaxes((kraw, vraw)[p % 2][p // 2], 0, 1)
        for copy in rest_load:
            copy.wait()
        for r in range(requests):
            rk_ref[r] = jnp.swapaxes(rkraw[r], 0, 1)
            rv_ref[r] = jnp.swapaxes(rvraw[r], 0, 1)
        steps = dqraw.shape[0]
        pair = steps * requests
        for k in range(heads):
            asked = jnp.stack(
                [dqraw[t, r, k].astype(f32) for t in range(steps) for r in range(requests)], axis=0
            )
            dq_ref[k] = jnp.swapaxes(asked, 0, 1).reshape(G * pair, hd).astype(bf16)
        q_load.wait()

    @pl.when(relays)
    def _():
        with region("rimpass"):
            remote(rimrel, rimrel, rel_send, rel_recv, s).wait_recv()
            rim_pass().start()

    @pl.when(s == 0)
    def _():
        kbuf[:, :, :OFF] = jnp.zeros((requests, heads, OFF, hd), kbuf.dtype)
        vbuf[:, :, :OFF] = jnp.zeros((requests, heads, OFF, hd), vbuf.dtype)

    def a_remote(v, x):
        kk, r, y = v // 4, lax.rem(v, 2), lax.rem(v // 2, 2)
        return remote(
            stage.at[v, x],
            act.at[h * 2 + kk, r, me],
            a_send.at[v, x],
            a_recv.at[kk, r, me],
            z * B + y * 2 + x,
        )

    def a_local(kk, r, v):
        return pltpu.make_async_copy(
            stage.at[v, lax.rem(me, 2)], act.at[h * 2 + kk, r, me], a_loc.at[kk, r]
        )

    def a_relay(kk, r):
        return remote(
            act.at[h * 2 + kk, r], act.at[h * 2 + kk, r], p_send.at[kk, r], p_recv.at[kk, r]
        )

    def a_gather(kk, r):
        a_local(kk, r, kk * 4 + (me // 2) * 2 + r).wait()
        for o in range(1, B):
            source = lax.rem(me + o, B)
            remote(
                stage.at[0, 0],
                act.at[h * 2 + kk, r, source],
                a_send.at[0, 0],
                a_recv.at[kk, r, source],
                s,
            ).wait_recv()
        a_relay(kk, r).start()

    def unit(u, carry):
        r, k = u // heads, lax.rem(u, heads)
        v = k * 2 + r

        @pl.when((k == 0) & (s > 0))
        def _():
            with region("rimwait"):
                for which in range(2):
                    p = r * 2 + which
                    remote(rimraw.at[p], rimraw.at[p], rim_send.at[p], rim_recv.at[p], s).wait_recv()
            kbuf[r, :, :OFF] = jnp.swapaxes(rimraw[r * 2], 0, 1)
            vbuf[r, :, :OFF] = jnp.swapaxes(rimraw[r * 2 + 1], 0, 1)

        with region("att"):
            qbuf[...] = jnp.swapaxes(qraw[r, :, k], 0, 1)
            for g in range(G):
                scores = (
                    lax.dot_general(
                        qbuf[g],
                        kbuf[r, k],
                        (((1,), (1,)), ((), ())),
                        preferred_element_type=f32,
                    )
                    * inv_root
                    + bias[r]
                )
                weights = jnp.exp(scores - jnp.max(scores, axis=-1, keepdims=True))
                total = jnp.sum(weights, axis=-1, keepdims=True)
                out = jnp.dot(weights.astype(bf16), vbuf[r, k], preferred_element_type=f32)
                at = (g % 4) * hd
                stage[v, g // 4, :, at : at + hd] = (out / total).astype(bf16)
        for x in range(2):
            member = lax.rem(k, 2) * 2 + x

            @pl.when(member == me)
            def _():
                a_local(k // 2, r, v).start()

            @pl.when(member != me)
            def _(x=x):
                a_remote(v, x).start()

        with region("relay"):

            @pl.when(u < CH)
            def _():
                w_relay(1, u)

            @pl.when(u >= 2 * heads - CH + 1)
            def _():
                w_relay(2, u - (2 * heads - CH + 1))

            @pl.when(u == heads + 1)
            def _():
                a_gather(0, 0)

            @pl.when(u == heads + 3)
            def _():
                a_gather(1, 0)

        return carry

    lax.fori_loop(0, 2 * heads, unit, 0)
    with region("gather"):
        a_gather(0, 1)
        w_relay(2, CH - 1)
        a_gather(1, 1)
        for kk in range(2):
            for r in range(requests):
                a_relay(kk, r).wait_recv()

    def p_copy(c, to, frm):
        return remote(
            psend.at[to, c], precv.at[frm, c], s_send.at[to, c], s_recv.at[frm, c], z * B + to
        )

    slot_row = lax.broadcasted_iota(jnp.int32, (nb, width), 0)

    def finish(c):
        with region("finish"):
            for o in range(1, B):
                source = lax.rem(me + o, B)
                p_copy(c, source, source).wait_recv()
        total = own[c]
        for o in range(1, B):
            total += precv[lax.rem(me + o, B), c].astype(f32)
        out_ref = (bk_ref, bv_ref)[c // (CH // 2)]
        at = (c % (CH // 2)) * width
        for r in range(requests):
            live = (slot_row + 1) * ratio_ref[r, s] <= interval
            out_ref[r * nb : (r + 1) * nb, at : at + width] = jnp.where(
                live, total[r * nb : (r + 1) * nb], 0.0
            ).astype(bf16)

    for c in range(CH):
        with region(f"wwait{c}"):
            w_wait(c)

        def product(o, carry, c=c):
            to = lax.rem(me + 1 + o, B)
            total = jnp.zeros((requests * nb, width), f32)
            for zi in range(depth):
                total += jnp.dot(
                    act[zi, :, to].reshape(requests * nb, act.shape[4]),
                    wbuf[zi, c],
                    preferred_element_type=f32,
                )

            @pl.when(o < B - 1)
            def _():
                psend[to, c] = total.astype(bf16)
                p_copy(c, to, me).start()

            @pl.when(o == B - 1)
            def _():
                own[c] = total

            return carry

        with region("prod"):
            lax.fori_loop(0, B, product, 0)
        if c > 0:
            finish(c - 1)
    finish(CH - 1)

    res = rk_ref.shape[2]
    qrows = dq_ref.shape[1]
    cells = res + nb + OFF
    row_request = lax.rem(lax.broadcasted_iota(jnp.int32, (qrows, cells), 0), requests)
    cell = lax.broadcasted_iota(jnp.int32, (qrows, cells), 1)
    last = jnp.where(s == n - 1, 1, 0)
    share = G * heads // n
    with region("decode"):
        masks = []
        for r in range(requests):
            usable = (
                (cell < rlen_ref[r, s])
                | (
                    (cell >= res)
                    & (cell < res + nb)
                    & ((cell - res + 1) * ratio_ref[r, s] <= interval)
                )
                | ((cell >= res + nb + OFF - phase_ref[r] * last) & (cell >= res + nb))
            )
            masks.append(usable & (row_request == r))
        for k in range(heads):
            lanes = slice(k * hd, (k + 1) * hd)
            pieces = []
            for r in range(requests):
                keys = (
                    rk_ref[r, k],
                    bk_ref[r * nb : (r + 1) * nb, lanes],
                    kbuf[r, k, rows - OFF :],
                )
                scores = jnp.concatenate(
                    [
                        lax.dot_general(
                            dq_ref[k], key, (((1,), (1,)), ((), ())), preferred_element_type=f32
                        )
                        for key in keys
                    ],
                    axis=1,
                )
                pieces.append(jnp.where(masks[r], scores * inv_root, masked_score))
            peak = jnp.maximum(
                jnp.max(pieces[0], axis=-1, keepdims=True),
                jnp.max(pieces[1], axis=-1, keepdims=True),
            )
            total = jnp.zeros((qrows, 1), f32)
            out = jnp.zeros((qrows, hd), f32)
            for r in range(requests):
                weights = jnp.exp(pieces[r] - peak)
                total += jnp.sum(weights, axis=-1, keepdims=True)
                low = weights.astype(bf16)
                out += jnp.dot(low[:, :res], rv_ref[r, k], preferred_element_type=f32)
                out += jnp.dot(
                    low[:, res : res + nb],
                    bv_ref[r * nb : (r + 1) * nb, lanes],
                    preferred_element_type=f32,
                )
                out += jnp.dot(
                    low[:, res + nb :], vbuf[r, k, rows - OFF :], preferred_element_type=f32
                )
            lane = lax.broadcasted_iota(jnp.int32, (qrows, hd), 1)
            slots = hd // (2 * share)
            stats = jnp.where(lax.rem(lane // slots, 2) == 0, peak, total)
            stats = stats.reshape(G // share, share, pair, hd)
            lane = lax.broadcasted_iota(jnp.int32, (G // share, pair, hd), 2)
            packed = stats[:, 0]
            for j in range(1, share):
                packed = jnp.where(lane >= 2 * slots * j, stats[:, j], packed)
            dests = slice(k * G // share, (k + 1) * G // share)
            snd[dests] = out.reshape(G // share, share * pair, hd).astype(bf16)
            snd_stats[dests] = packed

    def d_copy(to, frm):
        return remote(snd.at[to], rcv.at[frm], d_send.at[to], d_recv.at[frm], to)

    def e_copy(to, frm):
        return remote(snd_stats.at[to], rcv_stats.at[frm], e_send.at[to], e_recv.at[frm], to)

    def t_copy(to, frm):
        return remote(att.at[frm], att.at[frm], t_send.at[to], t_recv.at[frm], to)

    for o in range(1, n):
        e_copy(lax.rem(s + o, n), s).start()
        d_copy(lax.rem(s + o, n), s).start()
    rcv[s] = snd[s]
    rcv_stats[s] = snd_stats[s]

    with region("outs"):
        for made, out_ref in ((bk_ref, bk_out), (bv_ref, bv_out)):
            by_head = jnp.stack([made[:, k * hd : (k + 1) * hd] for k in range(heads)], axis=0)
            out_ref[...] = jnp.swapaxes(by_head, 0, 1)

    with region("drain"):
        for c in range(CH):
            for o in range(1, B):
                p_copy(c, lax.rem(me + o, B), me).wait_send()
        for kk in range(2):
            for r in range(requests):
                a_relay(kk, r).wait_send()
        for v in range(2 * heads):
            for x in range(2):

                @pl.when((v // 2 % 2) * 2 + x != me)
                def _(v=v, x=x):
                    a_remote(jnp.int32(v), x).wait_send()

        for way in range(2):
            for d in range(depth - 1):
                shard, target, there = w_out(way, d)

                @pl.when(there)
                def _(way=way, d=d, shard=shard, target=target):
                    for c in range(CH):
                        w_copy(way, d, c, shard, target).wait_send()

        @pl.when(me < B - 1)
        def _():
            for p in range(2 * requests):
                rim_near(p).wait_send()

        @pl.when(crosses)
        def _():
            rim_near(0).wait_send()
            for p in range(1, 2 * requests):
                rim_far(p).wait_send()

        @pl.when(relays)
        def _():
            rim_pass().wait_send()

    with region("dwait"):
        for o in range(1, n):
            source = lax.rem(s + o, n)
            e_copy(source, source).wait_recv()
            d_copy(source, source).wait_recv()
    landed = rcv[...].astype(f32)
    attended = []
    for j in range(share):
        at = 2 * slots * j
        peaks = rcv_stats[:, :, at : at + 1]
        sums = rcv_stats[:, :, at + slots : at + slots + 1]
        scale = jnp.exp(peaks - jnp.max(peaks, axis=0, keepdims=True))
        mixed = jnp.sum(scale * landed[:, j * pair : (j + 1) * pair], axis=0)
        attended.append(mixed / jnp.sum(scale * sums, axis=0))
    att[s] = jnp.concatenate(attended, axis=0).astype(bf16)
    for o in range(1, n):
        t_copy(lax.rem(s + o, n), s).start()
    ow_load.wait()
    with region("twait"):
        for o in range(1, n):
            d_copy(lax.rem(s + o, n), s).wait_send()
            e_copy(lax.rem(s + o, n), s).wait_send()
        for o in range(1, n):
            source = lax.rem(s + o, n)
            t_copy(source, source).wait_recv()
    wide = [att[i].astype(f32) for i in range(n)]
    vectors = jnp.concatenate(
        [wide[i][j * pair : (j + 1) * pair] for i in range(n) for j in range(share)], axis=1
    ).astype(bf16)
    with region("outproj"):
        partial_value = jnp.dot(vectors, owbuf[...], preferred_element_type=f32)
        part[0] = partial_value
    swap = remote(part.at[0], part.at[1], h_send, h_recv)
    swap.start()
    with region("swap"):
        for o in range(1, n):
            t_copy(lax.rem(s + o, n), s).wait_send()
        swap.wait_recv()
    first = jnp.where(h == 0, part[0], part[1])
    second = jnp.where(h == 0, part[1], part[0])
    summed = (first + second).astype(bf16)
    for t in range(steps):
        proj_ref[t] = summed[t * requests : (t + 1) * requests]
    swap.wait_send()


def fused_body(
    shard_count,
    raw_keys,
    raw_values,
    phase,
    ratio,
    resident_len,
    beacon_queries,
    beacon_wk,
    beacon_wv,
    resident_keys,
    resident_values,
    decode_queries,
    out_weight,
):
    n = shard_count
    depth = n // B
    requests, interval, heads, hd = raw_keys.shape
    steps = decode_queries.shape[0]
    nb = beacon_queries.shape[1]
    rows = interval + OFF
    res = resident_keys.shape[1]
    feature, columns = beacon_wk.shape
    width = 2 * columns // CH
    pair = requests * steps
    share = G * heads // n
    bf16, f32 = jnp.bfloat16, jnp.float32
    dma = pltpu.SemaphoreType.DMA
    smem = pl.BlockSpec(memory_space=pltpu.SMEM)
    anywhere = pl.BlockSpec(memory_space=pl.ANY)
    vmem = pl.BlockSpec(memory_space=pltpu.VMEM)
    keys, values, projected = pl.pallas_call(
        functools.partial(fused_kernel, n),
        out_shape=(
            jax.ShapeDtypeStruct((requests * nb, heads, hd), bf16),
            jax.ShapeDtypeStruct((requests * nb, heads, hd), bf16),
            jax.ShapeDtypeStruct((steps, requests, out_weight.shape[1]), bf16),
        ),
        in_specs=[smem] * 3 + [anywhere] * 9,
        out_specs=(vmem, vmem, vmem),
        scratch_shapes=[
            pltpu.VMEM(raw_keys.shape, bf16),
            pltpu.VMEM(raw_values.shape, bf16),
            pltpu.VMEM(beacon_queries.shape, bf16),
            pltpu.VMEM(resident_keys.shape, bf16),
            pltpu.VMEM(resident_values.shape, bf16),
            pltpu.VMEM(decode_queries.shape, bf16),
            pltpu.VMEM((2 * requests, OFF, heads, hd), bf16),
            pltpu.VMEM((OFF, heads, hd), bf16),
            pltpu.VMEM((requests, heads, rows, hd), bf16),
            pltpu.VMEM((requests, heads, rows, hd), bf16),
            pltpu.VMEM((G, nb, hd), bf16),
            pltpu.VMEM((depth, CH, feature, width), bf16),
            pltpu.VMEM((depth, requests, B, nb, feature), bf16),
            pltpu.VMEM((requests * heads, 2, nb, feature), bf16),
            pltpu.VMEM((B, CH, requests * nb, width), bf16),
            pltpu.VMEM((B, CH, requests * nb, width), bf16),
            pltpu.VMEM((CH, requests * nb, width), f32),
            pltpu.VMEM((requests, nb, rows), f32),
            pltpu.VMEM(out_weight.shape, bf16),
            pltpu.VMEM((requests, heads, res, hd), bf16),
            pltpu.VMEM((requests, heads, res, hd), bf16),
            pltpu.VMEM((heads, G * pair, hd), bf16),
            pltpu.VMEM((requests * nb, columns), bf16),
            pltpu.VMEM((requests * nb, columns), bf16),
            pltpu.VMEM((n, share * pair, hd), bf16),
            pltpu.VMEM((n, pair, hd), f32),
            pltpu.VMEM((n, share * pair, hd), bf16),
            pltpu.VMEM((n, pair, hd), f32),
            pltpu.VMEM((n, share * pair, hd), bf16),
            pltpu.VMEM((2, pair, out_weight.shape[1]), f32),
            dma((CH + 2 * requests + 5,)),
            dma((2 * requests,)),
            dma((2 * requests,)),
            dma,
            dma,
            dma((2, depth - 1, CH)),
            dma((2, depth - 1, CH)),
            dma((requests * heads, 2)),
            dma((2, requests, B)),
            dma((2, requests)),
            dma((2, requests)),
            dma((2, requests)),
            dma((B, CH)),
            dma((B, CH)),
            dma((n,)),
            dma((n,)),
            dma((n,)),
            dma((n,)),
            dma((n,)),
            dma((n,)),
            dma,
            dma,
        ],
        compiler_params=pltpu.CompilerParams(
            collective_id=0, has_side_effects=True, vmem_limit_bytes=60 * 1024 * 1024
        ),
    )(
        phase,
        ratio,
        resident_len,
        raw_keys,
        raw_values,
        beacon_queries,
        beacon_wk,
        beacon_wv,
        resident_keys,
        resident_values,
        decode_queries,
        out_weight,
    )
    return (
        keys.reshape(requests, nb, heads, hd),
        values.reshape(requests, nb, heads, hd),
        projected,
    )


def chosen_body(shard_count, head_count):
    def run(*arrays):
        requests, _, heads, hd = arrays[0].shape
        feature = arrays[6].shape[0]
        fits = (
            head_count == 2
            and shard_count == B * B
            and requests == 2
            and heads == B
            and 2 * feature == G * hd
        )
        return fused_body(shard_count, *arrays) if fits else body(*arrays)

    return run


def solution(mesh):
    return jax.shard_map(
        chosen_body(mesh.shape["seq"], mesh.shape["head"]),
        mesh=mesh,
        in_specs=(
            P(None, "seq", "head", None),
            P(None, "seq", "head", None),
            P(),
            P(),
            P(),
            P(None, "seq", "head", None, None),
            P("seq", "head"),
            P("seq", "head"),
            P(None, "seq", "head", None),
            P(None, "seq", "head", None),
            P(None, None, "head", None, None),
            P("head", "seq"),
        ),
        out_specs=(
            P(None, "seq", "head", None),
            P(None, "seq", "head", None),
            P(None, None, "seq"),
        ),
        check_vma=False,
    )
```

```python
import contextlib
import functools
import math

import jax
import jax.numpy as jnp
from jax import lax
from jax.experimental import pallas as pl
from jax.experimental.pallas import tpu as pltpu
from jax.sharding import PartitionSpec as P

G = 8
INTERVAL = 1024
NB = 128
OFF = 256
STEPS = 4


masked_score = -1e30


def region(name):
    return contextlib.nullcontext()


def shifted(value, axis, steps):
    count = lax.axis_size(axis)
    first, last = (max(0, -steps), min(count, count - steps))
    return lax.ppermute(value, axis, [(source, source + steps) for source in range(first, last)])


def joined(shard, axis, combine):
    everything = jax.tree.map(lambda part: lax.all_gather(part, axis), shard)
    first = jax.tree.map(lambda part: part[0], everything)

    def hop(k, so_far):
        return combine(so_far, jax.tree.map(lambda part: part[k], everything))

    return lax.fori_loop(1, lax.axis_size(axis), hop, first)


def blend(former, latter):
    row_peak = jnp.maximum(former[0], latter[0])
    former_scale = jnp.exp(former[0] - row_peak)
    latter_scale = jnp.exp(latter[0] - row_peak)
    weight_sum = former[1] * former_scale + latter[1] * latter_scale
    weighted = former[2] * former_scale[..., None] + latter[2] * latter_scale[..., None]
    return (row_peak, weight_sum, weighted)


def pool_part(queries, key_rows, value_rows, positions, present, reaches):
    inv_root = 1.0 / math.sqrt(queries.shape[-1])

    def per_request(members):
        query_block, key_block, value_block, position_row, present_row, reach_row = members
        scores = (
            jnp.einsum("jkgd,ikd->jkgi", query_block, key_block, preferred_element_type=jnp.float32)
            * inv_root
        )
        allowed = (
            present_row[None, :]
            & (position_row[None, :] >= 0)
            & (position_row[None, :] < INTERVAL)
            & (position_row[None, :] < reach_row[:, None])
        )
        cache_mask = allowed[:, None, None, :]
        row_peak = jnp.max(jnp.where(cache_mask, scores, masked_score), axis=-1)
        weights = jnp.where(cache_mask, jnp.exp(scores - row_peak[..., None]), 0.0)
        weight_sum = jnp.sum(weights, axis=-1)
        weighted = jnp.einsum(
            "jkgi,ikd->jkgd",
            weights.astype(jnp.bfloat16),
            value_block,
            preferred_element_type=jnp.float32,
        )
        return (row_peak, weight_sum, weighted)

    return lax.map(per_request, (queries, key_rows, value_rows, positions, present, reaches))


def body(
    raw_keys,
    raw_values,
    phase,
    ratio,
    resident_len,
    beacon_queries,
    beacon_wk,
    beacon_wv,
    resident_keys,
    resident_values,
    decode_queries,
    out_weight,
):
    requests = raw_keys.shape[0]
    kv_local = raw_keys.shape[2]
    head_dim = raw_keys.shape[3]
    shard_index = lax.axis_index("seq")
    shard_count = lax.axis_size("seq")
    is_first = shard_index == 0
    is_last = shard_index == shard_count - 1
    own_ratio = lax.dynamic_index_in_dim(ratio, shard_index, 1, keepdims=False)
    slot_ids = jnp.arange(NB, dtype=jnp.int32)
    lead_in = jnp.where(is_first, phase, 0)
    reaches = (slot_ids[None, :] + 1) * own_ratio[:, None] + lead_in[:, None]
    tail_keys = raw_keys[:, INTERVAL - OFF :]
    tail_values = raw_values[:, INTERVAL - OFF :]
    own_positions = jnp.arange(INTERVAL, dtype=jnp.int32)[None, :] + phase[:, None]
    rim_ids = jnp.arange(OFF, dtype=jnp.int32)
    rim_positions = rim_ids[None, :] - OFF + phase[:, None]
    near_keys, near_values = shifted((tail_keys, tail_values), "seq", 1)
    key_rows = jnp.concatenate([near_keys, raw_keys], axis=1)
    value_rows = jnp.concatenate([near_values, raw_values], axis=1)
    positions = jnp.concatenate([rim_positions, own_positions], axis=1)
    present = jnp.logical_not(is_first) | (positions >= phase[:, None])
    pooled_parts = pool_part(beacon_queries, key_rows, value_rows, positions, present, reaches)
    pooled = (pooled_parts[2] / pooled_parts[1][..., None]).astype(jnp.bfloat16)
    pooled_flat = pooled.reshape(requests * NB, kv_local * G * head_dim)
    pooled_whole = lax.all_gather(pooled_flat, "head", axis=1, tiled=True)
    key_sum = jnp.dot(
        pooled_whole,
        lax.all_gather(beacon_wk, "seq", axis=0, tiled=True),
        preferred_element_type=jnp.float32,
    )
    value_sum = jnp.dot(
        pooled_whole,
        lax.all_gather(beacon_wv, "seq", axis=0, tiled=True),
        preferred_element_type=jnp.float32,
    )
    made_keys = key_sum
    made_values = value_sum
    made_keys = made_keys.reshape(requests, NB, kv_local, head_dim)
    made_values = made_values.reshape(requests, NB, kv_local, head_dim)
    slot_live = slot_ids[None, :] < (INTERVAL // own_ratio)[:, None]
    beacon_keys = jnp.where(slot_live[:, :, None, None], made_keys, 0.0).astype(jnp.bfloat16)
    beacon_values = jnp.where(slot_live[:, :, None, None], made_values, 0.0).astype(jnp.bfloat16)
    cache_keys = jnp.concatenate([resident_keys, beacon_keys, tail_keys], axis=1)
    cache_values = jnp.concatenate([resident_values, beacon_values, tail_values], axis=1)
    own_len = lax.dynamic_index_in_dim(resident_len, shard_index, 1, keepdims=False)
    resident_ok = jnp.arange(resident_keys.shape[1], dtype=jnp.int32)[None, :] < own_len[:, None]
    leftover_ok = (rim_ids[None, :] >= OFF - phase[:, None]) & is_last
    usable = jnp.concatenate([resident_ok, slot_live, leftover_ok], axis=1)
    inv_root = 1.0 / math.sqrt(head_dim)
    scores = (
        jnp.einsum(
            "srkgd,rikd->rksgi", decode_queries, cache_keys, preferred_element_type=jnp.float32
        )
        * inv_root
    )
    cache_mask = usable[:, None, None, None, :]
    row_peak = jnp.max(jnp.where(cache_mask, scores, masked_score), axis=-1)
    weights = jnp.where(cache_mask, jnp.exp(scores - row_peak[..., None]), 0.0)
    weight_sum = jnp.sum(weights, axis=-1)
    weighted = jnp.einsum(
        "rksgi,rikd->rksgd",
        weights.astype(jnp.bfloat16),
        cache_values,
        preferred_element_type=jnp.float32,
    )
    merged = joined((row_peak, weight_sum, weighted), "seq", blend)
    total_sum = merged[1]
    total_weighted = merged[2]
    attended = (total_weighted / total_sum[..., None]).astype(jnp.bfloat16)
    attended = jnp.transpose(attended, (2, 0, 1, 3, 4)).reshape(
        STEPS * requests, kv_local * G * head_dim
    )
    partial_value = jnp.dot(attended, out_weight, preferred_element_type=jnp.float32)
    summed = lax.psum(partial_value, "head")
    projected = summed.astype(jnp.bfloat16).reshape(STEPS, requests, out_weight.shape[1])
    return (beacon_keys, beacon_values, projected)


B = 4
CH = 4


def fused_kernel(
    shard_count,
    phase_ref,
    ratio_ref,
    rlen_ref,
    k_hbm,
    v_hbm,
    q_hbm,
    wk_hbm,
    wv_hbm,
    rk_hbm,
    rv_hbm,
    dq_hbm,
    ow_hbm,
    bk_out,
    bv_out,
    proj_out,
    kraw,
    vraw,
    qraw,
    rkraw,
    rvraw,
    dqraw,
    rimraw,
    rimrel,
    kbuf,
    vbuf,
    qbuf,
    wbuf,
    act,
    stage,
    psend,
    precv,
    own,
    bias,
    owbuf,
    rk_ref,
    rv_ref,
    dq_ref,
    bk_ref,
    bv_ref,
    snd,
    snd_stats,
    rcv,
    rcv_stats,
    att,
    part,
    bk_rows,
    bv_rows,
    proj_rows,
    load_sem,
    out_sem,
    rim_send,
    rim_recv,
    rel_send,
    rel_recv,
    w_send,
    w_recv,
    a_send,
    a_recv,
    a_loc,
    p_send,
    p_recv,
    s_send,
    s_recv,
    d_send,
    d_recv,
    e_send,
    e_recv,
    t_send,
    t_recv,
    h_send,
    h_recv,
):
    n = shard_count
    depth = n // B
    s = lax.axis_index("seq")
    h = lax.axis_index("head")
    z = s // B
    me = lax.rem(s, B)
    requests, interval, heads, hd = kraw.shape
    rows = interval + OFF
    nb = bias.shape[1]
    width = wbuf.shape[3]
    inv_root = 1.0 / math.sqrt(hd)
    f32 = jnp.float32
    bf16 = jnp.bfloat16

    def remote(src, dst, send, recv, seq=None):
        target = {"head": 1 - h} if seq is None else {"seq": seq}
        return pltpu.make_async_remote_copy(
            src_ref=src,
            dst_ref=dst,
            send_sem=send,
            recv_sem=recv,
            device_id=target,
            device_id_type=pl.DeviceIdType.MESH,
        )

    loads = []

    def load(source, target):
        loads.append(pltpu.make_async_copy(source, target, load_sem.at[len(loads)]))
        loads[-1].start()
        return loads[-1]

    half = wk_hbm.shape[1] // (CH // 2)
    w_load = []
    for c in range(CH):
        source = (wk_hbm, wv_hbm)[c // (CH // 2)]
        first = (c % (CH // 2)) * half
        w_load.append(load(source.at[:, first : first + half], wbuf.at[z, c]))
    kv_load = [
        load((k_hbm, v_hbm)[p % 2].at[p // 2], (kraw, vraw)[p % 2].at[p // 2])
        for p in range(2 * requests)
    ]
    q_load = load(q_hbm, qraw)
    rest_load = [load(rk_hbm, rkraw), load(rv_hbm, rvraw), load(dq_hbm, dqraw)]
    ow_load = load(ow_hbm, owbuf)

    with region("barrier"):
        barrier = pltpu.get_barrier_semaphore()
        for o in range(1, n):
            pl.semaphore_signal(
                barrier,
                inc=1,
                device_id={"seq": lax.rem(s + o, n)},
                device_id_type=pl.DeviceIdType.MESH,
            )
        pl.semaphore_signal(
            barrier, inc=1, device_id={"head": 1 - h}, device_id_type=pl.DeviceIdType.MESH
        )
        pl.semaphore_wait(barrier, n)

    crosses = (me == B - 1) & (z < depth - 1)
    relays = (me < B - 1) & (z < depth - 1)

    def rim_near(p):
        source = (k_hbm, v_hbm)[p % 2].at[p // 2, interval - OFF :]
        return remote(source, rimraw.at[p], rim_send.at[p], rim_recv.at[p], lax.rem(s + 1, n))

    def rim_far(p):
        source = (k_hbm, v_hbm)[p % 2].at[p // 2, interval - OFF :]
        return remote(source, rimrel, rim_send.at[p], rel_recv, z * B + lax.rem(p, B - 1))

    def rim_pass():
        p = jnp.where(me == 0, B - 1, me)
        return remote(rimrel, rimraw.at[p], rel_send, rim_recv.at[p], lax.rem((z + 1) * B, n))

    @pl.when(me < B - 1)
    def _():
        for p in range(2 * requests):
            rim_near(p).start()

    @pl.when(crosses)
    def _():
        rim_near(0).start()
        for p in range(1, 2 * requests):
            rim_far(p).start()

    def w_copy(way, d, c, shard, target):
        return remote(
            wbuf.at[shard, c],
            wbuf.at[shard, c],
            w_send.at[way, d, c],
            w_recv.at[way, d, c],
            target * B + me,
        )

    def w_out(way, d):
        if way == 0:
            return z - d, z + 1, (z - d >= 0) & (z + 1 < depth)
        return z + d, z - 1, (z + d < depth) & (z - 1 >= 0)

    def w_in(way, d):
        if way == 0:
            return z - 1 - d, z - 1 - d >= 0
        return z + 1 + d, z + 1 + d < depth

    def w_own(c):
        w_load[c].wait()
        for way in range(2):
            shard, target, there = w_out(way, 0)

            @pl.when(there)
            def _(way=way, shard=shard, target=target):
                w_copy(way, 0, c, shard, target).start()

    def w_relay(d, c):
        for way in range(2):
            shard, target, onward = w_out(way, d)

            @pl.when(onward)
            def _(way=way, shard=shard, target=target):
                w_copy(way, d - 1, c, shard, z).wait_recv()
                w_copy(way, d, c, shard, target).start()

    def w_wait(c):
        for way in range(2):
            for d in range(depth - 1):
                shard, there = w_in(way, d)
                if d < depth - 2:
                    there = there & ((z == depth - 1) if way == 0 else (z == 0))

                @pl.when(there)
                def _(way=way, d=d, shard=shard):
                    w_copy(way, d, c, shard, z).wait_recv()

    def rim_relay():
        with region("rimpass"):
            remote(rimrel, rimrel, rel_send, rel_recv, s).wait_recv()
            rim_pass().start()

    w_own(0)

    @pl.when(me != 1)
    def _():
        w_own(1)

    @pl.when((me == 0) | (me == B - 1))
    def _():
        w_own(2)

    @pl.when(me == B - 1)
    def _():
        w_own(3)

    with region("prep"):
        for r in range(requests):
            slot = lax.broadcasted_iota(jnp.int32, (nb, rows), 0)
            position = lax.broadcasted_iota(jnp.int32, (nb, rows), 1) - OFF + phase_ref[r]
            lead = jnp.where(s == 0, phase_ref[r], 0)
            reach = (slot + 1) * ratio_ref[r, s] + lead
            allowed = (position >= lead) & (position < interval) & (position < reach)
            bias[r] = jnp.where(allowed, 0.0, masked_score).astype(f32)
        for p in range(2 * requests):
            kv_load[p].wait()
            (kbuf, vbuf)[p % 2][p // 2, :, OFF:] = jnp.swapaxes((kraw, vraw)[p % 2][p // 2], 0, 1)
        for copy in rest_load:
            copy.wait()
        for r in range(requests):
            rk_ref[r] = jnp.swapaxes(rkraw[r], 0, 1)
            rv_ref[r] = jnp.swapaxes(rvraw[r], 0, 1)
        steps = dqraw.shape[0]
        pair = steps * requests
        for k in range(heads):
            asked = jnp.stack(
                [dqraw[t, r, k].astype(f32) for t in range(steps) for r in range(requests)], axis=0
            )
            dq_ref[k] = jnp.swapaxes(asked, 0, 1).reshape(G * pair, hd).astype(bf16)
        q_load.wait()

    @pl.when(relays & (me != 0))
    def _():
        rim_relay()

    @pl.when(me == 1)
    def _():
        w_own(1)

    @pl.when((me == 1) | (me == 2))
    def _():
        w_own(2)
        w_own(3)

    @pl.when(s == 0)
    def _():
        kbuf[:, :, :OFF] = jnp.zeros((requests, heads, OFF, hd), kbuf.dtype)
        vbuf[:, :, :OFF] = jnp.zeros((requests, heads, OFF, hd), vbuf.dtype)

    def a_remote(v, x):
        kk, r, y = v // 4, lax.rem(v, 2), lax.rem(v // 2, 2)
        return remote(
            stage.at[v, x],
            act.at[h * 2 + kk, r, me],
            a_send.at[v, x],
            a_recv.at[kk, r, me],
            z * B + y * 2 + x,
        )

    def a_local(kk, r, v):
        return pltpu.make_async_copy(
            stage.at[v, lax.rem(me, 2)], act.at[h * 2 + kk, r, me], a_loc.at[kk, r]
        )

    def a_relay(kk, r):
        return remote(
            act.at[h * 2 + kk, r], act.at[h * 2 + kk, r], p_send.at[kk, r], p_recv.at[kk, r]
        )

    def a_gather(kk, r):
        a_local(kk, r, kk * 4 + (me // 2) * 2 + r).wait()
        for o in range(1, B):
            source = lax.rem(me + o, B)
            remote(
                stage.at[0, 0],
                act.at[h * 2 + kk, r, source],
                a_send.at[0, 0],
                a_recv.at[kk, r, source],
                s,
            ).wait_recv()
        a_relay(kk, r).start()

    def unit(u, carry):
        r, k = u // heads, lax.rem(u, heads)
        v = k * 2 + r

        @pl.when((k == 0) & (s > 0))
        def _():
            with region("rimwait"):
                for which in range(2):
                    p = r * 2 + which
                    remote(rimraw.at[p], rimraw.at[p], rim_send.at[p], rim_recv.at[p], s).wait_recv()
            kbuf[r, :, :OFF] = jnp.swapaxes(rimraw[r * 2], 0, 1)
            vbuf[r, :, :OFF] = jnp.swapaxes(rimraw[r * 2 + 1], 0, 1)

        with region("att"):
            qbuf[...] = jnp.swapaxes(qraw[r, :, k], 0, 1)
            for g in range(G):
                scores = (
                    lax.dot_general(
                        qbuf[g],
                        kbuf[r, k],
                        (((1,), (1,)), ((), ())),
                        preferred_element_type=f32,
                    )
                    * inv_root
                    + bias[r]
                )
                weights = jnp.exp(scores - jnp.max(scores, axis=-1, keepdims=True))
                total = jnp.sum(weights, axis=-1, keepdims=True)
                out = jnp.dot(weights.astype(bf16), vbuf[r, k], preferred_element_type=f32)
                at = (g % 4) * hd
                stage[v, g // 4, :, at : at + hd] = (out / total).astype(bf16)
        for x in range(2):
            member = lax.rem(k, 2) * 2 + x

            @pl.when(member == me)
            def _():
                a_local(k // 2, r, v).start()

            @pl.when(member != me)
            def _(x=x):
                a_remote(v, x).start()

        with region("relay"):

            @pl.when((u == 0) & (me == 0))
            def _():
                @pl.when(relays)
                def _():
                    rim_relay()

                w_own(3)

            @pl.when(u < CH)
            def _():
                w_relay(1, u)

            @pl.when(u >= 2 * heads - CH + 1)
            def _():
                w_relay(2, u - (2 * heads - CH + 1))

            @pl.when(u == heads + 1)
            def _():
                a_gather(0, 0)

            @pl.when(u == heads + 3)
            def _():
                a_gather(1, 0)

        return carry

    lax.fori_loop(0, 2 * heads, unit, 0)
    with region("gather"):
        a_gather(0, 1)
        w_relay(2, CH - 1)
        a_gather(1, 1)
        for kk in range(2):
            for r in range(requests):
                a_relay(kk, r).wait_recv()

    def p_copy(c, to, frm):
        return remote(
            psend.at[to, c], precv.at[frm, c], s_send.at[to, c], s_recv.at[frm, c], z * B + to
        )

    slot_row = lax.broadcasted_iota(jnp.int32, (nb, width), 0)

    def finish(c):
        with region("finish"):
            for o in range(1, B):
                source = lax.rem(me + o, B)
                p_copy(c, source, source).wait_recv()
        total = own[c]
        for o in range(1, B):
            total += precv[lax.rem(me + o, B), c].astype(f32)
        out_ref = (bk_ref, bv_ref)[c // (CH // 2)]
        at = (c % (CH // 2)) * width
        for r in range(requests):
            live = (slot_row + 1) * ratio_ref[r, s] <= interval
            out_ref[r * nb : (r + 1) * nb, at : at + width] = jnp.where(
                live, total[r * nb : (r + 1) * nb], 0.0
            ).astype(bf16)

    for c in range(CH):
        with region(f"wwait{c}"):
            w_wait(c)

        def product(o, carry, c=c):
            to = lax.rem(me + 1 + o, B)
            total = jnp.zeros((requests * nb, width), f32)
            for zi in range(depth):
                total += jnp.dot(
                    act[zi, :, to].reshape(requests * nb, act.shape[4]),
                    wbuf[zi, c],
                    preferred_element_type=f32,
                )

            @pl.when(o < B - 1)
            def _():
                psend[to, c] = total.astype(bf16)
                p_copy(c, to, me).start()

            @pl.when(o == B - 1)
            def _():
                own[c] = total

            return carry

        with region("prod"):
            lax.fori_loop(0, B, product, 0)
        if c > 0:
            finish(c - 1)
    finish(CH - 1)

    res = rk_ref.shape[2]
    qrows = dq_ref.shape[1]
    cells = res + nb + OFF
    row_request = lax.rem(lax.broadcasted_iota(jnp.int32, (qrows, cells), 0), requests)
    cell = lax.broadcasted_iota(jnp.int32, (qrows, cells), 1)
    last = jnp.where(s == n - 1, 1, 0)
    share = G * heads // n
    with region("decode"):
        masks = []
        for r in range(requests):
            usable = (
                (cell < rlen_ref[r, s])
                | (
                    (cell >= res)
                    & (cell < res + nb)
                    & ((cell - res + 1) * ratio_ref[r, s] <= interval)
                )
                | ((cell >= res + nb + OFF - phase_ref[r] * last) & (cell >= res + nb))
            )
            masks.append(usable & (row_request == r))
        for k in range(heads):
            lanes = slice(k * hd, (k + 1) * hd)
            pieces = []
            for r in range(requests):
                keys = (
                    rk_ref[r, k],
                    bk_ref[r * nb : (r + 1) * nb, lanes],
                    kbuf[r, k, rows - OFF :],
                )
                scores = jnp.concatenate(
                    [
                        lax.dot_general(
                            dq_ref[k], key, (((1,), (1,)), ((), ())), preferred_element_type=f32
                        )
                        for key in keys
                    ],
                    axis=1,
                )
                pieces.append(jnp.where(masks[r], scores * inv_root, masked_score))
            peak = jnp.maximum(
                jnp.max(pieces[0], axis=-1, keepdims=True),
                jnp.max(pieces[1], axis=-1, keepdims=True),
            )
            total = jnp.zeros((qrows, 1), f32)
            out = jnp.zeros((qrows, hd), f32)
            for r in range(requests):
                weights = jnp.exp(pieces[r] - peak)
                total += jnp.sum(weights, axis=-1, keepdims=True)
                low = weights.astype(bf16)
                out += jnp.dot(low[:, :res], rv_ref[r, k], preferred_element_type=f32)
                out += jnp.dot(
                    low[:, res : res + nb],
                    bv_ref[r * nb : (r + 1) * nb, lanes],
                    preferred_element_type=f32,
                )
                out += jnp.dot(
                    low[:, res + nb :], vbuf[r, k, rows - OFF :], preferred_element_type=f32
                )
            lane = lax.broadcasted_iota(jnp.int32, (qrows, hd), 1)
            slots = hd // (2 * share)
            stats = jnp.where(lax.rem(lane // slots, 2) == 0, peak, total)
            stats = stats.reshape(G // share, share, pair, hd)
            lane = lax.broadcasted_iota(jnp.int32, (G // share, pair, hd), 2)
            packed = stats[:, 0]
            for j in range(1, share):
                packed = jnp.where(lane >= 2 * slots * j, stats[:, j], packed)
            dests = slice(k * G // share, (k + 1) * G // share)
            snd[dests] = out.reshape(G // share, share * pair, hd).astype(bf16)
            snd_stats[dests] = packed

    def d_copy(to, frm):
        return remote(snd.at[to], rcv.at[frm], d_send.at[to], d_recv.at[frm], to)

    def e_copy(to, frm):
        return remote(snd_stats.at[to], rcv_stats.at[frm], e_send.at[to], e_recv.at[frm], to)

    def t_copy(to, frm):
        return remote(att.at[frm], att.at[frm], t_send.at[to], t_recv.at[frm], to)

    for o in range(1, n):
        e_copy(lax.rem(s + o, n), s).start()
        d_copy(lax.rem(s + o, n), s).start()
    rcv[s] = snd[s]
    rcv_stats[s] = snd_stats[s]

    with region("outs"):
        outs = []
        for i, (made, made_rows, out) in enumerate(
            ((bk_ref, bk_rows, bk_out), (bv_ref, bv_rows, bv_out))
        ):
            by_head = jnp.stack([made[:, k * hd : (k + 1) * hd] for k in range(heads)], axis=0)
            made_rows[...] = jnp.swapaxes(by_head, 0, 1)
            outs.append(pltpu.make_async_copy(made_rows, out, out_sem.at[i]))
            outs[-1].start()

    with region("drain"):
        for c in range(CH):
            for o in range(1, B):
                p_copy(c, lax.rem(me + o, B), me).wait_send()
        for kk in range(2):
            for r in range(requests):
                a_relay(kk, r).wait_send()
        for v in range(2 * heads):
            for x in range(2):

                @pl.when((v // 2 % 2) * 2 + x != me)
                def _(v=v, x=x):
                    a_remote(jnp.int32(v), x).wait_send()

        for way in range(2):
            for d in range(depth - 1):
                shard, target, there = w_out(way, d)

                @pl.when(there)
                def _(way=way, d=d, shard=shard, target=target):
                    for c in range(CH):
                        w_copy(way, d, c, shard, target).wait_send()

        @pl.when(me < B - 1)
        def _():
            for p in range(2 * requests):
                rim_near(p).wait_send()

        @pl.when(crosses)
        def _():
            rim_near(0).wait_send()
            for p in range(1, 2 * requests):
                rim_far(p).wait_send()

        @pl.when(relays)
        def _():
            rim_pass().wait_send()

    with region("dwait"):
        for o in range(1, n):
            source = lax.rem(s + o, n)
            e_copy(source, source).wait_recv()
            d_copy(source, source).wait_recv()
    landed = rcv[...].astype(f32)
    attended = []
    for j in range(share):
        at = 2 * slots * j
        peaks = rcv_stats[:, :, at : at + 1]
        sums = rcv_stats[:, :, at + slots : at + slots + 1]
        scale = jnp.exp(peaks - jnp.max(peaks, axis=0, keepdims=True))
        mixed = jnp.sum(scale * landed[:, j * pair : (j + 1) * pair], axis=0)
        attended.append(mixed / jnp.sum(scale * sums, axis=0))
    att[s] = jnp.concatenate(attended, axis=0).astype(bf16)
    for o in range(1, n):
        t_copy(lax.rem(s + o, n), s).start()
    ow_load.wait()
    with region("twait"):
        for o in range(1, n):
            d_copy(lax.rem(s + o, n), s).wait_send()
            e_copy(lax.rem(s + o, n), s).wait_send()
        for o in range(1, n):
            source = lax.rem(s + o, n)
            t_copy(source, source).wait_recv()
    wide = [att[i].astype(f32) for i in range(n)]
    vectors = jnp.concatenate(
        [wide[i][j * pair : (j + 1) * pair] for i in range(n) for j in range(share)], axis=1
    ).astype(bf16)
    with region("outproj"):
        partial_value = jnp.dot(vectors, owbuf[...], preferred_element_type=f32)
        part[0] = partial_value
    swap = remote(part.at[0], part.at[1], h_send, h_recv)
    swap.start()
    with region("swap"):
        for o in range(1, n):
            t_copy(lax.rem(s + o, n), s).wait_send()
        swap.wait_recv()
    first = jnp.where(h == 0, part[0], part[1])
    second = jnp.where(h == 0, part[1], part[0])
    summed = (first + second).astype(bf16)
    for t in range(steps):
        proj_rows[t] = summed[t * requests : (t + 1) * requests]
    outs.append(pltpu.make_async_copy(proj_rows, proj_out, out_sem.at[2]))
    outs[-1].start()
    swap.wait_send()
    with region("outwait"):
        for copy in outs:
            copy.wait()


def handed_on(keys_ref, values_ref, projected_ref, keys_out, values_out, projected_out):
    keys_out[...] = keys_ref[...]
    values_out[...] = values_ref[...]
    projected_out[...] = projected_ref[...]


def fused_body(
    shard_count,
    raw_keys,
    raw_values,
    phase,
    ratio,
    resident_len,
    beacon_queries,
    beacon_wk,
    beacon_wv,
    resident_keys,
    resident_values,
    decode_queries,
    out_weight,
):
    n = shard_count
    depth = n // B
    requests, interval, heads, hd = raw_keys.shape
    steps = decode_queries.shape[0]
    nb = beacon_queries.shape[1]
    rows = interval + OFF
    res = resident_keys.shape[1]
    feature, columns = beacon_wk.shape
    width = 2 * columns // CH
    pair = requests * steps
    share = G * heads // n
    bf16, f32 = jnp.bfloat16, jnp.float32
    dma = pltpu.SemaphoreType.DMA
    smem = pl.BlockSpec(memory_space=pltpu.SMEM)
    anywhere = pl.BlockSpec(memory_space=pl.ANY)
    vmem = pl.BlockSpec(memory_space=pltpu.VMEM)
    keys, values, projected = pl.pallas_call(
        functools.partial(fused_kernel, n),
        out_shape=(
            jax.ShapeDtypeStruct((requests * nb, heads, hd), bf16),
            jax.ShapeDtypeStruct((requests * nb, heads, hd), bf16),
            jax.ShapeDtypeStruct((steps, requests, out_weight.shape[1]), bf16),
        ),
        in_specs=[smem] * 3 + [anywhere] * 9,
        out_specs=(anywhere, anywhere, anywhere),
        scratch_shapes=[
            pltpu.VMEM(raw_keys.shape, bf16),
            pltpu.VMEM(raw_values.shape, bf16),
            pltpu.VMEM(beacon_queries.shape, bf16),
            pltpu.VMEM(resident_keys.shape, bf16),
            pltpu.VMEM(resident_values.shape, bf16),
            pltpu.VMEM(decode_queries.shape, bf16),
            pltpu.VMEM((2 * requests, OFF, heads, hd), bf16),
            pltpu.VMEM((OFF, heads, hd), bf16),
            pltpu.VMEM((requests, heads, rows, hd), bf16),
            pltpu.VMEM((requests, heads, rows, hd), bf16),
            pltpu.VMEM((G, nb, hd), bf16),
            pltpu.VMEM((depth, CH, feature, width), bf16),
            pltpu.VMEM((depth, requests, B, nb, feature), bf16),
            pltpu.VMEM((requests * heads, 2, nb, feature), bf16),
            pltpu.VMEM((B, CH, requests * nb, width), bf16),
            pltpu.VMEM((B, CH, requests * nb, width), bf16),
            pltpu.VMEM((CH, requests * nb, width), f32),
            pltpu.VMEM((requests, nb, rows), f32),
            pltpu.VMEM(out_weight.shape, bf16),
            pltpu.VMEM((requests, heads, res, hd), bf16),
            pltpu.VMEM((requests, heads, res, hd), bf16),
            pltpu.VMEM((heads, G * pair, hd), bf16),
            pltpu.VMEM((requests * nb, columns), bf16),
            pltpu.VMEM((requests * nb, columns), bf16),
            pltpu.VMEM((n, share * pair, hd), bf16),
            pltpu.VMEM((n, pair, hd), f32),
            pltpu.VMEM((n, share * pair, hd), bf16),
            pltpu.VMEM((n, pair, hd), f32),
            pltpu.VMEM((n, share * pair, hd), bf16),
            pltpu.VMEM((2, pair, out_weight.shape[1]), f32),
            pltpu.VMEM((requests * nb, heads, hd), bf16),
            pltpu.VMEM((requests * nb, heads, hd), bf16),
            pltpu.VMEM((steps, requests, out_weight.shape[1]), bf16),
            dma((CH + 2 * requests + 5,)),
            dma((3,)),
            dma((2 * requests,)),
            dma((2 * requests,)),
            dma,
            dma,
            dma((2, depth - 1, CH)),
            dma((2, depth - 1, CH)),
            dma((requests * heads, 2)),
            dma((2, requests, B)),
            dma((2, requests)),
            dma((2, requests)),
            dma((2, requests)),
            dma((B, CH)),
            dma((B, CH)),
            dma((n,)),
            dma((n,)),
            dma((n,)),
            dma((n,)),
            dma((n,)),
            dma((n,)),
            dma,
            dma,
        ],
        compiler_params=pltpu.CompilerParams(
            collective_id=0, has_side_effects=True, vmem_limit_bytes=60 * 1024 * 1024
        ),
    )(
        phase,
        ratio,
        resident_len,
        raw_keys,
        raw_values,
        beacon_queries,
        beacon_wk,
        beacon_wv,
        resident_keys,
        resident_values,
        decode_queries,
        out_weight,
    )
    keys, values, projected = pl.pallas_call(
        handed_on,
        out_shape=tuple(jax.ShapeDtypeStruct(x.shape, x.dtype) for x in (keys, values, projected)),
        in_specs=[vmem] * 3,
        out_specs=(vmem,) * 3,
    )(keys, values, projected)
    return (
        keys.reshape(requests, nb, heads, hd),
        values.reshape(requests, nb, heads, hd),
        projected,
    )


def chosen_body(shard_count, head_count):
    def run(*arrays):
        requests, _, heads, hd = arrays[0].shape
        feature = arrays[6].shape[0]
        fits = (
            head_count == 2
            and shard_count == B * B
            and requests == 2
            and heads == B
            and 2 * feature == G * hd
        )
        return fused_body(shard_count, *arrays) if fits else body(*arrays)

    return run


def solution(mesh):
    return jax.shard_map(
        chosen_body(mesh.shape["seq"], mesh.shape["head"]),
        mesh=mesh,
        in_specs=(
            P(None, "seq", "head", None),
            P(None, "seq", "head", None),
            P(),
            P(),
            P(),
            P(None, "seq", "head", None, None),
            P("seq", "head"),
            P("seq", "head"),
            P(None, "seq", "head", None),
            P(None, "seq", "head", None),
            P(None, None, "head", None, None),
            P("head", "seq"),
        ),
        out_specs=(
            P(None, "seq", "head", None),
            P(None, "seq", "head", None),
            P(None, None, "seq"),
        ),
        check_vma=False,
    )
```

```python
import contextlib
import functools
import math

import jax
import jax.numpy as jnp
from jax import lax
from jax.experimental import pallas as pl
from jax.experimental.pallas import tpu as pltpu
from jax.sharding import PartitionSpec as P

G = 8
INTERVAL = 1024
NB = 128
OFF = 256
STEPS = 4


masked_score = -1e30


def region(name):
    return contextlib.nullcontext()


def shifted(value, axis, steps):
    count = lax.axis_size(axis)
    first, last = (max(0, -steps), min(count, count - steps))
    return lax.ppermute(value, axis, [(source, source + steps) for source in range(first, last)])


def joined(shard, axis, combine):
    everything = jax.tree.map(lambda part: lax.all_gather(part, axis), shard)
    first = jax.tree.map(lambda part: part[0], everything)

    def hop(k, so_far):
        return combine(so_far, jax.tree.map(lambda part: part[k], everything))

    return lax.fori_loop(1, lax.axis_size(axis), hop, first)


def blend(former, latter):
    row_peak = jnp.maximum(former[0], latter[0])
    former_scale = jnp.exp(former[0] - row_peak)
    latter_scale = jnp.exp(latter[0] - row_peak)
    weight_sum = former[1] * former_scale + latter[1] * latter_scale
    weighted = former[2] * former_scale[..., None] + latter[2] * latter_scale[..., None]
    return (row_peak, weight_sum, weighted)


def pool_part(queries, key_rows, value_rows, positions, present, reaches):
    inv_root = 1.0 / math.sqrt(queries.shape[-1])

    def per_request(members):
        query_block, key_block, value_block, position_row, present_row, reach_row = members
        scores = (
            jnp.einsum("jkgd,ikd->jkgi", query_block, key_block, preferred_element_type=jnp.float32)
            * inv_root
        )
        allowed = (
            present_row[None, :]
            & (position_row[None, :] >= 0)
            & (position_row[None, :] < INTERVAL)
            & (position_row[None, :] < reach_row[:, None])
        )
        cache_mask = allowed[:, None, None, :]
        row_peak = jnp.max(jnp.where(cache_mask, scores, masked_score), axis=-1)
        weights = jnp.where(cache_mask, jnp.exp(scores - row_peak[..., None]), 0.0)
        weight_sum = jnp.sum(weights, axis=-1)
        weighted = jnp.einsum(
            "jkgi,ikd->jkgd",
            weights.astype(jnp.bfloat16),
            value_block,
            preferred_element_type=jnp.float32,
        )
        return (row_peak, weight_sum, weighted)

    return lax.map(per_request, (queries, key_rows, value_rows, positions, present, reaches))


def body(
    raw_keys,
    raw_values,
    phase,
    ratio,
    resident_len,
    beacon_queries,
    beacon_wk,
    beacon_wv,
    resident_keys,
    resident_values,
    decode_queries,
    out_weight,
):
    requests = raw_keys.shape[0]
    kv_local = raw_keys.shape[2]
    head_dim = raw_keys.shape[3]
    shard_index = lax.axis_index("seq")
    shard_count = lax.axis_size("seq")
    is_first = shard_index == 0
    is_last = shard_index == shard_count - 1
    own_ratio = lax.dynamic_index_in_dim(ratio, shard_index, 1, keepdims=False)
    slot_ids = jnp.arange(NB, dtype=jnp.int32)
    lead_in = jnp.where(is_first, phase, 0)
    reaches = (slot_ids[None, :] + 1) * own_ratio[:, None] + lead_in[:, None]
    tail_keys = raw_keys[:, INTERVAL - OFF :]
    tail_values = raw_values[:, INTERVAL - OFF :]
    own_positions = jnp.arange(INTERVAL, dtype=jnp.int32)[None, :] + phase[:, None]
    rim_ids = jnp.arange(OFF, dtype=jnp.int32)
    rim_positions = rim_ids[None, :] - OFF + phase[:, None]
    near_keys, near_values = shifted((tail_keys, tail_values), "seq", 1)
    key_rows = jnp.concatenate([near_keys, raw_keys], axis=1)
    value_rows = jnp.concatenate([near_values, raw_values], axis=1)
    positions = jnp.concatenate([rim_positions, own_positions], axis=1)
    present = jnp.logical_not(is_first) | (positions >= phase[:, None])
    pooled_parts = pool_part(beacon_queries, key_rows, value_rows, positions, present, reaches)
    pooled = (pooled_parts[2] / pooled_parts[1][..., None]).astype(jnp.bfloat16)
    pooled_flat = pooled.reshape(requests * NB, kv_local * G * head_dim)
    pooled_whole = lax.all_gather(pooled_flat, "head", axis=1, tiled=True)
    key_sum = jnp.dot(
        pooled_whole,
        lax.all_gather(beacon_wk, "seq", axis=0, tiled=True),
        preferred_element_type=jnp.float32,
    )
    value_sum = jnp.dot(
        pooled_whole,
        lax.all_gather(beacon_wv, "seq", axis=0, tiled=True),
        preferred_element_type=jnp.float32,
    )
    made_keys = key_sum
    made_values = value_sum
    made_keys = made_keys.reshape(requests, NB, kv_local, head_dim)
    made_values = made_values.reshape(requests, NB, kv_local, head_dim)
    slot_live = slot_ids[None, :] < (INTERVAL // own_ratio)[:, None]
    beacon_keys = jnp.where(slot_live[:, :, None, None], made_keys, 0.0).astype(jnp.bfloat16)
    beacon_values = jnp.where(slot_live[:, :, None, None], made_values, 0.0).astype(jnp.bfloat16)
    cache_keys = jnp.concatenate([resident_keys, beacon_keys, tail_keys], axis=1)
    cache_values = jnp.concatenate([resident_values, beacon_values, tail_values], axis=1)
    own_len = lax.dynamic_index_in_dim(resident_len, shard_index, 1, keepdims=False)
    resident_ok = jnp.arange(resident_keys.shape[1], dtype=jnp.int32)[None, :] < own_len[:, None]
    leftover_ok = (rim_ids[None, :] >= OFF - phase[:, None]) & is_last
    usable = jnp.concatenate([resident_ok, slot_live, leftover_ok], axis=1)
    inv_root = 1.0 / math.sqrt(head_dim)
    scores = (
        jnp.einsum(
            "srkgd,rikd->rksgi", decode_queries, cache_keys, preferred_element_type=jnp.float32
        )
        * inv_root
    )
    cache_mask = usable[:, None, None, None, :]
    row_peak = jnp.max(jnp.where(cache_mask, scores, masked_score), axis=-1)
    weights = jnp.where(cache_mask, jnp.exp(scores - row_peak[..., None]), 0.0)
    weight_sum = jnp.sum(weights, axis=-1)
    weighted = jnp.einsum(
        "rksgi,rikd->rksgd",
        weights.astype(jnp.bfloat16),
        cache_values,
        preferred_element_type=jnp.float32,
    )
    merged = joined((row_peak, weight_sum, weighted), "seq", blend)
    total_sum = merged[1]
    total_weighted = merged[2]
    attended = (total_weighted / total_sum[..., None]).astype(jnp.bfloat16)
    attended = jnp.transpose(attended, (2, 0, 1, 3, 4)).reshape(
        STEPS * requests, kv_local * G * head_dim
    )
    partial_value = jnp.dot(attended, out_weight, preferred_element_type=jnp.float32)
    summed = lax.psum(partial_value, "head")
    projected = summed.astype(jnp.bfloat16).reshape(STEPS, requests, out_weight.shape[1])
    return (beacon_keys, beacon_values, projected)


B = 4


def fused_kernel(
    shard_count,
    phase_ref,
    ratio_ref,
    rlen_ref,
    k_hbm,
    v_hbm,
    q_hbm,
    wk_hbm,
    wv_hbm,
    rk_hbm,
    rv_hbm,
    dq_hbm,
    ow_hbm,
    bk_out,
    bv_out,
    part_out,
    kraw,
    vraw,
    qraw,
    rkraw,
    rvraw,
    dqraw,
    rimraw,
    rimrel,
    kbuf,
    vbuf,
    qbuf,
    wbuf,
    act,
    stage,
    psend,
    precv,
    own,
    bias,
    owbuf,
    rk_ref,
    rv_ref,
    dq_ref,
    bk_ref,
    bv_ref,
    dacc,
    dlow,
    snd,
    snd_stats,
    rcv,
    rcv_stats,
    att,
    part,
    bk_rows,
    bv_rows,
    load_sem,
    w_load,
    out_sem,
    rim_send,
    rim_recv,
    rel_send,
    rel_recv,
    w_send,
    w_recv,
    a_send,
    a_recv,
    a_loc,
    p_send,
    p_recv,
    s_send,
    s_recv,
    d_send,
    d_recv,
    e_send,
    e_recv,
    t_send,
    t_recv,
    h_send,
    h_recv,
):
    n = shard_count
    depth = n // B
    s = lax.axis_index("seq")
    h = lax.axis_index("head")
    z = s // B
    me = lax.rem(s, B)
    requests, interval, heads, hd = kraw.shape
    rows = interval + OFF
    nb = bias.shape[1]
    blocks = wbuf.shape[1]
    units = [(b, 2) for b in range(0, blocks - 2, 2)] + [(blocks - 2, 1), (blocks - 1, 1)]
    inv_root = 1.0 / math.sqrt(hd)
    f32 = jnp.float32
    bf16 = jnp.bfloat16

    def remote(src, dst, send, recv, seq=None):
        target = {"head": 1 - h} if seq is None else {"seq": seq}
        return pltpu.make_async_remote_copy(
            src_ref=src,
            dst_ref=dst,
            send_sem=send,
            recv_sem=recv,
            device_id=target,
            device_id_type=pl.DeviceIdType.MESH,
        )

    def got(ref, sem):
        remote(ref, ref, sem, sem, s).wait_recv()

    def sent(ref, sem):
        remote(ref, ref, sem, sem, s).wait_send()

    loads = []

    def load(source, target):
        loads.append(pltpu.make_async_copy(source, target, load_sem.at[len(loads)]))
        loads[-1].start()
        return loads[-1]

    for i, (b, count) in enumerate(units):
        for at in range(b, b + count):
            source = (wk_hbm, wv_hbm)[at // heads].at[:, (at % heads) * hd : (at % heads + 1) * hd]
            pltpu.make_async_copy(source, wbuf.at[z, at], w_load.at[i]).start()
    kv_load = [
        load((k_hbm, v_hbm)[p % 2].at[p // 2], (kraw, vraw)[p % 2].at[p // 2])
        for p in range(2 * requests)
    ]
    q_load = load(q_hbm, qraw)
    rest_load = [load(rk_hbm, rkraw), load(rv_hbm, rvraw), load(dq_hbm, dqraw)]
    ow_load = load(ow_hbm, owbuf)

    with region("barrier"):
        barrier = pltpu.get_barrier_semaphore()
        for o in range(1, n):
            pl.semaphore_signal(
                barrier,
                inc=1,
                device_id={"seq": lax.rem(s + o, n)},
                device_id_type=pl.DeviceIdType.MESH,
            )
        pl.semaphore_signal(
            barrier, inc=1, device_id={"head": 1 - h}, device_id_type=pl.DeviceIdType.MESH
        )
        pl.semaphore_wait(barrier, n)

    crosses = (me == B - 1) & (z < depth - 1)
    relays = (me < B - 1) & (z < depth - 1)

    def rim_near(p):
        source = (k_hbm, v_hbm)[p % 2].at[p // 2, interval - OFF :]
        return remote(source, rimraw.at[p], rim_send, rim_recv.at[p // 2], lax.rem(s + 1, n))

    def rim_far(p):
        source = (k_hbm, v_hbm)[p % 2].at[p // 2, interval - OFF :]
        return remote(source, rimrel, rim_send, rel_recv, z * B + lax.rem(p, B - 1))

    def rim_pass():
        p = jnp.where(me == 0, B - 1, me)
        return remote(rimrel, rimraw.at[p], rel_send, rim_recv.at[p // 2], lax.rem((z + 1) * B, n))

    @pl.when(me < B - 1)
    def _():
        for p in range(2 * requests):
            rim_near(p).start()

    @pl.when(crosses)
    def _():
        rim_near(0).start()
        for p in range(1, 2 * requests):
            rim_far(p).start()

    def w_copy(way, d, i, shard, target):
        b, count = units[i]
        return remote(
            wbuf.at[shard, b : b + count],
            wbuf.at[shard, b : b + count],
            w_send.at[way, d],
            w_recv.at[way, d, i],
            target * B + me,
        )

    def w_out(way, d):
        if way == 0:
            return z - d, z + 1, (z - d >= 0) & (z + 1 < depth)
        return z + d, z - 1, (z + d < depth) & (z - 1 >= 0)

    def w_in(way, d):
        if way == 0:
            return z - 1 - d, z - 1 - d >= 0
        return z + 1 + d, z + 1 + d < depth

    def w_own(first, end):
        for i in range(first, end):
            b, count = units[i]
            pltpu.make_async_copy(
                wbuf.at[z, b : b + count], wbuf.at[z, b : b + count], w_load.at[i]
            ).wait()
            for way in range(2):
                shard, target, there = w_out(way, 0)

                @pl.when(there)
                def _(way=way, i=i, shard=shard, target=target):
                    w_copy(way, 0, i, shard, target).start()

    def w_relay(d, i):
        for way in range(2):
            shard, target, onward = w_out(way, d)

            @pl.when(onward)
            def _(way=way, shard=shard, target=target):
                w_copy(way, d - 1, i, shard, z).wait_recv()
                w_copy(way, d, i, shard, target).start()

    def w_wait(i):
        for way in range(2):
            for d in range(depth - 1):
                shard, there = w_in(way, d)
                if d < depth - 2:
                    there = there & ((z == depth - 1) if way == 0 else (z == 0))

                @pl.when(there)
                def _(way=way, d=d, shard=shard):
                    w_copy(way, d, i, shard, z).wait_recv()

    def rim_relay():
        with region("rimpass"):
            got(rimrel, rel_recv)
            rim_pass().start()

    w_own(0, 1)

    @pl.when(me != 1)
    def _():
        w_own(1, 2)

    @pl.when((me == 0) | (me == B - 1))
    def _():
        w_own(2, len(units))

    with region("prep"):
        for r in range(requests):
            slot = lax.broadcasted_iota(jnp.int32, (nb, rows), 0)
            position = lax.broadcasted_iota(jnp.int32, (nb, rows), 1) - OFF + phase_ref[r]
            lead = jnp.where(s == 0, phase_ref[r], 0)
            reach = (slot + 1) * ratio_ref[r, s] + lead
            allowed = (position >= lead) & (position < interval) & (position < reach)
            bias[r] = jnp.where(allowed, 0.0, masked_score).astype(f32)
        for p in range(2 * requests):
            kv_load[p].wait()
            (kbuf, vbuf)[p % 2][p // 2, :, OFF:] = jnp.swapaxes((kraw, vraw)[p % 2][p // 2], 0, 1)
        for copy in rest_load:
            copy.wait()
        for r in range(requests):
            rk_ref[r] = jnp.swapaxes(rkraw[r], 0, 1)
            rv_ref[r] = jnp.swapaxes(rvraw[r], 0, 1)
        steps = dqraw.shape[0]
        pair = steps * requests
        for k in range(heads):
            asked = jnp.stack(
                [dqraw[t, r, k].astype(f32) for t in range(steps) for r in range(requests)], axis=0
            )
            dq_ref[k] = jnp.swapaxes(asked, 0, 1).reshape(G * pair, hd).astype(bf16)
        q_load.wait()

    @pl.when(relays & (me != 0))
    def _():
        rim_relay()

    @pl.when(me == 1)
    def _():
        w_own(1, 2)

    @pl.when((me == 1) | (me == 2))
    def _():
        w_own(2, len(units))

    @pl.when(s == 0)
    def _():
        kbuf[:, :, :OFF] = jnp.zeros((requests, heads, OFF, hd), kbuf.dtype)
        vbuf[:, :, :OFF] = jnp.zeros((requests, heads, OFF, hd), vbuf.dtype)

    def a_remote(v, x):
        kk, r, y = v // 4, lax.rem(v, 2), lax.rem(v // 2, 2)
        return remote(
            stage.at[v, x],
            act.at[h * 2 + kk, r, me],
            a_send,
            a_recv.at[kk, r],
            z * B + y * 2 + x,
        )

    def a_local(kk, r, v):
        return pltpu.make_async_copy(
            stage.at[v, lax.rem(me, 2)], act.at[h * 2 + kk, r, me], a_loc.at[kk, r]
        )

    def a_relay(kk, r):
        return remote(
            act.at[h * 2 + kk, r], act.at[h * 2 + kk, r], p_send, p_recv
        )

    def a_gather(kk, r):
        a_local(kk, r, kk * 4 + (me // 2) * 2 + r).wait()
        got(act.at[0, 0, : B - 1], a_recv.at[kk, r])
        a_relay(kk, r).start()

    def unit(u, carry):
        r, k = u // heads, lax.rem(u, heads)
        v = k * 2 + r

        @pl.when((k == 0) & (s > 0))
        def _():
            with region("rimwait"):
                got(rimraw.at[:2], rim_recv.at[r])
            kbuf[r, :, :OFF] = jnp.swapaxes(rimraw[r * 2], 0, 1)
            vbuf[r, :, :OFF] = jnp.swapaxes(rimraw[r * 2 + 1], 0, 1)

        with region("att"):
            qbuf[...] = jnp.swapaxes(qraw[r, :, k], 0, 1)
            for g in range(G):
                scores = (
                    lax.dot_general(
                        qbuf[g],
                        kbuf[r, k],
                        (((1,), (1,)), ((), ())),
                        preferred_element_type=f32,
                    )
                    * inv_root
                    + bias[r]
                )
                weights = jnp.exp(scores - jnp.max(scores, axis=-1, keepdims=True))
                total = jnp.sum(weights, axis=-1, keepdims=True)
                out = jnp.dot(weights.astype(bf16), vbuf[r, k], preferred_element_type=f32)
                at = (g % 4) * hd
                stage[v, g // 4, :, at : at + hd] = (out / total).astype(bf16)
        for x in range(2):
            member = lax.rem(k, 2) * 2 + x

            @pl.when(member == me)
            def _():
                a_local(k // 2, r, v).start()

            @pl.when(member != me)
            def _(x=x):
                a_remote(v, x).start()

        with region("relay"):

            for i in range(len(units)):

                @pl.when(u == min(i, heads - 1))
                def _(i=i):
                    w_relay(1, i)

            @pl.when((u == 0) & (me == 0) & relays)
            def _():
                rim_relay()

            for i in range(len(units) - 2):

                @pl.when(u == heads + 1 + i)
                def _(i=i):
                    w_relay(2, i)

            @pl.when(u == heads + 1)
            def _():
                a_gather(0, 0)

            @pl.when(u == heads + 3)
            def _():
                a_gather(1, 0)

        return carry

    lax.fori_loop(0, 2 * heads, unit, 0)
    with region("gather"):
        a_gather(0, 1)
        w_relay(2, len(units) - 2)
        w_relay(2, len(units) - 1)
        a_gather(1, 1)
        got(act.at[:2], p_recv)

    def p_copy(i, to, frm):
        b, count = units[i]
        return remote(
            psend.at[to, b : b + count], precv.at[frm, b : b + count], s_send, s_recv.at[i], z * B + to
        )

    slot_row = lax.broadcasted_iota(jnp.int32, (nb, hd), 0)

    def finish(i):
        b, count = units[i]
        with region(f"finish{i}"):
            got(precv.at[: B - 1, b : b + count], s_recv.at[i])
        for at in range(b, b + count):
            total = own[at]
            for o in range(1, B):
                total += precv[lax.rem(me + o, B), at].astype(f32)
            out_ref = (bk_ref, bv_ref)[at // heads]
            for r in range(requests):
                live = (slot_row + 1) * ratio_ref[r, s] <= interval
                out_ref[at % heads, r * nb : (r + 1) * nb] = jnp.where(
                    live, total[r * nb : (r + 1) * nb], 0.0
                ).astype(bf16)

    def product(i):
        b, count = units[i]

        def step(o, carry):
            to = lax.rem(me + 1 + o, B)
            total = jnp.zeros((requests * nb, count * hd), f32)
            for zi in range(depth):
                total += jnp.dot(
                    act[zi, :, to].reshape(requests * nb, act.shape[4]),
                    jnp.concatenate([wbuf[zi, at] for at in range(b, b + count)], axis=1),
                    preferred_element_type=f32,
                )

            @pl.when(o < B - 1)
            def _():
                for at in range(count):
                    psend[to, b + at] = total[:, at * hd : (at + 1) * hd].astype(bf16)
                p_copy(i, to, me).start()

            @pl.when(o == B - 1)
            def _():
                for at in range(count):
                    own[b + at] = total[:, at * hd : (at + 1) * hd]

            return carry

        with region(f"prod{i}"):
            lax.fori_loop(0, B, step, 0)

    res = rk_ref.shape[2]
    qrows = dq_ref.shape[1]
    cells = res + nb + OFF
    mergers = snd.shape[0]
    share = G * heads // mergers
    slots = hd // (2 * share)
    per_head = G // share
    first_merger = (depth // 2) * B - mergers // 2
    mine = s - first_merger
    merges = (mine >= 0) & (mine < mergers)

    def e_copy(to):
        return remote(snd_stats.at[to], rcv_stats.at[s], e_send, e_recv, first_merger + to)

    def d_copy(to):
        return remote(snd.at[to], rcv.at[s], d_send, d_recv, first_merger + to)

    def to_mergers(copy, first, end):
        for to in range(first, end):

            @pl.when(mine != to)
            def _(to=to):
                copy(to).start()

    def decode_weights():
        row_request = lax.rem(lax.broadcasted_iota(jnp.int32, (qrows, cells), 0), requests)
        cell = lax.broadcasted_iota(jnp.int32, (qrows, cells), 1)
        last = jnp.where(s == n - 1, 1, 0)
        masks = []
        for r in range(requests):
            usable = (
                (cell < rlen_ref[r, s])
                | (
                    (cell >= res)
                    & (cell < res + nb)
                    & ((cell - res + 1) * ratio_ref[r, s] <= interval)
                )
                | ((cell >= res + nb + OFF - phase_ref[r] * last) & (cell >= res + nb))
            )
            masks.append(usable & (row_request == r))
        for k in range(heads):
            pieces = []
            for r in range(requests):
                keys = (
                    rk_ref[r, k],
                    bk_ref[k, r * nb : (r + 1) * nb],
                    kbuf[r, k, rows - OFF :],
                )
                scores = jnp.concatenate(
                    [
                        lax.dot_general(
                            dq_ref[k], key, (((1,), (1,)), ((), ())), preferred_element_type=f32
                        )
                        for key in keys
                    ],
                    axis=1,
                )
                pieces.append(jnp.where(masks[r], scores * inv_root, masked_score))
            peak = jnp.maximum(
                jnp.max(pieces[0], axis=-1, keepdims=True),
                jnp.max(pieces[1], axis=-1, keepdims=True),
            )
            total = jnp.zeros((qrows, 1), f32)
            out = jnp.zeros((qrows, hd), f32)
            for r in range(requests):
                weights = jnp.exp(pieces[r] - peak)
                total += jnp.sum(weights, axis=-1, keepdims=True)
                low = weights.astype(bf16)
                dlow[k, r] = low[:, res : res + nb]
                out += jnp.dot(low[:, :res], rv_ref[r, k], preferred_element_type=f32)
                out += jnp.dot(
                    low[:, res + nb :], vbuf[r, k, rows - OFF :], preferred_element_type=f32
                )
            dacc[k] = out
            lane = lax.broadcasted_iota(jnp.int32, (qrows, hd), 1)
            stats = jnp.where(lax.rem(lane // slots, 2) == 0, peak, total)
            stats = stats.reshape(per_head, share, pair, hd)
            lane = lax.broadcasted_iota(jnp.int32, (per_head, pair, hd), 2)
            packed = stats[:, 0]
            for j in range(1, share):
                packed = jnp.where(lane >= 2 * slots * j, stats[:, j], packed)
            snd_stats[k * per_head : (k + 1) * per_head] = packed
        to_mergers(e_copy, 0, mergers)

    def decode_values(k):
        out = dacc[k]
        for r in range(requests):
            out += jnp.dot(
                dlow[k, r], bv_ref[k, r * nb : (r + 1) * nb], preferred_element_type=f32
            )
        snd[k * per_head : (k + 1) * per_head] = out.reshape(per_head, share * pair, hd).astype(bf16)
        to_mergers(d_copy, k * per_head, (k + 1) * per_head)

    outs = []

    def emit(made, made_rows, out):
        made_rows[...] = jnp.swapaxes(made[...], 0, 1)
        outs.append(pltpu.make_async_copy(made_rows, out, out_sem.at[len(outs)]))
        outs[-1].start()

    key_units = heads // 2
    for i in range(len(units)):
        with region(f"wwait{i}"):
            w_wait(i)
        product(i)
        if i == len(units) - 2:
            for j in range(key_units):
                finish(j)
            with region("decode"):
                decode_weights()
    for i in range(key_units, len(units)):
        finish(i)
        b, count = units[i]
        with region("values"):
            for at in range(b, b + count):
                decode_values(at - heads)

    emit(bk_ref, bk_rows, bk_out)
    emit(bv_ref, bv_rows, bv_out)

    with region("drain"):
        sent(psend.at[: B - 1], s_send)
        sent(act.at[:2], p_send)
        sent(stage.at[: requests * heads * (B - 1) // B], a_send)
        for way in range(2):
            for d in range(depth - 1):
                shard, target, there = w_out(way, d)

                @pl.when(there)
                def _(way=way, d=d, shard=shard):
                    sent(wbuf.at[shard], w_send.at[way, d])

        @pl.when((me < B - 1) | crosses)
        def _():
            sent(rimraw, rim_send)

        @pl.when(relays)
        def _():
            sent(rimrel, rel_send)

    def t_copy(to):
        return remote(att.at[mine], att.at[mine], t_send, t_recv, to)

    with region("merge"):

        @pl.when(merges)
        def _():
            rcv[s] = snd[mine]
            rcv_stats[s] = snd_stats[mine]
            got(rcv_stats.at[: n - 1], e_recv)
            got(rcv.at[: n - 1], d_recv)
            landed = rcv[...].astype(f32)
            attended = []
            for j in range(share):
                at = 2 * slots * j
                peaks = rcv_stats[:, :, at : at + 1]
                sums = rcv_stats[:, :, at + slots : at + slots + 1]
                scale = jnp.exp(peaks - jnp.max(peaks, axis=0, keepdims=True))
                mixed = jnp.sum(scale * landed[:, j * pair : (j + 1) * pair], axis=0)
                attended.append(mixed / jnp.sum(scale * sums, axis=0))
            att[mine] = jnp.concatenate(attended, axis=0).astype(bf16)
            for o in range(1, n):
                t_copy(lax.rem(s + o, n)).start()
            sent(snd.at[: mergers - 1], d_send)
            sent(snd_stats.at[: mergers - 1], e_send)

        @pl.when(jnp.logical_not(merges))
        def _():
            sent(snd, d_send)
            sent(snd_stats, e_send)

    ow_load.wait()
    with region("twait"):

        @pl.when(merges)
        def _():
            got(att.at[: mergers - 1], t_recv)

        @pl.when(jnp.logical_not(merges))
        def _():
            got(att, t_recv)

    wide = [att[i].astype(f32) for i in range(mergers)]
    vectors = jnp.concatenate(
        [wide[i][j * pair : (j + 1) * pair] for i in range(mergers) for j in range(share)], axis=1
    ).astype(bf16)
    with region("outproj"):
        part[...] = jnp.dot(vectors, owbuf[...], preferred_element_type=f32)
    swap = remote(part, part_out.at[h], h_send, h_recv)
    swap.start()
    outs.append(pltpu.make_async_copy(part, part_out.at[h], out_sem.at[len(outs)]))
    outs[-1].start()
    with region("swap"):

        @pl.when(merges)
        def _():
            sent(rcv.at[: n - 1], t_send)

        swap.wait()
        for copy in outs:
            copy.wait()


def handed_on(keys_ref, values_ref, part_ref, keys_out, values_out, projected_out):
    keys_out[...] = keys_ref[...]
    values_out[...] = values_ref[...]
    summed = (part_ref[0] + part_ref[1]).astype(projected_out.dtype)
    steps, requests, _ = projected_out.shape
    for t in range(steps):
        projected_out[t] = summed[t * requests : (t + 1) * requests]


def fused_body(
    shard_count,
    raw_keys,
    raw_values,
    phase,
    ratio,
    resident_len,
    beacon_queries,
    beacon_wk,
    beacon_wv,
    resident_keys,
    resident_values,
    decode_queries,
    out_weight,
):
    n = shard_count
    depth = n // B
    requests, interval, heads, hd = raw_keys.shape
    steps = decode_queries.shape[0]
    nb = beacon_queries.shape[1]
    rows = interval + OFF
    res = resident_keys.shape[1]
    feature, columns = beacon_wk.shape
    blocks = 2 * columns // hd
    units = blocks // 2 + 1
    pair = requests * steps
    mergers = min(2 * B, n)
    share = G * heads // mergers
    bf16, f32 = jnp.bfloat16, jnp.float32
    dma = pltpu.SemaphoreType.DMA
    smem = pl.BlockSpec(memory_space=pltpu.SMEM)
    anywhere = pl.BlockSpec(memory_space=pl.ANY)
    vmem = pl.BlockSpec(memory_space=pltpu.VMEM)
    keys, values, partial_sums = pl.pallas_call(
        functools.partial(fused_kernel, n),
        out_shape=(
            jax.ShapeDtypeStruct((requests * nb, heads, hd), bf16),
            jax.ShapeDtypeStruct((requests * nb, heads, hd), bf16),
            jax.ShapeDtypeStruct((2, pair, out_weight.shape[1]), f32),
        ),
        in_specs=[smem] * 3 + [anywhere] * 9,
        out_specs=(anywhere, anywhere, anywhere),
        scratch_shapes=[
            pltpu.VMEM(raw_keys.shape, bf16),
            pltpu.VMEM(raw_values.shape, bf16),
            pltpu.VMEM(beacon_queries.shape, bf16),
            pltpu.VMEM(resident_keys.shape, bf16),
            pltpu.VMEM(resident_values.shape, bf16),
            pltpu.VMEM(decode_queries.shape, bf16),
            pltpu.VMEM((2 * requests, OFF, heads, hd), bf16),
            pltpu.VMEM((OFF, heads, hd), bf16),
            pltpu.VMEM((requests, heads, rows, hd), bf16),
            pltpu.VMEM((requests, heads, rows, hd), bf16),
            pltpu.VMEM((G, nb, hd), bf16),
            pltpu.VMEM((depth, blocks, feature, hd), bf16),
            pltpu.VMEM((depth, requests, B, nb, feature), bf16),
            pltpu.VMEM((requests * heads, 2, nb, feature), bf16),
            pltpu.VMEM((B, blocks, requests * nb, hd), bf16),
            pltpu.VMEM((B, blocks, requests * nb, hd), bf16),
            pltpu.VMEM((blocks, requests * nb, hd), f32),
            pltpu.VMEM((requests, nb, rows), f32),
            pltpu.VMEM(out_weight.shape, bf16),
            pltpu.VMEM((requests, heads, res, hd), bf16),
            pltpu.VMEM((requests, heads, res, hd), bf16),
            pltpu.VMEM((heads, G * pair, hd), bf16),
            pltpu.VMEM((heads, requests * nb, hd), bf16),
            pltpu.VMEM((heads, requests * nb, hd), bf16),
            pltpu.VMEM((heads, G * pair, hd), f32),
            pltpu.VMEM((heads, requests, G * pair, nb), bf16),
            pltpu.VMEM((mergers, share * pair, hd), bf16),
            pltpu.VMEM((mergers, pair, hd), f32),
            pltpu.VMEM((n, share * pair, hd), bf16),
            pltpu.VMEM((n, pair, hd), f32),
            pltpu.VMEM((mergers, share * pair, hd), bf16),
            pltpu.VMEM((pair, out_weight.shape[1]), f32),
            pltpu.VMEM((requests * nb, heads, hd), bf16),
            pltpu.VMEM((requests * nb, heads, hd), bf16),
            dma((2 * requests + 5,)),
            dma((units,)),
            dma((3,)),
            dma,
            dma((requests,)),
            dma,
            dma,
            dma((2, depth - 1)),
            dma((2, depth - 1, units)),
            dma,
            dma((2, requests)),
            dma((2, requests)),
            dma,
            dma,
            dma,
            dma((units,)),
            dma,
            dma,
            dma,
            dma,
            dma,
            dma,
            dma,
            dma,
        ],
        compiler_params=pltpu.CompilerParams(
            collective_id=0, has_side_effects=True, vmem_limit_bytes=60 * 1024 * 1024
        ),
    )(
        phase,
        ratio,
        resident_len,
        raw_keys,
        raw_values,
        beacon_queries,
        beacon_wk,
        beacon_wv,
        resident_keys,
        resident_values,
        decode_queries,
        out_weight,
    )
    keys, values, projected = pl.pallas_call(
        handed_on,
        out_shape=(
            jax.ShapeDtypeStruct(keys.shape, bf16),
            jax.ShapeDtypeStruct(values.shape, bf16),
            jax.ShapeDtypeStruct((steps, requests, out_weight.shape[1]), bf16),
        ),
        in_specs=[vmem] * 3,
        out_specs=(vmem,) * 3,
    )(keys, values, partial_sums)
    return (
        keys.reshape(requests, nb, heads, hd),
        values.reshape(requests, nb, heads, hd),
        projected,
    )


def chosen_body(shard_count, head_count):
    def run(*arrays):
        requests, _, heads, hd = arrays[0].shape
        feature = arrays[6].shape[0]
        fits = (
            head_count == 2
            and shard_count == B * B
            and requests == 2
            and heads == B
            and 2 * feature == G * hd
        )
        return fused_body(shard_count, *arrays) if fits else body(*arrays)

    return run


def solution(mesh):
    return jax.shard_map(
        chosen_body(mesh.shape["seq"], mesh.shape["head"]),
        mesh=mesh,
        in_specs=(
            P(None, "seq", "head", None),
            P(None, "seq", "head", None),
            P(),
            P(),
            P(),
            P(None, "seq", "head", None, None),
            P("seq", "head"),
            P("seq", "head"),
            P(None, "seq", "head", None),
            P(None, "seq", "head", None),
            P(None, None, "head", None, None),
            P("head", "seq"),
        ),
        out_specs=(
            P(None, "seq", "head", None),
            P(None, "seq", "head", None),
            P(None, None, "seq"),
        ),
        check_vma=False,
    )
```

```python
import contextlib
import functools
import math

import jax
import jax.numpy as jnp
from jax import lax
from jax.experimental import pallas as pl
from jax.experimental.pallas import tpu as pltpu
from jax.sharding import PartitionSpec as P

G = 8
INTERVAL = 1024
NB = 128
OFF = 256
STEPS = 4


masked_score = -1e30


def region(name):
    return contextlib.nullcontext()


def shifted(value, axis, steps):
    count = lax.axis_size(axis)
    first, last = (max(0, -steps), min(count, count - steps))
    return lax.ppermute(value, axis, [(source, source + steps) for source in range(first, last)])


def joined(shard, axis, combine):
    everything = jax.tree.map(lambda part: lax.all_gather(part, axis), shard)
    first = jax.tree.map(lambda part: part[0], everything)

    def hop(k, so_far):
        return combine(so_far, jax.tree.map(lambda part: part[k], everything))

    return lax.fori_loop(1, lax.axis_size(axis), hop, first)


def blend(former, latter):
    row_peak = jnp.maximum(former[0], latter[0])
    former_scale = jnp.exp(former[0] - row_peak)
    latter_scale = jnp.exp(latter[0] - row_peak)
    weight_sum = former[1] * former_scale + latter[1] * latter_scale
    weighted = former[2] * former_scale[..., None] + latter[2] * latter_scale[..., None]
    return (row_peak, weight_sum, weighted)


def pool_part(queries, key_rows, value_rows, positions, present, reaches):
    inv_root = 1.0 / math.sqrt(queries.shape[-1])

    def per_request(members):
        query_block, key_block, value_block, position_row, present_row, reach_row = members
        scores = (
            jnp.einsum("jkgd,ikd->jkgi", query_block, key_block, preferred_element_type=jnp.float32)
            * inv_root
        )
        allowed = (
            present_row[None, :]
            & (position_row[None, :] >= 0)
            & (position_row[None, :] < INTERVAL)
            & (position_row[None, :] < reach_row[:, None])
        )
        cache_mask = allowed[:, None, None, :]
        row_peak = jnp.max(jnp.where(cache_mask, scores, masked_score), axis=-1)
        weights = jnp.where(cache_mask, jnp.exp(scores - row_peak[..., None]), 0.0)
        weight_sum = jnp.sum(weights, axis=-1)
        weighted = jnp.einsum(
            "jkgi,ikd->jkgd",
            weights.astype(jnp.bfloat16),
            value_block,
            preferred_element_type=jnp.float32,
        )
        return (row_peak, weight_sum, weighted)

    return lax.map(per_request, (queries, key_rows, value_rows, positions, present, reaches))


def body(
    raw_keys,
    raw_values,
    phase,
    ratio,
    resident_len,
    beacon_queries,
    beacon_wk,
    beacon_wv,
    resident_keys,
    resident_values,
    decode_queries,
    out_weight,
):
    requests = raw_keys.shape[0]
    kv_local = raw_keys.shape[2]
    head_dim = raw_keys.shape[3]
    shard_index = lax.axis_index("seq")
    shard_count = lax.axis_size("seq")
    is_first = shard_index == 0
    is_last = shard_index == shard_count - 1
    own_ratio = lax.dynamic_index_in_dim(ratio, shard_index, 1, keepdims=False)
    slot_ids = jnp.arange(NB, dtype=jnp.int32)
    lead_in = jnp.where(is_first, phase, 0)
    reaches = (slot_ids[None, :] + 1) * own_ratio[:, None] + lead_in[:, None]
    tail_keys = raw_keys[:, INTERVAL - OFF :]
    tail_values = raw_values[:, INTERVAL - OFF :]
    own_positions = jnp.arange(INTERVAL, dtype=jnp.int32)[None, :] + phase[:, None]
    rim_ids = jnp.arange(OFF, dtype=jnp.int32)
    rim_positions = rim_ids[None, :] - OFF + phase[:, None]
    near_keys, near_values = shifted((tail_keys, tail_values), "seq", 1)
    key_rows = jnp.concatenate([near_keys, raw_keys], axis=1)
    value_rows = jnp.concatenate([near_values, raw_values], axis=1)
    positions = jnp.concatenate([rim_positions, own_positions], axis=1)
    present = jnp.logical_not(is_first) | (positions >= phase[:, None])
    pooled_parts = pool_part(beacon_queries, key_rows, value_rows, positions, present, reaches)
    pooled = (pooled_parts[2] / pooled_parts[1][..., None]).astype(jnp.bfloat16)
    pooled_flat = pooled.reshape(requests * NB, kv_local * G * head_dim)
    pooled_whole = lax.all_gather(pooled_flat, "head", axis=1, tiled=True)
    key_sum = jnp.dot(
        pooled_whole,
        lax.all_gather(beacon_wk, "seq", axis=0, tiled=True),
        preferred_element_type=jnp.float32,
    )
    value_sum = jnp.dot(
        pooled_whole,
        lax.all_gather(beacon_wv, "seq", axis=0, tiled=True),
        preferred_element_type=jnp.float32,
    )
    made_keys = key_sum
    made_values = value_sum
    made_keys = made_keys.reshape(requests, NB, kv_local, head_dim)
    made_values = made_values.reshape(requests, NB, kv_local, head_dim)
    slot_live = slot_ids[None, :] < (INTERVAL // own_ratio)[:, None]
    beacon_keys = jnp.where(slot_live[:, :, None, None], made_keys, 0.0).astype(jnp.bfloat16)
    beacon_values = jnp.where(slot_live[:, :, None, None], made_values, 0.0).astype(jnp.bfloat16)
    cache_keys = jnp.concatenate([resident_keys, beacon_keys, tail_keys], axis=1)
    cache_values = jnp.concatenate([resident_values, beacon_values, tail_values], axis=1)
    own_len = lax.dynamic_index_in_dim(resident_len, shard_index, 1, keepdims=False)
    resident_ok = jnp.arange(resident_keys.shape[1], dtype=jnp.int32)[None, :] < own_len[:, None]
    leftover_ok = (rim_ids[None, :] >= OFF - phase[:, None]) & is_last
    usable = jnp.concatenate([resident_ok, slot_live, leftover_ok], axis=1)
    inv_root = 1.0 / math.sqrt(head_dim)
    scores = (
        jnp.einsum(
            "srkgd,rikd->rksgi", decode_queries, cache_keys, preferred_element_type=jnp.float32
        )
        * inv_root
    )
    cache_mask = usable[:, None, None, None, :]
    row_peak = jnp.max(jnp.where(cache_mask, scores, masked_score), axis=-1)
    weights = jnp.where(cache_mask, jnp.exp(scores - row_peak[..., None]), 0.0)
    weight_sum = jnp.sum(weights, axis=-1)
    weighted = jnp.einsum(
        "rksgi,rikd->rksgd",
        weights.astype(jnp.bfloat16),
        cache_values,
        preferred_element_type=jnp.float32,
    )
    merged = joined((row_peak, weight_sum, weighted), "seq", blend)
    total_sum = merged[1]
    total_weighted = merged[2]
    attended = (total_weighted / total_sum[..., None]).astype(jnp.bfloat16)
    attended = jnp.transpose(attended, (2, 0, 1, 3, 4)).reshape(
        STEPS * requests, kv_local * G * head_dim
    )
    partial_value = jnp.dot(attended, out_weight, preferred_element_type=jnp.float32)
    summed = lax.psum(partial_value, "head")
    projected = summed.astype(jnp.bfloat16).reshape(STEPS, requests, out_weight.shape[1])
    return (beacon_keys, beacon_values, projected)


B = 4
GB = 2
STRAIGHT = 2


def fused_kernel(
    shard_count,
    phase_ref,
    ratio_ref,
    rlen_ref,
    k_hbm,
    v_hbm,
    q_hbm,
    wk_hbm,
    wv_hbm,
    rk_hbm,
    rv_hbm,
    dq_hbm,
    ow_hbm,
    bk_out,
    bv_out,
    part_out,
    kraw,
    vraw,
    qraw,
    rkraw,
    rvraw,
    dqraw,
    rimraw,
    rimrel,
    kbuf,
    vbuf,
    qbuf,
    wbuf,
    act,
    stage,
    psend,
    precv,
    pdiag,
    hold,
    own,
    acc,
    bias,
    owbuf,
    rk_ref,
    rv_ref,
    dq_ref,
    bk_ref,
    bv_ref,
    dacc,
    dstat,
    dlow,
    snd,
    snd_stats,
    rcv,
    rcv_stats,
    att,
    part,
    bk_rows,
    bv_rows,
    load_sem,
    w_load,
    out_sem,
    rim_send,
    rim_recv,
    rel_send,
    rel_recv,
    w_send,
    w_recv,
    a_send,
    a_recv,
    a_loc,
    p_send,
    p_recv,
    s_send,
    s_recv,
    g_recv,
    d_send,
    d_recv,
    e_send,
    e_recv,
    t_send,
    t_recv,
    h_send,
    h_recv,
):
    n = shard_count
    depth = n // B
    s = lax.axis_index("seq")
    h = lax.axis_index("head")
    z = s // B
    me = lax.rem(s, B)
    requests, interval, heads, hd = kraw.shape
    rows = interval + OFF
    nb = psend.shape[2] // requests
    blocks = wbuf.shape[1]
    units = [(b, 2) for b in range(0, blocks - 2, 2)] + [(blocks - 2, 1), (blocks - 1, 1)]
    inv_root = 1.0 / math.sqrt(hd)
    to_log2 = inv_root / math.log(2.0)
    f32 = jnp.float32
    bf16 = jnp.bfloat16

    def remote(src, dst, send, recv, seq=None):
        target = {"head": 1 - h} if seq is None else {"seq": seq}
        return pltpu.make_async_remote_copy(
            src_ref=src,
            dst_ref=dst,
            send_sem=send,
            recv_sem=recv,
            device_id=target,
            device_id_type=pl.DeviceIdType.MESH,
        )

    def got(ref, sem):
        remote(ref, ref, sem, sem, s).wait_recv()

    def sent(ref, sem):
        remote(ref, ref, sem, sem, s).wait_send()

    barrier = pltpu.get_barrier_semaphore()
    for o in range(1, n):
        pl.semaphore_signal(
            barrier,
            inc=1,
            device_id={"seq": lax.rem(s + o, n)},
            device_id_type=pl.DeviceIdType.MESH,
        )
    pl.semaphore_signal(
        barrier, inc=1, device_id={"head": 1 - h}, device_id_type=pl.DeviceIdType.MESH
    )

    loads = []

    def load(source, target):
        loads.append(pltpu.make_async_copy(source, target, load_sem.at[len(loads)]))
        loads[-1].start()
        return loads[-1]

    for i, (b, count) in enumerate(units):
        for at in range(b, b + count):
            source = (wk_hbm, wv_hbm)[at // heads].at[:, (at % heads) * hd : (at % heads + 1) * hd]
            pltpu.make_async_copy(source, wbuf.at[z, at], w_load.at[i]).start()
    kv_load = [
        load((k_hbm, v_hbm)[p % 2].at[p // 2], (kraw, vraw)[p % 2].at[p // 2])
        for p in range(2 * requests)
    ]
    q_load = load(q_hbm, qraw)
    rest_load = [load(rk_hbm, rkraw), load(rv_hbm, rvraw), load(dq_hbm, dqraw)]
    ow_load = load(ow_hbm, owbuf)

    with region("barrier"):
        pl.semaphore_wait(barrier, n)

    crosses = (me == B - 1) & (z < depth - 1)
    relays = (me < B - 1) & (z < depth - 1)

    def rim_near(p):
        source = (k_hbm, v_hbm)[p % 2].at[p // 2, interval - OFF :]
        return remote(source, rimraw.at[p], rim_send, rim_recv.at[p // 2], lax.rem(s + 1, n))

    def rim_far(p):
        source = (k_hbm, v_hbm)[p % 2].at[p // 2, interval - OFF :]
        return remote(source, rimrel, rim_send, rel_recv, z * B + lax.rem(p, B - 1))

    def rim_pass():
        p = jnp.where(me == 0, B - 1, me)
        return remote(rimrel, rimraw.at[p], rel_send, rim_recv.at[p // 2], lax.rem((z + 1) * B, n))

    @pl.when(me < B - 1)
    def _():
        for p in range(2 * requests):
            rim_near(p).start()

    @pl.when(crosses)
    def _():
        rim_near(0).start()
        rim_far(1).start()

    def w_copy(way, d, i, shard, target):
        b, count = units[i]
        return remote(
            wbuf.at[shard, b : b + count],
            wbuf.at[shard, b : b + count],
            w_send.at[way, d],
            w_recv.at[way, d, i],
            target * B + me,
        )

    def w_out(way, d):
        if way == 0:
            return z - d, z + 1, (z - d >= 0) & (z + 1 < depth)
        return z + d, z - 1, (z + d < depth) & (z - 1 >= 0)

    def w_in(way, d):
        if way == 0:
            return z - 1 - d, z - 1 - d >= 0
        return z + 1 + d, z + 1 + d < depth

    def w_own(first, end):
        for i in range(first, end):
            b, count = units[i]
            pltpu.make_async_copy(
                wbuf.at[z, b : b + count], wbuf.at[z, b : b + count], w_load.at[i]
            ).wait()
            for way in range(2):
                shard, target, there = w_out(way, 0)

                @pl.when(there)
                def _(way=way, i=i, shard=shard, target=target):
                    w_copy(way, 0, i, shard, target).start()

    def w_relay(d, i):
        for way in range(2):
            shard, target, onward = w_out(way, d)

            @pl.when(onward)
            def _(way=way, shard=shard, target=target):
                w_copy(way, d - 1, i, shard, z).wait_recv()
                w_copy(way, d, i, shard, target).start()

    ends = (z == 0) | (z == depth - 1)
    far = depth - 1 - z

    def w_wait(i, first, end):
        for way in range(2):
            for d in range(first, end):
                shard, there = w_in(way, d)
                there = there & ((z == depth - 1) if way == 0 else (z == 0))

                @pl.when(there)
                def _(way=way, d=d, shard=shard):
                    w_copy(way, d, i, shard, z).wait_recv()

    def rim_relay():
        with region("rimpass"):
            got(rimrel, rel_recv)
            rim_pass().start()

    w_own(0, 1)

    @pl.when(me != 1)
    def _():
        w_own(1, len(units))

    with region("prep"):
        for r in range(requests):
            slot = lax.broadcasted_iota(jnp.int32, (rows, nb), 1)
            position = lax.broadcasted_iota(jnp.int32, (rows, nb), 0) - OFF + phase_ref[r]
            lead = jnp.where(s == 0, phase_ref[r], 0)
            reach = (slot + 1) * ratio_ref[r, s] + lead
            allowed = (position >= lead) & (position < interval) & (position < reach)
            bias[r] = jnp.where(allowed, 0.0, masked_score).astype(bf16)
        for p in range(2 * requests):
            kv_load[p].wait()
            (kbuf, vbuf)[p % 2][p // 2, :, OFF:] = jnp.swapaxes((kraw, vraw)[p % 2][p // 2], 0, 1)
        chosen = lax.broadcasted_iota(jnp.int32, (nb, nb), 0) == lax.broadcasted_iota(
            jnp.int32, (nb, nb), 1
        )
        for g in range(G):
            qbuf[g, :, hd:] = jnp.where(chosen, 1.0, 0.0).astype(bf16)
        for copy in rest_load:
            copy.wait()
        for r in range(requests):
            rk_ref[r] = jnp.swapaxes(rkraw[r], 0, 1)
            rv_ref[r] = jnp.swapaxes(rvraw[r], 0, 1)
        steps = dqraw.shape[0]
        pair = steps * requests
        for k in range(heads):
            asked = jnp.stack(
                [dqraw[t, r, k].astype(f32) for t in range(steps) for r in range(requests)], axis=0
            )
            dq_ref[k] = jnp.swapaxes(asked, 0, 1).reshape(G * pair, hd).astype(bf16)
        q_load.wait()

    @pl.when(relays & (me == 1))
    def _():
        rim_relay()

    @pl.when(crosses)
    def _():
        for p in range(2, 2 * requests):
            rim_far(p).start()

    @pl.when(me == 1)
    def _():
        w_own(1, len(units))

    @pl.when(s == 0)
    def _():
        kbuf[:, :, :OFF] = jnp.zeros((requests, heads, OFF, hd), kbuf.dtype)
        vbuf[:, :, :OFF] = jnp.zeros((requests, heads, OFF, hd), vbuf.dtype)

    def a_remote(v, x):
        kk, r, y = v // 4, lax.rem(v, 2), lax.rem(v // 2, 2)
        return remote(
            stage.at[v, x],
            act.at[h * 2 + kk, r, me],
            a_send,
            a_recv.at[kk, r],
            z * B + y * 2 + x,
        )

    def a_local(kk, r, v):
        return pltpu.make_async_copy(
            stage.at[v, lax.rem(me, 2)], act.at[h * 2 + kk, r, me], a_loc.at[kk, r]
        )

    def a_relay(kk, r):
        return remote(
            act.at[h * 2 + kk, r], act.at[h * 2 + kk, r], p_send, p_recv
        )

    def a_gather(kk, r):
        a_local(kk, r, kk * 4 + (me // 2) * 2 + r).wait()
        got(act.at[0, 0, : B - 1], a_recv.at[kk, r])
        a_relay(kk, r).start()

    def unit(u, carry):
        r, k = u // heads, lax.rem(u, heads)
        v = k * 2 + r

        @pl.when((k == 0) & (s > 0))
        def _():
            with region("rimwait"):
                got(rimraw.at[:2], rim_recv.at[r])
            kbuf[r, :, :OFF] = jnp.swapaxes(rimraw[r * 2], 0, 1)
            vbuf[r, :, :OFF] = jnp.swapaxes(rimraw[r * 2 + 1], 0, 1)

        with region("att"):
            qbuf[:, :, :hd] = jnp.swapaxes(qraw[r, :, k], 0, 1)
            ones = jnp.ones((rows, hd), bf16)
            for first in range(0, G, GB):
                scores = lax.dot_general(
                    qbuf[first : first + GB].reshape(GB * nb, hd + nb),
                    jnp.concatenate([kbuf[r, k], bias[r]], axis=1),
                    (((1,), (1,)), ((), ())),
                    preferred_element_type=f32,
                )
                peak = jnp.max(scores, axis=-1, keepdims=True)
                weights = jnp.exp2((scores - peak) * to_log2).astype(bf16)
                out = jnp.dot(
                    weights,
                    jnp.concatenate([vbuf[r, k], ones], axis=1),
                    preferred_element_type=f32,
                )
                out = (out[:, :hd] / out[:, hd:]).astype(bf16)
                for g in range(first, first + GB):
                    at = (g % 4) * hd
                    stage[v, g // 4, :, at : at + hd] = out[(g - first) * nb : (g - first + 1) * nb]
        for x in range(2):
            member = lax.rem(k, 2) * 2 + x

            @pl.when(member == me)
            def _():
                a_local(k // 2, r, v).start()

            @pl.when(member != me)
            def _(x=x):
                a_remote(v, x).start()

        with region("relay"):

            @pl.when((u == jnp.where(me == 0, 1, 0)) & (me != 1) & relays)
            def _():
                rim_relay()

            for i in range(len(units)):

                @pl.when(u == min(i + 1 + i // 2, heads + 1))
                def _(i=i):
                    w_relay(1, i)

            @pl.when(u == heads + 1)
            def _():
                a_gather(0, 0)

            @pl.when(u == heads + 3)
            def _():
                a_gather(1, 0)
                w_relay(2, 0)

        return carry

    lax.fori_loop(0, 2 * heads, unit, 0)
    with region("gather"):
        a_gather(0, 1)
        a_gather(1, 1)
        for i in range(1, len(units)):
            w_relay(2, i)
        got(act.at[:2], p_recv)

    x_side = me + 1 - 2 * lax.rem(me, 2)
    y_side = lax.rem(me + 2, B)
    across = B - 1 - me
    straight = blocks - STRAIGHT

    def p_copy(lane, at):
        if at >= straight:
            i = min(at // 2, len(units) - 2) + (at == blocks - 1)
            return remote(
                psend.at[lane, at],
                pdiag.at[at] if lane == 0 else precv.at[lane - 1, at],
                s_send,
                (g_recv if lane == 0 else s_recv).at[i],
                z * B + (across, x_side, y_side)[lane],
            )
        if lane == 0:
            side, target = at % 2, pdiag.at[at]
        else:
            side = at % 2 if lane == 1 else 1 - at % 2
            target = precv.at[side, at]
        i = min(at // 2, len(units) - 2) + (at == blocks - 1)
        return remote(
            psend.at[lane, at],
            target,
            s_send,
            (g_recv if lane == 0 else s_recv).at[i],
            z * B + (x_side, y_side)[side],
        )

    slot_row = lax.broadcasted_iota(jnp.int32, (nb, hd), 0)

    def finish(i):
        b, count = units[i]
        with region(f"finish{i}"):
            got(precv.at[:, b : b + count], s_recv.at[i])
            if b >= straight:
                got(pdiag.at[b : b + count], g_recv.at[i])
        for at in range(b, b + count):
            total = own[at]
            for side in range(2):
                total += precv[side, at].astype(f32)
            if b >= straight:
                total += pdiag[at].astype(f32)
            out_ref = (bk_ref, bv_ref)[at // heads]
            for r in range(requests):
                live = (slot_row + 1) * ratio_ref[r, s] <= interval
                out_ref[at % heads, r * nb : (r + 1) * nb] = jnp.where(
                    live, total[r * nb : (r + 1) * nb], 0.0
                ).astype(bf16)

    def times(zi, to, b, count):
        return jnp.dot(
            act[zi, :, to].reshape(requests * nb, act.shape[4]),
            jnp.concatenate([wbuf[zi, at] for at in range(b, b + count)], axis=1),
            preferred_element_type=f32,
        )

    def near_products():
        near = jnp.where(z == 0, 0, 1)
        for b in range(0, blocks, 2):
            for i in range(len(units)):
                if b <= units[i][0] < b + 2:
                    w_wait(i, 0, depth - 2)

            def step(to, carry, b=b):
                total = times(near, to, b, 2)
                for zi in range(1, depth - 1):
                    total += times(near + zi, to, b, 2)
                for at in range(2):
                    acc[to, b + at] = total[:, at * hd : (at + 1) * hd]
                return carry

            lax.fori_loop(0, B, step, 0)

    def product(i, late):
        b, count = units[i]

        def step(o, carry):
            to = jnp.where(o == 0, across, jnp.where(o == 1, x_side, jnp.where(o == 2, y_side, me)))
            if late:
                total = jnp.concatenate([acc[to, b + at] for at in range(count)], axis=1)
                total += times(far, to, b, count)
            else:
                total = times(0, to, b, count)
                for zi in range(1, depth):
                    total += times(zi, to, b, count)

            def part_of(at):
                return total[:, (at - b) * hd : (at - b + 1) * hd]

            @pl.when(o == 0)
            def _():
                for at in range(b, b + count):
                    psend[0, at] = part_of(at).astype(bf16)
                    p_copy(0, at).start()

            for side in range(2):

                @pl.when(o == 1 + side)
                def _(side=side):
                    for at in range(b, b + count):
                        if at >= straight:
                            psend[1 + side, at] = part_of(at).astype(bf16)
                            p_copy(1 + side, at).start()
                        elif at % 2 == side:
                            psend[1, at] = part_of(at).astype(bf16)
                            p_copy(1, at).start()
                        else:
                            hold[at] = part_of(at)

            @pl.when(o == B - 1)
            def _():
                for at in range(b, b + count):
                    own[at] = part_of(at)

            return carry

        with region(f"prod{i}"):
            lax.fori_loop(0, B, step, 0)

    def forward(i):
        b, count = units[i]
        if b >= straight:
            return
        with region(f"forward{i}"):
            got(pdiag.at[b : b + count], g_recv.at[i])
            for at in range(b, b + count):
                psend[2, at] = (hold[at] + pdiag[at].astype(f32)).astype(bf16)
                p_copy(2, at).start()

    res = rk_ref.shape[2]
    qrows = dq_ref.shape[1]
    mergers = snd.shape[0]
    share = G * heads // mergers
    slots = hd // (2 * share)
    per_head = G // share
    first_merger = (depth // 2) * B - mergers // 2
    mine = s - first_merger
    merges = (mine >= 0) & (mine < mergers)

    def e_copy(to):
        return remote(snd_stats.at[to], rcv_stats.at[s], e_send, e_recv, first_merger + to)

    def d_copy(to):
        return remote(snd.at[to], rcv.at[s], d_send, d_recv, first_merger + to)

    def to_mergers(copy, first, end):
        for to in range(first, end):

            @pl.when(mine != to)
            def _(to=to):
                copy(to).start()

    def scored(k, r, key, mask):
        scores = lax.dot_general(
            dq_ref[k], key, (((1,), (1,)), ((), ())), preferred_element_type=f32
        )
        return jnp.where(mask, scores * inv_root, masked_score)

    def row_of(count):
        return (
            lax.rem(lax.broadcasted_iota(jnp.int32, (qrows, count), 0), requests),
            lax.broadcasted_iota(jnp.int32, (qrows, count), 1),
        )

    def decode_early():
        row_request, cell = row_of(res)
        row_rim, rim = row_of(OFF)
        last = jnp.where(s == n - 1, 1, 0)
        for k in range(heads):
            pieces = []
            for r in range(requests):
                usable = (cell < rlen_ref[r, s]) & (row_request == r)
                pieces.append((scored(k, r, rk_ref[r, k], usable), rv_ref, r, slice(0, res)))
                usable = (rim >= OFF - phase_ref[r] * last) & (row_rim == r)
                left = slice(rows - OFF, rows)
                pieces.append((scored(k, r, kbuf[r, k, left], usable), vbuf, r, left))
            peak = jnp.max(pieces[0][0], axis=-1, keepdims=True)
            for piece in pieces[1:]:
                peak = jnp.maximum(peak, jnp.max(piece[0], axis=-1, keepdims=True))
            total = jnp.zeros((qrows, 1), f32)
            out = jnp.zeros((qrows, hd), f32)
            for scores, source, r, span in pieces:
                weights = jnp.exp(scores - peak)
                total += jnp.sum(weights, axis=-1, keepdims=True)
                out += jnp.dot(weights.astype(bf16), source[r, k, span], preferred_element_type=f32)
            dacc[k] = out
            dstat[k, 0] = jnp.broadcast_to(peak, (qrows, hd))
            dstat[k, 1] = jnp.broadcast_to(total, (qrows, hd))

    def decode_weights():
        row_request, slot = row_of(nb)
        for k in range(heads):
            pieces = []
            for r in range(requests):
                usable = ((slot + 1) * ratio_ref[r, s] <= interval) & (row_request == r)
                pieces.append(scored(k, r, bk_ref[k, r * nb : (r + 1) * nb], usable))
            former = dstat[k, 0]
            peak = former
            for piece in pieces:
                peak = jnp.maximum(peak, jnp.max(piece, axis=-1, keepdims=True))
            scale = jnp.exp(former - peak)
            total = dstat[k, 1] * scale
            for r in range(requests):
                weights = jnp.exp(pieces[r] - peak)
                total += jnp.sum(weights, axis=-1, keepdims=True)
                dlow[k, r] = weights.astype(bf16)
            dacc[k] = dacc[k] * scale
            lane = lax.broadcasted_iota(jnp.int32, (qrows, hd), 1)
            stats = jnp.where(lax.rem(lane // slots, 2) == 0, peak, total)
            stats = stats.reshape(per_head, share, pair, hd)
            lane = lax.broadcasted_iota(jnp.int32, (per_head, pair, hd), 2)
            packed = stats[:, 0]
            for j in range(1, share):
                packed = jnp.where(lane >= 2 * slots * j, stats[:, j], packed)
            snd_stats[k * per_head : (k + 1) * per_head] = packed
        to_mergers(e_copy, 0, mergers)

    def decode_values(k):
        out = dacc[k]
        for r in range(requests):
            out += jnp.dot(
                dlow[k, r], bv_ref[k, r * nb : (r + 1) * nb], preferred_element_type=f32
            )
        snd[k * per_head : (k + 1) * per_head] = out.reshape(per_head, share * pair, hd).astype(bf16)
        to_mergers(d_copy, k * per_head, (k + 1) * per_head)

    outs = []

    def emit(made, made_rows, out):
        made_rows[...] = jnp.swapaxes(made[...], 0, 1)
        outs.append(pltpu.make_async_copy(made_rows, out, out_sem.at[len(outs)]))
        outs[-1].start()

    key_units = heads // 2

    @pl.when(ends)
    def _():
        with region("near"):
            near_products()

    for i in range(len(units)):
        @pl.when(ends)
        def _(i=i):
            with region(f"wwait{i}"):
                w_wait(i, depth - 2, depth - 1)
            product(i, True)

        @pl.when(jnp.logical_not(ends))
        def _(i=i):
            product(i, False)

        if i > 0:
            forward(i - 1)
        if i == 1:
            with region("early"):
                decode_early()
    forward(len(units) - 1)
    for i in range(key_units):
        finish(i)
    with region("decode"):
        decode_weights()
    for i in range(key_units, len(units)):
        finish(i)
        b, count = units[i]
        with region("values"):
            for at in range(b, b + count):
                decode_values(at - heads)

    emit(bk_ref, bk_rows, bk_out)
    emit(bv_ref, bv_rows, bv_out)

    with region("drain"):
        sent(psend, s_send)
        sent(act.at[:2], p_send)
        sent(stage.at[: requests * heads * (B - 1) // B], a_send)
        for way in range(2):
            for d in range(depth - 1):
                shard, target, there = w_out(way, d)

                @pl.when(there)
                def _(way=way, d=d, shard=shard):
                    sent(wbuf.at[shard], w_send.at[way, d])

        @pl.when((me < B - 1) | crosses)
        def _():
            sent(rimraw, rim_send)

        @pl.when(relays)
        def _():
            sent(rimrel, rel_send)

    early = mergers - mergers // heads
    late = jnp.where(mine >= early, 1, 0)

    def t_copy(to):
        return remote(att.at[mine], att.at[mine], t_send, t_recv.at[late], to)

    with region("merge"):

        @pl.when(merges)
        def _():
            rcv[s] = snd[mine]
            rcv_stats[s] = snd_stats[mine]
            got(rcv_stats.at[: n - 1], e_recv)
            got(rcv.at[: n - 1], d_recv)
            landed = rcv[...].astype(f32)
            attended = []
            for j in range(share):
                at = 2 * slots * j
                peaks = rcv_stats[:, :, at : at + 1]
                sums = rcv_stats[:, :, at + slots : at + slots + 1]
                scale = jnp.exp(peaks - jnp.max(peaks, axis=0, keepdims=True))
                mixed = jnp.sum(scale * landed[:, j * pair : (j + 1) * pair], axis=0)
                attended.append(mixed / jnp.sum(scale * sums, axis=0))
            att[mine] = jnp.concatenate(attended, axis=0).astype(bf16)
            for o in range(1, n):
                t_copy(lax.rem(s + o, n)).start()
            sent(snd.at[: mergers - 1], d_send)
            sent(snd_stats.at[: mergers - 1], e_send)

        @pl.when(jnp.logical_not(merges))
        def _():
            sent(snd, d_send)
            sent(snd_stats, e_send)

    ow_load.wait()

    def attended_rows(first, end, group):
        @pl.when(merges & (late == group))
        def _():
            got(att.at[first : end - 1], t_recv.at[group])

        @pl.when(jnp.logical_not(merges & (late == group)))
        def _():
            got(att.at[first:end], t_recv.at[group])

        wide = [att[i].astype(f32) for i in range(first, end)]
        vectors = jnp.concatenate(
            [piece[j * pair : (j + 1) * pair] for piece in wide for j in range(share)], axis=1
        ).astype(bf16)
        span = share * hd
        return jnp.dot(vectors, owbuf[first * span : end * span], preferred_element_type=f32)

    with region("twait"):
        sums = attended_rows(0, early, 0)
    with region("twait2"):
        sums += attended_rows(early, mergers, 1)
    part[...] = sums
    swap = remote(part, part_out.at[h], h_send, h_recv)
    swap.start()
    outs.append(pltpu.make_async_copy(part, part_out.at[h], out_sem.at[len(outs)]))
    outs[-1].start()
    with region("swap"):

        @pl.when(merges)
        def _():
            sent(rcv.at[: n - 1], t_send)

        swap.wait()
        for copy in outs:
            copy.wait()


def handed_on(keys_ref, values_ref, part_ref, keys_out, values_out, projected_out):
    keys_out[...] = keys_ref[...]
    values_out[...] = values_ref[...]
    summed = (part_ref[0] + part_ref[1]).astype(projected_out.dtype)
    steps, requests, _ = projected_out.shape
    for t in range(steps):
        projected_out[t] = summed[t * requests : (t + 1) * requests]


def fused_body(
    shard_count,
    raw_keys,
    raw_values,
    phase,
    ratio,
    resident_len,
    beacon_queries,
    beacon_wk,
    beacon_wv,
    resident_keys,
    resident_values,
    decode_queries,
    out_weight,
):
    n = shard_count
    depth = n // B
    requests, interval, heads, hd = raw_keys.shape
    steps = decode_queries.shape[0]
    nb = beacon_queries.shape[1]
    rows = interval + OFF
    res = resident_keys.shape[1]
    feature, columns = beacon_wk.shape
    blocks = 2 * columns // hd
    units = blocks // 2 + 1
    pair = requests * steps
    mergers = min(2 * B, n)
    share = G * heads // mergers
    bf16, f32 = jnp.bfloat16, jnp.float32
    dma = pltpu.SemaphoreType.DMA
    smem = pl.BlockSpec(memory_space=pltpu.SMEM)
    anywhere = pl.BlockSpec(memory_space=pl.ANY)
    vmem = pl.BlockSpec(memory_space=pltpu.VMEM)
    keys, values, partial_sums = pl.pallas_call(
        functools.partial(fused_kernel, n),
        out_shape=(
            jax.ShapeDtypeStruct((requests * nb, heads, hd), bf16),
            jax.ShapeDtypeStruct((requests * nb, heads, hd), bf16),
            jax.ShapeDtypeStruct((2, pair, out_weight.shape[1]), f32),
        ),
        in_specs=[smem] * 3 + [anywhere] * 9,
        out_specs=(anywhere, anywhere, anywhere),
        scratch_shapes=[
            pltpu.VMEM(raw_keys.shape, bf16),
            pltpu.VMEM(raw_values.shape, bf16),
            pltpu.VMEM(beacon_queries.shape, bf16),
            pltpu.VMEM(resident_keys.shape, bf16),
            pltpu.VMEM(resident_values.shape, bf16),
            pltpu.VMEM(decode_queries.shape, bf16),
            pltpu.VMEM((2 * requests, OFF, heads, hd), bf16),
            pltpu.VMEM((OFF, heads, hd), bf16),
            pltpu.VMEM((requests, heads, rows, hd), bf16),
            pltpu.VMEM((requests, heads, rows, hd), bf16),
            pltpu.VMEM((G, nb, hd + nb), bf16),
            pltpu.VMEM((depth, blocks, feature, hd), bf16),
            pltpu.VMEM((depth, requests, B, nb, feature), bf16),
            pltpu.VMEM((requests * heads, 2, nb, feature), bf16),
            pltpu.VMEM((3, blocks, requests * nb, hd), bf16),
            pltpu.VMEM((2, blocks, requests * nb, hd), bf16),
            pltpu.VMEM((blocks, requests * nb, hd), bf16),
            pltpu.VMEM((blocks, requests * nb, hd), f32),
            pltpu.VMEM((blocks, requests * nb, hd), f32),
            pltpu.VMEM((B, blocks, requests * nb, hd), f32),
            pltpu.VMEM((requests, rows, nb), bf16),
            pltpu.VMEM(out_weight.shape, bf16),
            pltpu.VMEM((requests, heads, res, hd), bf16),
            pltpu.VMEM((requests, heads, res, hd), bf16),
            pltpu.VMEM((heads, G * pair, hd), bf16),
            pltpu.VMEM((heads, requests * nb, hd), bf16),
            pltpu.VMEM((heads, requests * nb, hd), bf16),
            pltpu.VMEM((heads, G * pair, hd), f32),
            pltpu.VMEM((heads, 2, G * pair, hd), f32),
            pltpu.VMEM((heads, requests, G * pair, nb), bf16),
            pltpu.VMEM((mergers, share * pair, hd), bf16),
            pltpu.VMEM((mergers, pair, hd), f32),
            pltpu.VMEM((n, share * pair, hd), bf16),
            pltpu.VMEM((n, pair, hd), f32),
            pltpu.VMEM((mergers, share * pair, hd), bf16),
            pltpu.VMEM((pair, out_weight.shape[1]), f32),
            pltpu.VMEM((requests * nb, heads, hd), bf16),
            pltpu.VMEM((requests * nb, heads, hd), bf16),
            dma((2 * requests + 5,)),
            dma((units,)),
            dma((3,)),
            dma,
            dma((requests,)),
            dma,
            dma,
            dma((2, depth - 1)),
            dma((2, depth - 1, units)),
            dma,
            dma((2, requests)),
            dma((2, requests)),
            dma,
            dma,
            dma,
            dma((units,)),
            dma((units,)),
            dma,
            dma,
            dma,
            dma,
            dma,
            dma((2,)),
            dma,
            dma,
        ],
        compiler_params=pltpu.CompilerParams(
            collective_id=0, has_side_effects=True, vmem_limit_bytes=60 * 1024 * 1024
        ),
    )(
        phase,
        ratio,
        resident_len,
        raw_keys,
        raw_values,
        beacon_queries,
        beacon_wk,
        beacon_wv,
        resident_keys,
        resident_values,
        decode_queries,
        out_weight,
    )
    keys, values, projected = pl.pallas_call(
        handed_on,
        out_shape=(
            jax.ShapeDtypeStruct(keys.shape, bf16),
            jax.ShapeDtypeStruct(values.shape, bf16),
            jax.ShapeDtypeStruct((steps, requests, out_weight.shape[1]), bf16),
        ),
        in_specs=[vmem] * 3,
        out_specs=(vmem,) * 3,
    )(keys, values, partial_sums)
    return (
        keys.reshape(requests, nb, heads, hd),
        values.reshape(requests, nb, heads, hd),
        projected,
    )


def chosen_body(shard_count, head_count):
    def run(*arrays):
        requests, _, heads, hd = arrays[0].shape
        feature = arrays[6].shape[0]
        fits = (
            head_count == 2
            and shard_count == B * B
            and requests == 2
            and heads == B
            and 2 * feature == G * hd
        )
        return fused_body(shard_count, *arrays) if fits else body(*arrays)

    return run


def solution(mesh):
    return jax.shard_map(
        chosen_body(mesh.shape["seq"], mesh.shape["head"]),
        mesh=mesh,
        in_specs=(
            P(None, "seq", "head", None),
            P(None, "seq", "head", None),
            P(),
            P(),
            P(),
            P(None, "seq", "head", None, None),
            P("seq", "head"),
            P("seq", "head"),
            P(None, "seq", "head", None),
            P(None, "seq", "head", None),
            P(None, None, "head", None, None),
            P("head", "seq"),
        ),
        out_specs=(
            P(None, "seq", "head", None),
            P(None, "seq", "head", None),
            P(None, None, "seq"),
        ),
        check_vma=False,
    )
```

```python
import contextlib
import functools
import math

import jax
import jax.numpy as jnp
from jax import lax
from jax.experimental import pallas as pl
from jax.experimental.pallas import tpu as pltpu
from jax.sharding import PartitionSpec as P

G = 8
INTERVAL = 1024
NB = 128
OFF = 256
STEPS = 4


masked_score = -1e30


def region(name):
    return contextlib.nullcontext()


def shifted(value, axis, steps):
    count = lax.axis_size(axis)
    first, last = (max(0, -steps), min(count, count - steps))
    return lax.ppermute(value, axis, [(source, source + steps) for source in range(first, last)])


def joined(shard, axis, combine):
    everything = jax.tree.map(lambda part: lax.all_gather(part, axis), shard)
    first = jax.tree.map(lambda part: part[0], everything)

    def hop(k, so_far):
        return combine(so_far, jax.tree.map(lambda part: part[k], everything))

    return lax.fori_loop(1, lax.axis_size(axis), hop, first)


def blend(former, latter):
    row_peak = jnp.maximum(former[0], latter[0])
    former_scale = jnp.exp(former[0] - row_peak)
    latter_scale = jnp.exp(latter[0] - row_peak)
    weight_sum = former[1] * former_scale + latter[1] * latter_scale
    weighted = former[2] * former_scale[..., None] + latter[2] * latter_scale[..., None]
    return (row_peak, weight_sum, weighted)


def pool_part(queries, key_rows, value_rows, positions, present, reaches):
    inv_root = 1.0 / math.sqrt(queries.shape[-1])

    def per_request(members):
        query_block, key_block, value_block, position_row, present_row, reach_row = members
        scores = (
            jnp.einsum("jkgd,ikd->jkgi", query_block, key_block, preferred_element_type=jnp.float32)
            * inv_root
        )
        allowed = (
            present_row[None, :]
            & (position_row[None, :] >= 0)
            & (position_row[None, :] < INTERVAL)
            & (position_row[None, :] < reach_row[:, None])
        )
        cache_mask = allowed[:, None, None, :]
        row_peak = jnp.max(jnp.where(cache_mask, scores, masked_score), axis=-1)
        weights = jnp.where(cache_mask, jnp.exp(scores - row_peak[..., None]), 0.0)
        weight_sum = jnp.sum(weights, axis=-1)
        weighted = jnp.einsum(
            "jkgi,ikd->jkgd",
            weights.astype(jnp.bfloat16),
            value_block,
            preferred_element_type=jnp.float32,
        )
        return (row_peak, weight_sum, weighted)

    return lax.map(per_request, (queries, key_rows, value_rows, positions, present, reaches))


def body(
    raw_keys,
    raw_values,
    phase,
    ratio,
    resident_len,
    beacon_queries,
    beacon_wk,
    beacon_wv,
    resident_keys,
    resident_values,
    decode_queries,
    out_weight,
):
    requests = raw_keys.shape[0]
    kv_local = raw_keys.shape[2]
    head_dim = raw_keys.shape[3]
    shard_index = lax.axis_index("seq")
    shard_count = lax.axis_size("seq")
    is_first = shard_index == 0
    is_last = shard_index == shard_count - 1
    own_ratio = lax.dynamic_index_in_dim(ratio, shard_index, 1, keepdims=False)
    slot_ids = jnp.arange(NB, dtype=jnp.int32)
    lead_in = jnp.where(is_first, phase, 0)
    reaches = (slot_ids[None, :] + 1) * own_ratio[:, None] + lead_in[:, None]
    tail_keys = raw_keys[:, INTERVAL - OFF :]
    tail_values = raw_values[:, INTERVAL - OFF :]
    own_positions = jnp.arange(INTERVAL, dtype=jnp.int32)[None, :] + phase[:, None]
    rim_ids = jnp.arange(OFF, dtype=jnp.int32)
    rim_positions = rim_ids[None, :] - OFF + phase[:, None]
    near_keys, near_values = shifted((tail_keys, tail_values), "seq", 1)
    key_rows = jnp.concatenate([near_keys, raw_keys], axis=1)
    value_rows = jnp.concatenate([near_values, raw_values], axis=1)
    positions = jnp.concatenate([rim_positions, own_positions], axis=1)
    present = jnp.logical_not(is_first) | (positions >= phase[:, None])
    pooled_parts = pool_part(beacon_queries, key_rows, value_rows, positions, present, reaches)
    pooled = (pooled_parts[2] / pooled_parts[1][..., None]).astype(jnp.bfloat16)
    pooled_flat = pooled.reshape(requests * NB, kv_local * G * head_dim)
    pooled_whole = lax.all_gather(pooled_flat, "head", axis=1, tiled=True)
    key_sum = jnp.dot(
        pooled_whole,
        lax.all_gather(beacon_wk, "seq", axis=0, tiled=True),
        preferred_element_type=jnp.float32,
    )
    value_sum = jnp.dot(
        pooled_whole,
        lax.all_gather(beacon_wv, "seq", axis=0, tiled=True),
        preferred_element_type=jnp.float32,
    )
    made_keys = key_sum
    made_values = value_sum
    made_keys = made_keys.reshape(requests, NB, kv_local, head_dim)
    made_values = made_values.reshape(requests, NB, kv_local, head_dim)
    slot_live = slot_ids[None, :] < (INTERVAL // own_ratio)[:, None]
    beacon_keys = jnp.where(slot_live[:, :, None, None], made_keys, 0.0).astype(jnp.bfloat16)
    beacon_values = jnp.where(slot_live[:, :, None, None], made_values, 0.0).astype(jnp.bfloat16)
    cache_keys = jnp.concatenate([resident_keys, beacon_keys, tail_keys], axis=1)
    cache_values = jnp.concatenate([resident_values, beacon_values, tail_values], axis=1)
    own_len = lax.dynamic_index_in_dim(resident_len, shard_index, 1, keepdims=False)
    resident_ok = jnp.arange(resident_keys.shape[1], dtype=jnp.int32)[None, :] < own_len[:, None]
    leftover_ok = (rim_ids[None, :] >= OFF - phase[:, None]) & is_last
    usable = jnp.concatenate([resident_ok, slot_live, leftover_ok], axis=1)
    inv_root = 1.0 / math.sqrt(head_dim)
    scores = (
        jnp.einsum(
            "srkgd,rikd->rksgi", decode_queries, cache_keys, preferred_element_type=jnp.float32
        )
        * inv_root
    )
    cache_mask = usable[:, None, None, None, :]
    row_peak = jnp.max(jnp.where(cache_mask, scores, masked_score), axis=-1)
    weights = jnp.where(cache_mask, jnp.exp(scores - row_peak[..., None]), 0.0)
    weight_sum = jnp.sum(weights, axis=-1)
    weighted = jnp.einsum(
        "rksgi,rikd->rksgd",
        weights.astype(jnp.bfloat16),
        cache_values,
        preferred_element_type=jnp.float32,
    )
    merged = joined((row_peak, weight_sum, weighted), "seq", blend)
    total_sum = merged[1]
    total_weighted = merged[2]
    attended = (total_weighted / total_sum[..., None]).astype(jnp.bfloat16)
    attended = jnp.transpose(attended, (2, 0, 1, 3, 4)).reshape(
        STEPS * requests, kv_local * G * head_dim
    )
    partial_value = jnp.dot(attended, out_weight, preferred_element_type=jnp.float32)
    summed = lax.psum(partial_value, "head")
    projected = summed.astype(jnp.bfloat16).reshape(STEPS, requests, out_weight.shape[1])
    return (beacon_keys, beacon_values, projected)


B = 4
GB = 2
STRAIGHT = 2


def fused_kernel(
    shard_count,
    phase_ref,
    ratio_ref,
    rlen_ref,
    k_hbm,
    v_hbm,
    q_hbm,
    wk_hbm,
    wv_hbm,
    rk_hbm,
    rv_hbm,
    dq_hbm,
    ow_hbm,
    bk_out,
    bv_out,
    part_out,
    kraw,
    vraw,
    qraw,
    rkraw,
    rvraw,
    dqraw,
    rimraw,
    rimrel,
    kbuf,
    vbuf,
    qbuf,
    wbuf,
    act,
    stage,
    psend,
    precv,
    pdiag,
    hold,
    own,
    acc,
    bias,
    owbuf,
    rk_ref,
    rv_ref,
    dq_ref,
    bk_ref,
    bv_ref,
    dacc,
    dstat,
    dlow,
    snd,
    snd_stats,
    rcv,
    rcv_stats,
    att,
    part,
    bk_rows,
    bv_rows,
    load_sem,
    w_load,
    out_sem,
    rim_send,
    rim_recv,
    rel_send,
    rel_recv,
    w_send,
    w_recv,
    a_send,
    a_recv,
    a_loc,
    p_send,
    p_recv,
    s_send,
    s_recv,
    g_recv,
    d_send,
    d_recv,
    e_send,
    e_recv,
    t_send,
    t_recv,
    h_send,
    h_recv,
):
    n = shard_count
    depth = n // B
    s = lax.axis_index("seq")
    h = lax.axis_index("head")
    z = s // B
    me = lax.rem(s, B)
    requests, interval, heads, hd = kraw.shape
    rows = interval + OFF
    nb = psend.shape[2] // requests
    blocks = wbuf.shape[1]
    units = [(b, 2) for b in range(0, blocks - 2, 2)] + [(blocks - 2, 1), (blocks - 1, 1)]
    inv_root = 1.0 / math.sqrt(hd)
    to_log2 = inv_root / math.log(2.0)
    f32 = jnp.float32
    bf16 = jnp.bfloat16

    def remote(src, dst, send, recv, seq=None):
        target = {"head": 1 - h} if seq is None else {"seq": seq}
        return pltpu.make_async_remote_copy(
            src_ref=src,
            dst_ref=dst,
            send_sem=send,
            recv_sem=recv,
            device_id=target,
            device_id_type=pl.DeviceIdType.MESH,
        )

    def got(ref, sem):
        remote(ref, ref, sem, sem, s).wait_recv()

    def sent(ref, sem):
        remote(ref, ref, sem, sem, s).wait_send()

    barrier = pltpu.get_barrier_semaphore()
    for o in range(1, n):
        pl.semaphore_signal(
            barrier,
            inc=1,
            device_id={"seq": lax.rem(s + o, n)},
            device_id_type=pl.DeviceIdType.MESH,
        )
    pl.semaphore_signal(
        barrier, inc=1, device_id={"head": 1 - h}, device_id_type=pl.DeviceIdType.MESH
    )

    loads = []

    def load(source, target):
        loads.append(pltpu.make_async_copy(source, target, load_sem.at[len(loads)]))
        loads[-1].start()
        return loads[-1]

    for i, (b, count) in enumerate(units):
        for at in range(b, b + count):
            source = (wk_hbm, wv_hbm)[at // heads].at[:, (at % heads) * hd : (at % heads + 1) * hd]
            pltpu.make_async_copy(source, wbuf.at[z, at], w_load.at[i]).start()
    kv_load = [
        load((k_hbm, v_hbm)[p % 2].at[p // 2], (kraw, vraw)[p % 2].at[p // 2])
        for p in range(2 * requests)
    ]
    q_load = load(q_hbm, qraw)
    rest_load = [load(rk_hbm, rkraw), load(rv_hbm, rvraw), load(dq_hbm, dqraw)]
    ow_load = load(ow_hbm, owbuf)

    with region("barrier"):
        pl.semaphore_wait(barrier, n)

    crosses = (me == B - 1) & (z < depth - 1)
    relays = (me < B - 1) & (z < depth - 1)

    def rim_near(p):
        source = (k_hbm, v_hbm)[p % 2].at[p // 2, interval - OFF :]
        return remote(source, rimraw.at[p], rim_send, rim_recv.at[p // 2], lax.rem(s + 1, n))

    def rim_far(p):
        source = (k_hbm, v_hbm)[p % 2].at[p // 2, interval - OFF :]
        return remote(source, rimrel, rim_send, rel_recv, z * B + lax.rem(p, B - 1))

    def rim_pass():
        p = jnp.where(me == 0, B - 1, me)
        return remote(rimrel, rimraw.at[p], rel_send, rim_recv.at[p // 2], lax.rem((z + 1) * B, n))

    @pl.when(me < B - 1)
    def _():
        for p in range(2 * requests):
            rim_near(p).start()

    @pl.when(crosses)
    def _():
        rim_near(0).start()
        rim_far(1).start()

    def w_copy(way, d, i, shard, target):
        b, count = units[i]
        return remote(
            wbuf.at[shard, b : b + count],
            wbuf.at[shard, b : b + count],
            w_send.at[way, d],
            w_recv.at[way, d, i],
            target * B + me,
        )

    def w_out(way, d):
        if way == 0:
            return z - d, z + 1, (z - d >= 0) & (z + 1 < depth)
        return z + d, z - 1, (z + d < depth) & (z - 1 >= 0)

    def w_in(way, d):
        if way == 0:
            return z - 1 - d, z - 1 - d >= 0
        return z + 1 + d, z + 1 + d < depth

    def w_own(first, end):
        for i in range(first, end):
            b, count = units[i]
            pltpu.make_async_copy(
                wbuf.at[z, b : b + count], wbuf.at[z, b : b + count], w_load.at[i]
            ).wait()
            for way in range(2):
                shard, target, there = w_out(way, 0)

                @pl.when(there)
                def _(way=way, i=i, shard=shard, target=target):
                    w_copy(way, 0, i, shard, target).start()

    def w_relay(d, i):
        for way in range(2):
            shard, target, onward = w_out(way, d)

            @pl.when(onward)
            def _(way=way, shard=shard, target=target):
                w_copy(way, d - 1, i, shard, z).wait_recv()
                w_copy(way, d, i, shard, target).start()

    ends = (z == 0) | (z == depth - 1)
    far = depth - 1 - z

    def w_wait(i, first, end):
        for way in range(2):
            for d in range(first, end):
                shard, there = w_in(way, d)
                there = there & ((z == depth - 1) if way == 0 else (z == 0))

                @pl.when(there)
                def _(way=way, d=d, shard=shard):
                    w_copy(way, d, i, shard, z).wait_recv()

    def rim_relay():
        with region("rimpass"):
            got(rimrel, rel_recv)
            rim_pass().start()

    w_own(0, 1)

    @pl.when(me != 1)
    def _():
        w_own(1, len(units))

    with region("prep"):
        for r in range(requests):
            slot = lax.broadcasted_iota(jnp.int32, (rows, nb), 1)
            position = lax.broadcasted_iota(jnp.int32, (rows, nb), 0) - OFF + phase_ref[r]
            lead = jnp.where(s == 0, phase_ref[r], 0)
            reach = (slot + 1) * ratio_ref[r, s] + lead
            allowed = (position >= lead) & (position < interval) & (position < reach)
            bias[r] = jnp.where(allowed, 0.0, masked_score).astype(bf16)
        for p in range(2 * requests):
            kv_load[p].wait()
            (kbuf, vbuf)[p % 2][p // 2, :, OFF:] = jnp.swapaxes((kraw, vraw)[p % 2][p // 2], 0, 1)
        chosen = lax.broadcasted_iota(jnp.int32, (nb, nb), 0) == lax.broadcasted_iota(
            jnp.int32, (nb, nb), 1
        )
        for g in range(G):
            qbuf[g, :, hd:] = jnp.where(chosen, 1.0, 0.0).astype(bf16)
        for copy in rest_load:
            copy.wait()
        for r in range(requests):
            rk_ref[r] = jnp.swapaxes(rkraw[r], 0, 1)
            rv_ref[r] = jnp.swapaxes(rvraw[r], 0, 1)
        steps = dqraw.shape[0]
        pair = steps * requests
        for k in range(heads):
            asked = jnp.stack(
                [dqraw[t, r, k].astype(f32) for t in range(steps) for r in range(requests)], axis=0
            )
            dq_ref[k] = jnp.swapaxes(asked, 0, 1).reshape(G * pair, hd).astype(bf16)
        q_load.wait()

    @pl.when(relays & (me == 1))
    def _():
        rim_relay()

    @pl.when(crosses)
    def _():
        for p in range(2, 2 * requests):
            rim_far(p).start()

    @pl.when(me == 1)
    def _():
        w_own(1, len(units))

    @pl.when(s == 0)
    def _():
        kbuf[:, :, :OFF] = jnp.zeros((requests, heads, OFF, hd), kbuf.dtype)
        vbuf[:, :, :OFF] = jnp.zeros((requests, heads, OFF, hd), vbuf.dtype)

    def a_remote(v, x):
        kk, r, y = v // 4, lax.rem(v, 2), lax.rem(v // 2, 2)
        return remote(
            stage.at[v, x],
            act.at[h * 2 + kk, r, me],
            a_send,
            a_recv.at[kk, r],
            z * B + y * 2 + x,
        )

    def a_local(kk, r, v):
        return pltpu.make_async_copy(
            stage.at[v, lax.rem(me, 2)], act.at[h * 2 + kk, r, me], a_loc.at[kk, r]
        )

    def a_relay(kk, r):
        return remote(
            act.at[h * 2 + kk, r], act.at[h * 2 + kk, r], p_send, p_recv
        )

    def a_gather(kk, r):
        a_local(kk, r, kk * 4 + (me // 2) * 2 + r).wait()
        got(act.at[0, 0, : B - 1], a_recv.at[kk, r])
        a_relay(kk, r).start()

    def unit(u, carry):
        r, k = u // heads, lax.rem(u, heads)
        v = k * 2 + r

        @pl.when((k == 0) & (s > 0))
        def _():
            with region("rimwait"):
                got(rimraw.at[:2], rim_recv.at[r])
            kbuf[r, :, :OFF] = jnp.swapaxes(rimraw[r * 2], 0, 1)
            vbuf[r, :, :OFF] = jnp.swapaxes(rimraw[r * 2 + 1], 0, 1)

        with region("att"):
            qbuf[:, :, :hd] = jnp.swapaxes(qraw[r, :, k], 0, 1)
            ones = jnp.ones((rows, hd), bf16)
            for first in range(0, G, GB):
                scores = lax.dot_general(
                    qbuf[first : first + GB].reshape(GB * nb, hd + nb),
                    jnp.concatenate([kbuf[r, k], bias[r]], axis=1),
                    (((1,), (1,)), ((), ())),
                    preferred_element_type=f32,
                )
                peak = jnp.max(scores, axis=-1, keepdims=True)
                weights = jnp.exp2((scores - peak) * to_log2).astype(bf16)
                out = jnp.dot(
                    weights,
                    jnp.concatenate([vbuf[r, k], ones], axis=1),
                    preferred_element_type=f32,
                )
                out = (out[:, :hd] / out[:, hd:]).astype(bf16)
                for g in range(first, first + GB):
                    at = (g % 4) * hd
                    stage[v, g // 4, :, at : at + hd] = out[(g - first) * nb : (g - first + 1) * nb]
        for x in range(2):
            member = lax.rem(k, 2) * 2 + x

            @pl.when(member == me)
            def _():
                a_local(k // 2, r, v).start()

            @pl.when(member != me)
            def _(x=x):
                a_remote(v, x).start()

        with region("relay"):

            @pl.when((u == jnp.where(me == 0, 1, 0)) & (me != 1) & relays)
            def _():
                rim_relay()

            for i in range(3):

                @pl.when(u == heads - 2 + i)
                def _(i=i):
                    w_relay(1, i)

            @pl.when(u == heads + 2)
            def _():
                w_relay(2, 0)

            @pl.when(u == heads + 1)
            def _():
                a_gather(0, 0)

            @pl.when(u == heads + 3)
            def _():
                a_gather(1, 0)

        return carry

    lax.fori_loop(0, 2 * heads, unit, 0)
    with region("gather"):
        w_relay(2, 1)
        a_gather(0, 1)
        a_gather(1, 1)
        w_relay(2, 2)
        w_relay(1, 3)
        w_relay(1, 4)
        got(act.at[:2], p_recv)

    x_side = me + 1 - 2 * lax.rem(me, 2)
    y_side = lax.rem(me + 2, B)
    across = B - 1 - me
    straight = blocks - STRAIGHT

    def p_copy(lane, at):
        if at >= straight:
            i = min(at // 2, len(units) - 2) + (at == blocks - 1)
            return remote(
                psend.at[lane, at],
                pdiag.at[at] if lane == 0 else precv.at[lane - 1, at],
                s_send,
                (g_recv if lane == 0 else s_recv).at[i],
                z * B + (across, x_side, y_side)[lane],
            )
        if lane == 0:
            side, target = at % 2, pdiag.at[at]
        else:
            side = at % 2 if lane == 1 else 1 - at % 2
            target = precv.at[side, at]
        i = min(at // 2, len(units) - 2) + (at == blocks - 1)
        return remote(
            psend.at[lane, at],
            target,
            s_send,
            (g_recv if lane == 0 else s_recv).at[i],
            z * B + (x_side, y_side)[side],
        )

    key_units = heads // 2
    slot_row = lax.broadcasted_iota(jnp.int32, (nb, hd), 0)

    def finish(i):
        b, count = units[i]
        with region(f"finish{i}"):
            got(precv.at[:, b : b + count], s_recv.at[i])
            if b >= straight:
                got(pdiag.at[b : b + count], g_recv.at[i])
        for at in range(b, b + count):
            total = own[at]
            for side in range(2):
                total += precv[side, at].astype(f32)
            if b >= straight:
                total += pdiag[at].astype(f32)
            out_ref = (bk_ref, bv_ref)[at // heads]
            for r in range(requests):
                live = (slot_row + 1) * ratio_ref[r, s] <= interval
                out_ref[at % heads, r * nb : (r + 1) * nb] = jnp.where(
                    live, total[r * nb : (r + 1) * nb], 0.0
                ).astype(bf16)

    def times(zi, to, b, count):
        return jnp.dot(
            act[zi, :, to].reshape(requests * nb, act.shape[4]),
            jnp.concatenate([wbuf[zi, at] for at in range(b, b + count)], axis=1),
            preferred_element_type=f32,
        )

    ahead = units[key_units + 1][0]

    def near_products():
        near = jnp.where(z == 0, 0, 1)
        for i in range(key_units + 1, len(units)):
            w_wait(i, 0, depth - 2)
        for b in range(ahead, blocks, 2):

            def step(to, carry, b=b):
                total = times(near, to, b, 2)
                for zi in range(1, depth - 1):
                    total += times(near + zi, to, b, 2)
                for at in range(2):
                    acc[to, b - ahead + at] = total[:, at * hd : (at + 1) * hd]
                return carry

            with region("near"):
                lax.fori_loop(0, B, step, 0)

    def product(i, late):
        b, count = units[i]

        def step(o, carry):
            to = jnp.where(o == 0, across, jnp.where(o == 1, x_side, jnp.where(o == 2, y_side, me)))
            if late:
                total = jnp.concatenate([acc[to, b - ahead + at] for at in range(count)], axis=1)
                total += times(far, to, b, count)
            else:
                total = times(0, to, b, count)
                for zi in range(1, depth):
                    total += times(zi, to, b, count)

            def part_of(at):
                return total[:, (at - b) * hd : (at - b + 1) * hd]

            @pl.when(o == 0)
            def _():
                for at in range(b, b + count):
                    psend[0, at] = part_of(at).astype(bf16)
                    p_copy(0, at).start()

            for side in range(2):

                @pl.when(o == 1 + side)
                def _(side=side):
                    for at in range(b, b + count):
                        if at >= straight:
                            psend[1 + side, at] = part_of(at).astype(bf16)
                            p_copy(1 + side, at).start()
                        elif at % 2 == side:
                            psend[1, at] = part_of(at).astype(bf16)
                            p_copy(1, at).start()
                        else:
                            hold[at] = part_of(at)

            @pl.when(o == B - 1)
            def _():
                for at in range(b, b + count):
                    own[at] = part_of(at)

            return carry

        with region(f"prod{i}"):
            lax.fori_loop(0, B, step, 0)

    def forward(i):
        b, count = units[i]
        if b >= straight:
            return
        with region(f"forward{i}"):
            got(pdiag.at[b : b + count], g_recv.at[i])
            for at in range(b, b + count):
                psend[2, at] = (hold[at] + pdiag[at].astype(f32)).astype(bf16)
                p_copy(2, at).start()

    res = rk_ref.shape[2]
    qrows = dq_ref.shape[1]
    mergers = snd.shape[0]
    share = G * heads // mergers
    slots = hd // (2 * share)
    per_head = G // share
    first_merger = (depth // 2) * B - mergers // 2
    mine = s - first_merger
    merges = (mine >= 0) & (mine < mergers)

    def e_copy(to):
        return remote(snd_stats.at[to], rcv_stats.at[s], e_send, e_recv, first_merger + to)

    def d_copy(to):
        return remote(snd.at[to], rcv.at[s], d_send, d_recv, first_merger + to)

    def to_mergers(copy, first, end):
        for to in range(first, end):

            @pl.when(mine != to)
            def _(to=to):
                copy(to).start()

    def scored(k, r, key, mask):
        scores = lax.dot_general(
            dq_ref[k], key, (((1,), (1,)), ((), ())), preferred_element_type=f32
        )
        return jnp.where(mask, scores * inv_root, masked_score)

    def row_of(count):
        return (
            lax.rem(lax.broadcasted_iota(jnp.int32, (qrows, count), 0), requests),
            lax.broadcasted_iota(jnp.int32, (qrows, count), 1),
        )

    def decode_early():
        row_request, cell = row_of(res)
        row_rim, rim = row_of(OFF)
        last = jnp.where(s == n - 1, 1, 0)
        for k in range(heads):
            pieces = []
            for r in range(requests):
                usable = (cell < rlen_ref[r, s]) & (row_request == r)
                pieces.append((scored(k, r, rk_ref[r, k], usable), rv_ref, r, slice(0, res)))
                usable = (rim >= OFF - phase_ref[r] * last) & (row_rim == r)
                left = slice(rows - OFF, rows)
                pieces.append((scored(k, r, kbuf[r, k, left], usable), vbuf, r, left))
            peak = jnp.max(pieces[0][0], axis=-1, keepdims=True)
            for piece in pieces[1:]:
                peak = jnp.maximum(peak, jnp.max(piece[0], axis=-1, keepdims=True))
            total = jnp.zeros((qrows, 1), f32)
            out = jnp.zeros((qrows, hd), f32)
            for scores, source, r, span in pieces:
                weights = jnp.exp(scores - peak)
                total += jnp.sum(weights, axis=-1, keepdims=True)
                out += jnp.dot(weights.astype(bf16), source[r, k, span], preferred_element_type=f32)
            dacc[k] = out
            dstat[k, 0] = jnp.broadcast_to(peak, (qrows, hd))
            dstat[k, 1] = jnp.broadcast_to(total, (qrows, hd))

    def decode_weights():
        row_request, slot = row_of(nb)
        for k in range(heads):
            pieces = []
            for r in range(requests):
                usable = ((slot + 1) * ratio_ref[r, s] <= interval) & (row_request == r)
                pieces.append(scored(k, r, bk_ref[k, r * nb : (r + 1) * nb], usable))
            former = dstat[k, 0]
            peak = former
            for piece in pieces:
                peak = jnp.maximum(peak, jnp.max(piece, axis=-1, keepdims=True))
            scale = jnp.exp(former - peak)
            total = dstat[k, 1] * scale
            for r in range(requests):
                weights = jnp.exp(pieces[r] - peak)
                total += jnp.sum(weights, axis=-1, keepdims=True)
                dlow[k, r] = weights.astype(bf16)
            dacc[k] = dacc[k] * scale
            lane = lax.broadcasted_iota(jnp.int32, (qrows, hd), 1)
            stats = jnp.where(lax.rem(lane // slots, 2) == 0, peak, total)
            stats = stats.reshape(per_head, share, pair, hd)
            lane = lax.broadcasted_iota(jnp.int32, (per_head, pair, hd), 2)
            packed = stats[:, 0]
            for j in range(1, share):
                packed = jnp.where(lane >= 2 * slots * j, stats[:, j], packed)
            snd_stats[k * per_head : (k + 1) * per_head] = packed
        to_mergers(e_copy, 0, mergers)

    def decode_values(k):
        out = dacc[k]
        for r in range(requests):
            out += jnp.dot(
                dlow[k, r], bv_ref[k, r * nb : (r + 1) * nb], preferred_element_type=f32
            )
        snd[k * per_head : (k + 1) * per_head] = out.reshape(per_head, share * pair, hd).astype(bf16)
        to_mergers(d_copy, k * per_head, (k + 1) * per_head)

    outs = []

    def emit(made, made_rows, out):
        made_rows[...] = jnp.swapaxes(made[...], 0, 1)
        outs.append(pltpu.make_async_copy(made_rows, out, out_sem.at[len(outs)]))
        outs[-1].start()

    for i in range(len(units)):

        @pl.when(ends)
        def _(i=i):
            late = i > key_units
            if i == key_units + 1:
                near_products()
            with region(f"wwait{i}"):
                w_wait(i, depth - 2 if late else 0, depth - 1)
            product(i, late)
            if i <= key_units:
                forward(i)
            elif i > key_units + 1:
                forward(i - 1)

        @pl.when(jnp.logical_not(ends))
        def _(i=i):
            if i == key_units:
                w_relay(2, 3)
                w_relay(2, 4)
            product(i, False)
            if i > 0:
                forward(i - 1)

        if i == 1:
            with region("early"):
                decode_early()
    forward(len(units) - 1)
    for i in range(key_units):
        finish(i)
    with region("decode"):
        decode_weights()
    for i in range(key_units, len(units)):
        finish(i)
        b, count = units[i]
        with region("values"):
            for at in range(b, b + count):
                decode_values(at - heads)

    emit(bk_ref, bk_rows, bk_out)
    emit(bv_ref, bv_rows, bv_out)

    with region("drain"):
        sent(psend, s_send)
        sent(act.at[:2], p_send)
        sent(stage.at[: requests * heads * (B - 1) // B], a_send)
        for way in range(2):
            for d in range(depth - 1):
                shard, target, there = w_out(way, d)

                @pl.when(there)
                def _(way=way, d=d, shard=shard):
                    sent(wbuf.at[shard], w_send.at[way, d])

        @pl.when((me < B - 1) | crosses)
        def _():
            sent(rimraw, rim_send)

        @pl.when(relays)
        def _():
            sent(rimrel, rel_send)

    early = mergers - mergers // heads
    late = jnp.where(mine >= early, 1, 0)

    def t_copy(to):
        return remote(att.at[mine], att.at[mine], t_send, t_recv.at[late], to)

    with region("merge"):

        @pl.when(merges)
        def _():
            rcv[s] = snd[mine]
            rcv_stats[s] = snd_stats[mine]
            got(rcv_stats.at[: n - 1], e_recv)
            shares = []
            for j in range(share):
                at = 2 * slots * j
                peaks = rcv_stats[:, :, at : at + 1]
                scale = jnp.exp(peaks - jnp.max(peaks, axis=0, keepdims=True))
                total = jnp.sum(scale * rcv_stats[:, :, at + slots : at + slots + 1], axis=0)
                shares.append((scale, total))
            got(rcv.at[: n - 1], d_recv)
            landed = rcv[...].astype(f32)
            attended = []
            for j, (scale, total) in enumerate(shares):
                mixed = jnp.sum(scale * landed[:, j * pair : (j + 1) * pair], axis=0)
                attended.append(mixed / total)
            att[mine] = jnp.concatenate(attended, axis=0).astype(bf16)
            for to in range(n):

                @pl.when(to != s)
                def _(to=to):
                    t_copy(to).start()

            sent(snd.at[: mergers - 1], d_send)
            sent(snd_stats.at[: mergers - 1], e_send)

        @pl.when(jnp.logical_not(merges))
        def _():
            sent(snd, d_send)
            sent(snd_stats, e_send)

    ow_load.wait()

    def attended_rows(first, end, group):
        @pl.when(merges & (late == group))
        def _():
            got(att.at[first : end - 1], t_recv.at[group])

        @pl.when(jnp.logical_not(merges & (late == group)))
        def _():
            got(att.at[first:end], t_recv.at[group])

        wide = [att[i].astype(f32) for i in range(first, end)]
        vectors = jnp.concatenate(
            [piece[j * pair : (j + 1) * pair] for piece in wide for j in range(share)], axis=1
        ).astype(bf16)
        span = share * hd
        return jnp.dot(vectors, owbuf[first * span : end * span], preferred_element_type=f32)

    with region("twait"):
        sums = attended_rows(0, early, 0)
    with region("twait2"):
        sums += attended_rows(early, mergers, 1)
    part[...] = sums
    swap = remote(part, part_out.at[h], h_send, h_recv)
    swap.start()
    outs.append(pltpu.make_async_copy(part, part_out.at[h], out_sem.at[len(outs)]))
    outs[-1].start()
    with region("swap"):

        @pl.when(merges)
        def _():
            sent(rcv.at[: n - 1], t_send)

        swap.wait()
        for copy in outs:
            copy.wait()


def handed_on(keys_ref, values_ref, part_ref, keys_out, values_out, projected_out):
    keys_out[...] = keys_ref[...]
    values_out[...] = values_ref[...]
    summed = (part_ref[0] + part_ref[1]).astype(projected_out.dtype)
    steps, requests, _ = projected_out.shape
    for t in range(steps):
        projected_out[t] = summed[t * requests : (t + 1) * requests]


def fused_body(
    shard_count,
    raw_keys,
    raw_values,
    phase,
    ratio,
    resident_len,
    beacon_queries,
    beacon_wk,
    beacon_wv,
    resident_keys,
    resident_values,
    decode_queries,
    out_weight,
):
    n = shard_count
    depth = n // B
    requests, interval, heads, hd = raw_keys.shape
    steps = decode_queries.shape[0]
    nb = beacon_queries.shape[1]
    rows = interval + OFF
    res = resident_keys.shape[1]
    feature, columns = beacon_wk.shape
    blocks = 2 * columns // hd
    units = blocks // 2 + 1
    pair = requests * steps
    mergers = min(2 * B, n)
    share = G * heads // mergers
    bf16, f32 = jnp.bfloat16, jnp.float32
    dma = pltpu.SemaphoreType.DMA
    smem = pl.BlockSpec(memory_space=pltpu.SMEM)
    anywhere = pl.BlockSpec(memory_space=pl.ANY)
    vmem = pl.BlockSpec(memory_space=pltpu.VMEM)
    keys, values, partial_sums = pl.pallas_call(
        functools.partial(fused_kernel, n),
        out_shape=(
            jax.ShapeDtypeStruct((requests * nb, heads, hd), bf16),
            jax.ShapeDtypeStruct((requests * nb, heads, hd), bf16),
            jax.ShapeDtypeStruct((2, pair, out_weight.shape[1]), f32),
        ),
        in_specs=[smem] * 3 + [anywhere] * 9,
        out_specs=(anywhere, anywhere, anywhere),
        scratch_shapes=[
            pltpu.VMEM(raw_keys.shape, bf16),
            pltpu.VMEM(raw_values.shape, bf16),
            pltpu.VMEM(beacon_queries.shape, bf16),
            pltpu.VMEM(resident_keys.shape, bf16),
            pltpu.VMEM(resident_values.shape, bf16),
            pltpu.VMEM(decode_queries.shape, bf16),
            pltpu.VMEM((2 * requests, OFF, heads, hd), bf16),
            pltpu.VMEM((OFF, heads, hd), bf16),
            pltpu.VMEM((requests, heads, rows, hd), bf16),
            pltpu.VMEM((requests, heads, rows, hd), bf16),
            pltpu.VMEM((G, nb, hd + nb), bf16),
            pltpu.VMEM((depth, blocks, feature, hd), bf16),
            pltpu.VMEM((depth, requests, B, nb, feature), bf16),
            pltpu.VMEM((requests * heads, 2, nb, feature), bf16),
            pltpu.VMEM((3, blocks, requests * nb, hd), bf16),
            pltpu.VMEM((2, blocks, requests * nb, hd), bf16),
            pltpu.VMEM((blocks, requests * nb, hd), bf16),
            pltpu.VMEM((blocks, requests * nb, hd), f32),
            pltpu.VMEM((blocks, requests * nb, hd), f32),
            pltpu.VMEM((B, blocks // 2, requests * nb, hd), f32),
            pltpu.VMEM((requests, rows, nb), bf16),
            pltpu.VMEM(out_weight.shape, bf16),
            pltpu.VMEM((requests, heads, res, hd), bf16),
            pltpu.VMEM((requests, heads, res, hd), bf16),
            pltpu.VMEM((heads, G * pair, hd), bf16),
            pltpu.VMEM((heads, requests * nb, hd), bf16),
            pltpu.VMEM((heads, requests * nb, hd), bf16),
            pltpu.VMEM((heads, G * pair, hd), f32),
            pltpu.VMEM((heads, 2, G * pair, hd), f32),
            pltpu.VMEM((heads, requests, G * pair, nb), bf16),
            pltpu.VMEM((mergers, share * pair, hd), bf16),
            pltpu.VMEM((mergers, pair, hd), f32),
            pltpu.VMEM((n, share * pair, hd), bf16),
            pltpu.VMEM((n, pair, hd), f32),
            pltpu.VMEM((mergers, share * pair, hd), bf16),
            pltpu.VMEM((pair, out_weight.shape[1]), f32),
            pltpu.VMEM((requests * nb, heads, hd), bf16),
            pltpu.VMEM((requests * nb, heads, hd), bf16),
            dma((2 * requests + 5,)),
            dma((units,)),
            dma((3,)),
            dma,
            dma((requests,)),
            dma,
            dma,
            dma((2, depth - 1)),
            dma((2, depth - 1, units)),
            dma,
            dma((2, requests)),
            dma((2, requests)),
            dma,
            dma,
            dma,
            dma((units,)),
            dma((units,)),
            dma,
            dma,
            dma,
            dma,
            dma,
            dma((2,)),
            dma,
            dma,
        ],
        compiler_params=pltpu.CompilerParams(
            collective_id=0, has_side_effects=True, vmem_limit_bytes=60 * 1024 * 1024
        ),
    )(
        phase,
        ratio,
        resident_len,
        raw_keys,
        raw_values,
        beacon_queries,
        beacon_wk,
        beacon_wv,
        resident_keys,
        resident_values,
        decode_queries,
        out_weight,
    )
    keys, values, projected = pl.pallas_call(
        handed_on,
        out_shape=(
            jax.ShapeDtypeStruct(keys.shape, bf16),
            jax.ShapeDtypeStruct(values.shape, bf16),
            jax.ShapeDtypeStruct((steps, requests, out_weight.shape[1]), bf16),
        ),
        in_specs=[vmem] * 3,
        out_specs=(vmem,) * 3,
    )(keys, values, partial_sums)
    return (
        keys.reshape(requests, nb, heads, hd),
        values.reshape(requests, nb, heads, hd),
        projected,
    )


def chosen_body(shard_count, head_count):
    def run(*arrays):
        requests, _, heads, hd = arrays[0].shape
        feature = arrays[6].shape[0]
        fits = (
            head_count == 2
            and shard_count == B * B
            and requests == 2
            and heads == B
            and 2 * feature == G * hd
        )
        return fused_body(shard_count, *arrays) if fits else body(*arrays)

    return run


def solution(mesh):
    return jax.shard_map(
        chosen_body(mesh.shape["seq"], mesh.shape["head"]),
        mesh=mesh,
        in_specs=(
            P(None, "seq", "head", None),
            P(None, "seq", "head", None),
            P(),
            P(),
            P(),
            P(None, "seq", "head", None, None),
            P("seq", "head"),
            P("seq", "head"),
            P(None, "seq", "head", None),
            P(None, "seq", "head", None),
            P(None, None, "head", None, None),
            P("head", "seq"),
        ),
        out_specs=(
            P(None, "seq", "head", None),
            P(None, "seq", "head", None),
            P(None, None, "seq"),
        ),
        check_vma=False,
    )
```

```python
import contextlib
import functools
import math

import jax
import jax.numpy as jnp
from jax import lax
from jax.experimental import pallas as pl
from jax.experimental.pallas import tpu as pltpu
from jax.sharding import PartitionSpec as P

G = 8
INTERVAL = 1024
NB = 128
OFF = 256
STEPS = 4


masked_score = -1e30


def region(name):
    return contextlib.nullcontext()


def shifted(value, axis, steps):
    count = lax.axis_size(axis)
    first, last = (max(0, -steps), min(count, count - steps))
    return lax.ppermute(value, axis, [(source, source + steps) for source in range(first, last)])


def joined(shard, axis, combine):
    everything = jax.tree.map(lambda part: lax.all_gather(part, axis), shard)
    first = jax.tree.map(lambda part: part[0], everything)

    def hop(k, so_far):
        return combine(so_far, jax.tree.map(lambda part: part[k], everything))

    return lax.fori_loop(1, lax.axis_size(axis), hop, first)


def blend(former, latter):
    row_peak = jnp.maximum(former[0], latter[0])
    former_scale = jnp.exp(former[0] - row_peak)
    latter_scale = jnp.exp(latter[0] - row_peak)
    weight_sum = former[1] * former_scale + latter[1] * latter_scale
    weighted = former[2] * former_scale[..., None] + latter[2] * latter_scale[..., None]
    return (row_peak, weight_sum, weighted)


def pool_part(queries, key_rows, value_rows, positions, present, reaches):
    inv_root = 1.0 / math.sqrt(queries.shape[-1])

    def per_request(members):
        query_block, key_block, value_block, position_row, present_row, reach_row = members
        scores = (
            jnp.einsum("jkgd,ikd->jkgi", query_block, key_block, preferred_element_type=jnp.float32)
            * inv_root
        )
        allowed = (
            present_row[None, :]
            & (position_row[None, :] >= 0)
            & (position_row[None, :] < INTERVAL)
            & (position_row[None, :] < reach_row[:, None])
        )
        cache_mask = allowed[:, None, None, :]
        row_peak = jnp.max(jnp.where(cache_mask, scores, masked_score), axis=-1)
        weights = jnp.where(cache_mask, jnp.exp(scores - row_peak[..., None]), 0.0)
        weight_sum = jnp.sum(weights, axis=-1)
        weighted = jnp.einsum(
            "jkgi,ikd->jkgd",
            weights.astype(jnp.bfloat16),
            value_block,
            preferred_element_type=jnp.float32,
        )
        return (row_peak, weight_sum, weighted)

    return lax.map(per_request, (queries, key_rows, value_rows, positions, present, reaches))


def body(
    raw_keys,
    raw_values,
    phase,
    ratio,
    resident_len,
    beacon_queries,
    beacon_wk,
    beacon_wv,
    resident_keys,
    resident_values,
    decode_queries,
    out_weight,
):
    requests = raw_keys.shape[0]
    kv_local = raw_keys.shape[2]
    head_dim = raw_keys.shape[3]
    shard_index = lax.axis_index("seq")
    shard_count = lax.axis_size("seq")
    is_first = shard_index == 0
    is_last = shard_index == shard_count - 1
    own_ratio = lax.dynamic_index_in_dim(ratio, shard_index, 1, keepdims=False)
    slot_ids = jnp.arange(NB, dtype=jnp.int32)
    lead_in = jnp.where(is_first, phase, 0)
    reaches = (slot_ids[None, :] + 1) * own_ratio[:, None] + lead_in[:, None]
    tail_keys = raw_keys[:, INTERVAL - OFF :]
    tail_values = raw_values[:, INTERVAL - OFF :]
    own_positions = jnp.arange(INTERVAL, dtype=jnp.int32)[None, :] + phase[:, None]
    rim_ids = jnp.arange(OFF, dtype=jnp.int32)
    rim_positions = rim_ids[None, :] - OFF + phase[:, None]
    near_keys, near_values = shifted((tail_keys, tail_values), "seq", 1)
    key_rows = jnp.concatenate([near_keys, raw_keys], axis=1)
    value_rows = jnp.concatenate([near_values, raw_values], axis=1)
    positions = jnp.concatenate([rim_positions, own_positions], axis=1)
    present = jnp.logical_not(is_first) | (positions >= phase[:, None])
    pooled_parts = pool_part(beacon_queries, key_rows, value_rows, positions, present, reaches)
    pooled = (pooled_parts[2] / pooled_parts[1][..., None]).astype(jnp.bfloat16)
    pooled_flat = pooled.reshape(requests * NB, kv_local * G * head_dim)
    pooled_whole = lax.all_gather(pooled_flat, "head", axis=1, tiled=True)
    key_sum = jnp.dot(
        pooled_whole,
        lax.all_gather(beacon_wk, "seq", axis=0, tiled=True),
        preferred_element_type=jnp.float32,
    )
    value_sum = jnp.dot(
        pooled_whole,
        lax.all_gather(beacon_wv, "seq", axis=0, tiled=True),
        preferred_element_type=jnp.float32,
    )
    made_keys = key_sum
    made_values = value_sum
    made_keys = made_keys.reshape(requests, NB, kv_local, head_dim)
    made_values = made_values.reshape(requests, NB, kv_local, head_dim)
    slot_live = slot_ids[None, :] < (INTERVAL // own_ratio)[:, None]
    beacon_keys = jnp.where(slot_live[:, :, None, None], made_keys, 0.0).astype(jnp.bfloat16)
    beacon_values = jnp.where(slot_live[:, :, None, None], made_values, 0.0).astype(jnp.bfloat16)
    cache_keys = jnp.concatenate([resident_keys, beacon_keys, tail_keys], axis=1)
    cache_values = jnp.concatenate([resident_values, beacon_values, tail_values], axis=1)
    own_len = lax.dynamic_index_in_dim(resident_len, shard_index, 1, keepdims=False)
    resident_ok = jnp.arange(resident_keys.shape[1], dtype=jnp.int32)[None, :] < own_len[:, None]
    leftover_ok = (rim_ids[None, :] >= OFF - phase[:, None]) & is_last
    usable = jnp.concatenate([resident_ok, slot_live, leftover_ok], axis=1)
    inv_root = 1.0 / math.sqrt(head_dim)
    scores = (
        jnp.einsum(
            "srkgd,rikd->rksgi", decode_queries, cache_keys, preferred_element_type=jnp.float32
        )
        * inv_root
    )
    cache_mask = usable[:, None, None, None, :]
    row_peak = jnp.max(jnp.where(cache_mask, scores, masked_score), axis=-1)
    weights = jnp.where(cache_mask, jnp.exp(scores - row_peak[..., None]), 0.0)
    weight_sum = jnp.sum(weights, axis=-1)
    weighted = jnp.einsum(
        "rksgi,rikd->rksgd",
        weights.astype(jnp.bfloat16),
        cache_values,
        preferred_element_type=jnp.float32,
    )
    merged = joined((row_peak, weight_sum, weighted), "seq", blend)
    total_sum = merged[1]
    total_weighted = merged[2]
    attended = (total_weighted / total_sum[..., None]).astype(jnp.bfloat16)
    attended = jnp.transpose(attended, (2, 0, 1, 3, 4)).reshape(
        STEPS * requests, kv_local * G * head_dim
    )
    partial_value = jnp.dot(attended, out_weight, preferred_element_type=jnp.float32)
    summed = lax.psum(partial_value, "head")
    projected = summed.astype(jnp.bfloat16).reshape(STEPS, requests, out_weight.shape[1])
    return (beacon_keys, beacon_values, projected)


B = 4
GB = 2
STRAIGHT = 2


def fused_kernel(
    shard_count,
    phase_ref,
    ratio_ref,
    rlen_ref,
    k_hbm,
    v_hbm,
    q_hbm,
    wk_hbm,
    wv_hbm,
    rk_hbm,
    rv_hbm,
    dq_hbm,
    ow_hbm,
    bk_out,
    bv_out,
    part_out,
    kraw,
    vraw,
    qraw,
    rkraw,
    rvraw,
    dqraw,
    rimraw,
    rimrel,
    kbuf,
    vbuf,
    qbuf,
    wbuf,
    act,
    stage,
    psend,
    precv,
    pdiag,
    hold,
    own,
    acc,
    bias,
    owbuf,
    rk_ref,
    rv_ref,
    dq_ref,
    bk_ref,
    bv_ref,
    dacc,
    dstat,
    dlow,
    snd,
    snd_stats,
    rcv,
    rcv_stats,
    att,
    part,
    bk_rows,
    bv_rows,
    load_sem,
    w_load,
    out_sem,
    rim_send,
    rim_recv,
    rel_send,
    rel_recv,
    w_send,
    w_recv,
    a_send,
    a_recv,
    a_loc,
    p_send,
    p_recv,
    s_send,
    s_recv,
    g_recv,
    d_send,
    d_recv,
    e_send,
    e_recv,
    t_send,
    t_recv,
    h_send,
    h_recv,
):
    n = shard_count
    depth = n // B
    s = lax.axis_index("seq")
    h = lax.axis_index("head")
    z = s // B
    me = lax.rem(s, B)
    requests, interval, heads, hd = kraw.shape
    rows = interval + OFF
    nb = psend.shape[2] // requests
    blocks = wbuf.shape[1]
    units = [(b, 2) for b in range(0, blocks - 2, 2)] + [(blocks - 2, 1), (blocks - 1, 1)]
    inv_root = 1.0 / math.sqrt(hd)
    to_log2 = inv_root / math.log(2.0)
    f32 = jnp.float32
    bf16 = jnp.bfloat16

    def remote(src, dst, send, recv, seq=None):
        target = {"head": 1 - h} if seq is None else {"seq": seq}
        return pltpu.make_async_remote_copy(
            src_ref=src,
            dst_ref=dst,
            send_sem=send,
            recv_sem=recv,
            device_id=target,
            device_id_type=pl.DeviceIdType.MESH,
        )

    def got(ref, sem):
        remote(ref, ref, sem, sem, s).wait_recv()

    def sent(ref, sem):
        remote(ref, ref, sem, sem, s).wait_send()

    barrier = pltpu.get_barrier_semaphore()
    for o in range(1, n):
        pl.semaphore_signal(
            barrier,
            inc=1,
            device_id={"seq": lax.rem(s + o, n)},
            device_id_type=pl.DeviceIdType.MESH,
        )
    pl.semaphore_signal(
        barrier, inc=1, device_id={"head": 1 - h}, device_id_type=pl.DeviceIdType.MESH
    )

    loads = []

    def load(source, target):
        loads.append(pltpu.make_async_copy(source, target, load_sem.at[len(loads)]))
        loads[-1].start()
        return loads[-1]

    for i, (b, count) in enumerate(units):
        for at in range(b, b + count):
            source = (wk_hbm, wv_hbm)[at // heads].at[:, (at % heads) * hd : (at % heads + 1) * hd]
            pltpu.make_async_copy(source, wbuf.at[z, at], w_load.at[i]).start()
    kv_load = [
        load((k_hbm, v_hbm)[p % 2].at[p // 2], (kraw, vraw)[p % 2].at[p // 2])
        for p in range(2 * requests)
    ]
    q_load = load(q_hbm, qraw)
    rest_load = [load(rk_hbm, rkraw), load(rv_hbm, rvraw), load(dq_hbm, dqraw)]
    ow_load = load(ow_hbm, owbuf)

    with region("barrier"):
        pl.semaphore_wait(barrier, n)

    crosses = (me == B - 1) & (z < depth - 1)
    relays = (me < B - 1) & (z < depth - 1)

    def rim_near(p):
        source = (k_hbm, v_hbm)[p % 2].at[p // 2, interval - OFF :]
        return remote(source, rimraw.at[p], rim_send, rim_recv.at[p // 2], lax.rem(s + 1, n))

    def rim_far(p):
        source = (k_hbm, v_hbm)[p % 2].at[p // 2, interval - OFF :]
        return remote(source, rimrel, rim_send, rel_recv, z * B + lax.rem(p, B - 1))

    def rim_pass():
        p = jnp.where(me == 0, B - 1, me)
        return remote(rimrel, rimraw.at[p], rel_send, rim_recv.at[p // 2], lax.rem((z + 1) * B, n))

    @pl.when(me < B - 1)
    def _():
        for p in range(2 * requests):
            rim_near(p).start()

    @pl.when(crosses)
    def _():
        rim_near(0).start()
        rim_far(1).start()

    def w_copy(way, d, i, shard, target):
        b, count = units[i]
        return remote(
            wbuf.at[shard, b : b + count],
            wbuf.at[shard, b : b + count],
            w_send.at[way, d],
            w_recv.at[way, d, i],
            target * B + me,
        )

    def w_out(way, d):
        if way == 0:
            return z - d, z + 1, (z - d >= 0) & (z + 1 < depth)
        return z + d, z - 1, (z + d < depth) & (z - 1 >= 0)

    def w_in(way, d):
        if way == 0:
            return z - 1 - d, z - 1 - d >= 0
        return z + 1 + d, z + 1 + d < depth

    def w_own(first, end):
        for i in range(first, end):
            b, count = units[i]
            pltpu.make_async_copy(
                wbuf.at[z, b : b + count], wbuf.at[z, b : b + count], w_load.at[i]
            ).wait()
            for way in range(2):
                shard, target, there = w_out(way, 0)

                @pl.when(there)
                def _(way=way, i=i, shard=shard, target=target):
                    w_copy(way, 0, i, shard, target).start()

    def w_relay(d, i):
        for way in range(2):
            shard, target, onward = w_out(way, d)

            @pl.when(onward)
            def _(way=way, shard=shard, target=target):
                w_copy(way, d - 1, i, shard, z).wait_recv()
                w_copy(way, d, i, shard, target).start()

    ends = (z == 0) | (z == depth - 1)
    far = depth - 1 - z

    def w_wait(i, first, end):
        for way in range(2):
            for d in range(first, end):
                shard, there = w_in(way, d)
                there = there & ((z == depth - 1) if way == 0 else (z == 0))

                @pl.when(there)
                def _(way=way, d=d, shard=shard):
                    w_copy(way, d, i, shard, z).wait_recv()

    def rim_relay():
        with region("rimpass"):
            got(rimrel, rel_recv)
            rim_pass().start()

    w_own(0, 1)

    @pl.when(me != 1)
    def _():
        w_own(1, len(units))

    with region("prep"):
        for r in range(requests):
            slot = lax.broadcasted_iota(jnp.int32, (rows, nb), 1)
            position = lax.broadcasted_iota(jnp.int32, (rows, nb), 0) - OFF + phase_ref[r]
            lead = jnp.where(s == 0, phase_ref[r], 0)
            reach = (slot + 1) * ratio_ref[r, s] + lead
            allowed = (position >= lead) & (position < interval) & (position < reach)
            bias[r] = jnp.where(allowed, 0.0, masked_score).astype(bf16)
        for p in range(2 * requests):
            kv_load[p].wait()
            (kbuf, vbuf)[p % 2][p // 2, :, OFF:] = jnp.swapaxes((kraw, vraw)[p % 2][p // 2], 0, 1)
        chosen = lax.broadcasted_iota(jnp.int32, (nb, nb), 0) == lax.broadcasted_iota(
            jnp.int32, (nb, nb), 1
        )
        for g in range(G):
            qbuf[g, :, hd:] = jnp.where(chosen, 1.0, 0.0).astype(bf16)
        for copy in rest_load:
            copy.wait()
        for r in range(requests):
            rk_ref[r] = jnp.swapaxes(rkraw[r], 0, 1)
            rv_ref[r] = jnp.swapaxes(rvraw[r], 0, 1)
        steps = dqraw.shape[0]
        pair = steps * requests
        for k in range(heads):
            asked = jnp.stack(
                [dqraw[t, r, k].astype(f32) for t in range(steps) for r in range(requests)], axis=0
            )
            dq_ref[k] = jnp.swapaxes(asked, 0, 1).reshape(G * pair, hd).astype(bf16)
        q_load.wait()

    @pl.when(relays & (me == 1))
    def _():
        rim_relay()

    @pl.when(crosses)
    def _():
        for p in range(2, 2 * requests):
            rim_far(p).start()

    @pl.when(me == 1)
    def _():
        w_own(1, len(units))

    @pl.when(s == 0)
    def _():
        kbuf[:, :, :OFF] = jnp.zeros((requests, heads, OFF, hd), kbuf.dtype)
        vbuf[:, :, :OFF] = jnp.zeros((requests, heads, OFF, hd), vbuf.dtype)

    def a_remote(v, x):
        kk, r, y = v // 4, lax.rem(v, 2), lax.rem(v // 2, 2)
        return remote(
            stage.at[v, x],
            act.at[h * 2 + kk, r, me],
            a_send,
            a_recv.at[kk, r],
            z * B + y * 2 + x,
        )

    def a_local(kk, r, v):
        return pltpu.make_async_copy(
            stage.at[v, lax.rem(me, 2)], act.at[h * 2 + kk, r, me], a_loc.at[kk, r]
        )

    def a_relay(kk, r):
        return remote(
            act.at[h * 2 + kk, r], act.at[h * 2 + kk, r], p_send, p_recv
        )

    def a_gather(kk, r):
        a_local(kk, r, kk * 4 + (me // 2) * 2 + r).wait()
        got(act.at[0, 0, : B - 1], a_recv.at[kk, r])
        a_relay(kk, r).start()

    def unit(u, carry):
        r, k = u // heads, lax.rem(u, heads)
        v = k * 2 + r

        @pl.when((k == 0) & (s > 0))
        def _():
            with region("rimwait"):
                got(rimraw.at[:2], rim_recv.at[r])
            kbuf[r, :, :OFF] = jnp.swapaxes(rimraw[r * 2], 0, 1)
            vbuf[r, :, :OFF] = jnp.swapaxes(rimraw[r * 2 + 1], 0, 1)

        with region("att"):
            qbuf[:, :, :hd] = jnp.swapaxes(qraw[r, :, k], 0, 1)
            ones = jnp.ones((rows, hd), bf16)
            for first in range(0, G, GB):
                scores = lax.dot_general(
                    qbuf[first : first + GB].reshape(GB * nb, hd + nb),
                    jnp.concatenate([kbuf[r, k], bias[r]], axis=1),
                    (((1,), (1,)), ((), ())),
                    preferred_element_type=f32,
                )
                peak = jnp.max(scores, axis=-1, keepdims=True)
                weights = jnp.exp2((scores - peak) * to_log2).astype(bf16)
                out = jnp.dot(
                    weights,
                    jnp.concatenate([vbuf[r, k], ones], axis=1),
                    preferred_element_type=f32,
                )
                out = (out[:, :hd] / out[:, hd:]).astype(bf16)
                for g in range(first, first + GB):
                    at = (g % 4) * hd
                    stage[v, g // 4, :, at : at + hd] = out[(g - first) * nb : (g - first + 1) * nb]
        for x in range(2):
            member = lax.rem(k, 2) * 2 + x

            @pl.when(member == me)
            def _():
                a_local(k // 2, r, v).start()

            @pl.when(member != me)
            def _(x=x):
                a_remote(v, x).start()

        with region("relay"):

            @pl.when((u == jnp.where(me == 0, 1, 0)) & (me != 1) & relays)
            def _():
                rim_relay()

            for i in range(3):

                @pl.when(u == heads - 2 + i)
                def _(i=i):
                    w_relay(1, i)

            @pl.when(u == heads + 2)
            def _():
                w_relay(2, 0)

            @pl.when(u == heads + 1)
            def _():
                a_gather(0, 0)

            @pl.when(u == heads + 3)
            def _():
                a_gather(1, 0)

        return carry

    lax.fori_loop(0, 2 * heads, unit, 0)
    with region("gather"):
        w_relay(2, 1)
        a_gather(0, 1)
        a_gather(1, 1)
        w_relay(2, 2)
        w_relay(1, 3)
        w_relay(1, 4)
        got(act.at[:2], p_recv)

    x_side = me + 1 - 2 * lax.rem(me, 2)
    y_side = lax.rem(me + 2, B)
    across = B - 1 - me
    straight = blocks - STRAIGHT

    def p_copy(lane, at):
        if at >= straight:
            i = min(at // 2, len(units) - 2) + (at == blocks - 1)
            return remote(
                psend.at[lane, at],
                pdiag.at[at] if lane == 0 else precv.at[lane - 1, at],
                s_send,
                (g_recv if lane == 0 else s_recv).at[i],
                z * B + (across, x_side, y_side)[lane],
            )
        if lane == 0:
            side, target = at % 2, pdiag.at[at]
        else:
            side = at % 2 if lane == 1 else 1 - at % 2
            target = precv.at[side, at]
        i = min(at // 2, len(units) - 2) + (at == blocks - 1)
        return remote(
            psend.at[lane, at],
            target,
            s_send,
            (g_recv if lane == 0 else s_recv).at[i],
            z * B + (x_side, y_side)[side],
        )

    key_units = heads // 2
    slot_row = lax.broadcasted_iota(jnp.int32, (nb, hd), 0)

    def finish(i):
        b, count = units[i]
        with region(f"finish{i}"):
            got(precv.at[:, b : b + count], s_recv.at[i])
            if b >= straight:
                got(pdiag.at[b : b + count], g_recv.at[i])
        for at in range(b, b + count):
            total = own[at]
            for side in range(2):
                total += precv[side, at].astype(f32)
            if b >= straight:
                total += pdiag[at].astype(f32)
            out_ref = (bk_ref, bv_ref)[at // heads]
            for r in range(requests):
                live = (slot_row + 1) * ratio_ref[r, s] <= interval
                out_ref[at % heads, r * nb : (r + 1) * nb] = jnp.where(
                    live, total[r * nb : (r + 1) * nb], 0.0
                ).astype(bf16)

    def times(zi, to, b, count):
        return jnp.dot(
            act[zi, :, to].reshape(requests * nb, act.shape[4]),
            jnp.concatenate([wbuf[zi, at] for at in range(b, b + count)], axis=1),
            preferred_element_type=f32,
        )

    ahead = units[key_units + 1][0]

    def near_products():
        near = jnp.where(z == 0, 0, 1)
        for i in range(key_units + 1, len(units)):
            w_wait(i, 0, depth - 2)
        for b in range(ahead, blocks, 2):

            def step(to, carry, b=b):
                total = times(near, to, b, 2)
                for zi in range(1, depth - 1):
                    total += times(near + zi, to, b, 2)
                for at in range(2):
                    acc[to, b - ahead + at] = total[:, at * hd : (at + 1) * hd]
                return carry

            with region("near"):
                lax.fori_loop(0, B, step, 0)

    def product(i, late):
        b, count = units[i]

        def step(o, carry):
            to = jnp.where(o == 0, across, jnp.where(o == 1, x_side, jnp.where(o == 2, y_side, me)))
            if late:
                total = jnp.concatenate([acc[to, b - ahead + at] for at in range(count)], axis=1)
                total += times(far, to, b, count)
            else:
                total = times(0, to, b, count)
                for zi in range(1, depth):
                    total += times(zi, to, b, count)

            def part_of(at):
                return total[:, (at - b) * hd : (at - b + 1) * hd]

            @pl.when(o == 0)
            def _():
                for at in range(b, b + count):
                    psend[0, at] = part_of(at).astype(bf16)
                    p_copy(0, at).start()

            for side in range(2):

                @pl.when(o == 1 + side)
                def _(side=side):
                    for at in range(b, b + count):
                        if at >= straight:
                            psend[1 + side, at] = part_of(at).astype(bf16)
                            p_copy(1 + side, at).start()
                        elif at % 2 == side:
                            psend[1, at] = part_of(at).astype(bf16)
                            p_copy(1, at).start()
                        else:
                            hold[at] = part_of(at)

            @pl.when(o == B - 1)
            def _():
                for at in range(b, b + count):
                    own[at] = part_of(at)

            return carry

        with region(f"prod{i}"):
            lax.fori_loop(0, B, step, 0, unroll=B if late else 1)

    def forward(i):
        b, count = units[i]
        if b >= straight:
            return
        with region(f"forward{i}"):
            got(pdiag.at[b : b + count], g_recv.at[i])
            for at in range(b, b + count):
                psend[2, at] = (hold[at] + pdiag[at].astype(f32)).astype(bf16)
                p_copy(2, at).start()

    res = rk_ref.shape[2]
    qrows = dq_ref.shape[1]
    mergers = snd.shape[0]
    share = G * heads // mergers
    slots = hd // (2 * share)
    per_head = G // share
    first_merger = (depth // 2) * B - mergers // 2
    mine = s - first_merger
    merges = (mine >= 0) & (mine < mergers)

    def e_copy(to):
        return remote(snd_stats.at[to], rcv_stats.at[s], e_send, e_recv, first_merger + to)

    def d_copy(to):
        return remote(snd.at[to], rcv.at[s], d_send, d_recv, first_merger + to)

    def to_mergers(copy, first, end):
        for to in range(first, end):

            @pl.when(mine != to)
            def _(to=to):
                copy(to).start()

    def scored(k, r, key, mask):
        scores = lax.dot_general(
            dq_ref[k], key, (((1,), (1,)), ((), ())), preferred_element_type=f32
        )
        return jnp.where(mask, scores * inv_root, masked_score)

    def row_of(count):
        return (
            lax.rem(lax.broadcasted_iota(jnp.int32, (qrows, count), 0), requests),
            lax.broadcasted_iota(jnp.int32, (qrows, count), 1),
        )

    def decode_early():
        row_request, cell = row_of(res)
        row_rim, rim = row_of(OFF)
        last = jnp.where(s == n - 1, 1, 0)
        for k in range(heads):
            pieces = []
            for r in range(requests):
                usable = (cell < rlen_ref[r, s]) & (row_request == r)
                pieces.append((scored(k, r, rk_ref[r, k], usable), rv_ref, r, slice(0, res)))
                usable = (rim >= OFF - phase_ref[r] * last) & (row_rim == r)
                left = slice(rows - OFF, rows)
                pieces.append((scored(k, r, kbuf[r, k, left], usable), vbuf, r, left))
            peak = jnp.max(pieces[0][0], axis=-1, keepdims=True)
            for piece in pieces[1:]:
                peak = jnp.maximum(peak, jnp.max(piece[0], axis=-1, keepdims=True))
            total = jnp.zeros((qrows, 1), f32)
            out = jnp.zeros((qrows, hd), f32)
            for scores, source, r, span in pieces:
                weights = jnp.exp(scores - peak)
                total += jnp.sum(weights, axis=-1, keepdims=True)
                out += jnp.dot(weights.astype(bf16), source[r, k, span], preferred_element_type=f32)
            dacc[k] = out
            dstat[k, 0] = jnp.broadcast_to(peak, (qrows, hd))
            dstat[k, 1] = jnp.broadcast_to(total, (qrows, hd))

    def decode_weights():
        row_request, slot = row_of(nb)
        for k in range(heads):
            pieces = []
            for r in range(requests):
                usable = ((slot + 1) * ratio_ref[r, s] <= interval) & (row_request == r)
                pieces.append(scored(k, r, bk_ref[k, r * nb : (r + 1) * nb], usable))
            former = dstat[k, 0]
            peak = former
            for piece in pieces:
                peak = jnp.maximum(peak, jnp.max(piece, axis=-1, keepdims=True))
            scale = jnp.exp(former - peak)
            total = dstat[k, 1] * scale
            for r in range(requests):
                weights = jnp.exp(pieces[r] - peak)
                total += jnp.sum(weights, axis=-1, keepdims=True)
                dlow[k, r] = weights.astype(bf16)
            dacc[k] = dacc[k] * scale
            lane = lax.broadcasted_iota(jnp.int32, (qrows, hd), 1)
            stats = jnp.where(lax.rem(lane // slots, 2) == 0, peak, total)
            stats = stats.reshape(per_head, share, pair, hd)
            lane = lax.broadcasted_iota(jnp.int32, (per_head, pair, hd), 2)
            packed = stats[:, 0]
            for j in range(1, share):
                packed = jnp.where(lane >= 2 * slots * j, stats[:, j], packed)
            snd_stats[k * per_head : (k + 1) * per_head] = packed
        to_mergers(e_copy, 0, mergers)

    def decode_values(k):
        out = dacc[k]
        for r in range(requests):
            out += jnp.dot(
                dlow[k, r], bv_ref[k, r * nb : (r + 1) * nb], preferred_element_type=f32
            )
        snd[k * per_head : (k + 1) * per_head] = out.reshape(per_head, share * pair, hd).astype(bf16)
        to_mergers(d_copy, k * per_head, (k + 1) * per_head)

    outs = []

    def emit(made, made_rows, out):
        made_rows[...] = jnp.swapaxes(made[...], 0, 1)
        outs.append(pltpu.make_async_copy(made_rows, out, out_sem.at[len(outs)]))
        outs[-1].start()

    for i in range(len(units)):

        @pl.when(ends)
        def _(i=i):
            late = i > key_units
            if i == key_units + 1:
                near_products()
            with region(f"wwait{i}"):
                w_wait(i, depth - 2 if late else 0, depth - 1)
            product(i, late)
            if i <= key_units:
                forward(i)
            elif i > key_units + 1:
                forward(i - 1)

        @pl.when(jnp.logical_not(ends))
        def _(i=i):
            if i == key_units:
                w_relay(2, 3)
                w_relay(2, 4)
            product(i, False)
            if i > 0:
                forward(i - 1)

        if i == 1:
            with region("early"):
                decode_early()
    forward(len(units) - 1)
    for i in range(key_units):
        finish(i)
    with region("decode"):
        decode_weights()
    for i in range(key_units, len(units)):
        finish(i)
        b, count = units[i]
        with region("values"):
            for at in range(b, b + count):
                decode_values(at - heads)

    emit(bk_ref, bk_rows, bk_out)
    emit(bv_ref, bv_rows, bv_out)

    with region("drain"):
        sent(psend, s_send)
        sent(act.at[:2], p_send)
        sent(stage.at[: requests * heads * (B - 1) // B], a_send)
        for way in range(2):
            for d in range(depth - 1):
                shard, target, there = w_out(way, d)

                @pl.when(there)
                def _(way=way, d=d, shard=shard):
                    sent(wbuf.at[shard], w_send.at[way, d])

        @pl.when((me < B - 1) | crosses)
        def _():
            sent(rimraw, rim_send)

        @pl.when(relays)
        def _():
            sent(rimrel, rel_send)

    early = mergers - mergers // heads
    late = jnp.where(mine >= early, 1, 0)

    def t_copy(to):
        return remote(att.at[mine], att.at[mine], t_send, t_recv.at[late], to)

    with region("merge"):

        @pl.when(merges)
        def _():
            rcv[s] = snd[mine]
            rcv_stats[s] = snd_stats[mine]
            got(rcv_stats.at[: n - 1], e_recv)
            shares = []
            for j in range(share):
                at = 2 * slots * j
                peaks = rcv_stats[:, :, at : at + 1]
                scale = jnp.exp(peaks - jnp.max(peaks, axis=0, keepdims=True))
                total = jnp.sum(scale * rcv_stats[:, :, at + slots : at + slots + 1], axis=0)
                shares.append((scale, total))
            got(rcv.at[: n - 1], d_recv)
            landed = rcv[...].astype(f32)
            attended = []
            for j, (scale, total) in enumerate(shares):
                mixed = jnp.sum(scale * landed[:, j * pair : (j + 1) * pair], axis=0)
                attended.append(mixed / total)
            att[mine] = jnp.concatenate(attended, axis=0).astype(bf16)
            for to in range(n):

                @pl.when(to != s)
                def _(to=to):
                    t_copy(to).start()

            sent(snd.at[: mergers - 1], d_send)
            sent(snd_stats.at[: mergers - 1], e_send)

        @pl.when(jnp.logical_not(merges))
        def _():
            sent(snd, d_send)
            sent(snd_stats, e_send)

    ow_load.wait()

    def attended_rows(first, end, group):
        @pl.when(merges & (late == group))
        def _():
            got(att.at[first : end - 1], t_recv.at[group])

        @pl.when(jnp.logical_not(merges & (late == group)))
        def _():
            got(att.at[first:end], t_recv.at[group])

        wide = [att[i].astype(f32) for i in range(first, end)]
        vectors = jnp.concatenate(
            [piece[j * pair : (j + 1) * pair] for piece in wide for j in range(share)], axis=1
        ).astype(bf16)
        span = share * hd
        return jnp.dot(vectors, owbuf[first * span : end * span], preferred_element_type=f32)

    with region("twait"):
        sums = attended_rows(0, early, 0)
    with region("twait2"):
        sums += attended_rows(early, mergers, 1)
    part[...] = sums
    swap = remote(part, part_out.at[h], h_send, h_recv)
    swap.start()
    outs.append(pltpu.make_async_copy(part, part_out.at[h], out_sem.at[len(outs)]))
    outs[-1].start()
    with region("swap"):

        @pl.when(merges)
        def _():
            sent(rcv.at[: n - 1], t_send)

        swap.wait()
        for copy in outs:
            copy.wait()


def handed_on(keys_ref, values_ref, part_ref, keys_out, values_out, projected_out):
    keys_out[...] = keys_ref[...]
    values_out[...] = values_ref[...]
    summed = (part_ref[0] + part_ref[1]).astype(projected_out.dtype)
    steps, requests, _ = projected_out.shape
    for t in range(steps):
        projected_out[t] = summed[t * requests : (t + 1) * requests]


def fused_body(
    shard_count,
    raw_keys,
    raw_values,
    phase,
    ratio,
    resident_len,
    beacon_queries,
    beacon_wk,
    beacon_wv,
    resident_keys,
    resident_values,
    decode_queries,
    out_weight,
):
    n = shard_count
    depth = n // B
    requests, interval, heads, hd = raw_keys.shape
    steps = decode_queries.shape[0]
    nb = beacon_queries.shape[1]
    rows = interval + OFF
    res = resident_keys.shape[1]
    feature, columns = beacon_wk.shape
    blocks = 2 * columns // hd
    units = blocks // 2 + 1
    pair = requests * steps
    mergers = min(2 * B, n)
    share = G * heads // mergers
    bf16, f32 = jnp.bfloat16, jnp.float32
    dma = pltpu.SemaphoreType.DMA
    smem = pl.BlockSpec(memory_space=pltpu.SMEM)
    anywhere = pl.BlockSpec(memory_space=pl.ANY)
    vmem = pl.BlockSpec(memory_space=pltpu.VMEM)
    keys, values, partial_sums = pl.pallas_call(
        functools.partial(fused_kernel, n),
        out_shape=(
            jax.ShapeDtypeStruct((requests * nb, heads, hd), bf16),
            jax.ShapeDtypeStruct((requests * nb, heads, hd), bf16),
            jax.ShapeDtypeStruct((2, pair, out_weight.shape[1]), f32),
        ),
        in_specs=[smem] * 3 + [anywhere] * 9,
        out_specs=(anywhere, anywhere, anywhere),
        scratch_shapes=[
            pltpu.VMEM(raw_keys.shape, bf16),
            pltpu.VMEM(raw_values.shape, bf16),
            pltpu.VMEM(beacon_queries.shape, bf16),
            pltpu.VMEM(resident_keys.shape, bf16),
            pltpu.VMEM(resident_values.shape, bf16),
            pltpu.VMEM(decode_queries.shape, bf16),
            pltpu.VMEM((2 * requests, OFF, heads, hd), bf16),
            pltpu.VMEM((OFF, heads, hd), bf16),
            pltpu.VMEM((requests, heads, rows, hd), bf16),
            pltpu.VMEM((requests, heads, rows, hd), bf16),
            pltpu.VMEM((G, nb, hd + nb), bf16),
            pltpu.VMEM((depth, blocks, feature, hd), bf16),
            pltpu.VMEM((depth, requests, B, nb, feature), bf16),
            pltpu.VMEM((requests * heads, 2, nb, feature), bf16),
            pltpu.VMEM((3, blocks, requests * nb, hd), bf16),
            pltpu.VMEM((2, blocks, requests * nb, hd), bf16),
            pltpu.VMEM((blocks, requests * nb, hd), bf16),
            pltpu.VMEM((blocks, requests * nb, hd), f32),
            pltpu.VMEM((blocks, requests * nb, hd), f32),
            pltpu.VMEM((B, blocks // 2, requests * nb, hd), f32),
            pltpu.VMEM((requests, rows, nb), bf16),
            pltpu.VMEM(out_weight.shape, bf16),
            pltpu.VMEM((requests, heads, res, hd), bf16),
            pltpu.VMEM((requests, heads, res, hd), bf16),
            pltpu.VMEM((heads, G * pair, hd), bf16),
            pltpu.VMEM((heads, requests * nb, hd), bf16),
            pltpu.VMEM((heads, requests * nb, hd), bf16),
            pltpu.VMEM((heads, G * pair, hd), f32),
            pltpu.VMEM((heads, 2, G * pair, hd), f32),
            pltpu.VMEM((heads, requests, G * pair, nb), bf16),
            pltpu.VMEM((mergers, share * pair, hd), bf16),
            pltpu.VMEM((mergers, pair, hd), f32),
            pltpu.VMEM((n, share * pair, hd), bf16),
            pltpu.VMEM((n, pair, hd), f32),
            pltpu.VMEM((mergers, share * pair, hd), bf16),
            pltpu.VMEM((pair, out_weight.shape[1]), f32),
            pltpu.VMEM((requests * nb, heads, hd), bf16),
            pltpu.VMEM((requests * nb, heads, hd), bf16),
            dma((2 * requests + 5,)),
            dma((units,)),
            dma((3,)),
            dma,
            dma((requests,)),
            dma,
            dma,
            dma((2, depth - 1)),
            dma((2, depth - 1, units)),
            dma,
            dma((2, requests)),
            dma((2, requests)),
            dma,
            dma,
            dma,
            dma((units,)),
            dma((units,)),
            dma,
            dma,
            dma,
            dma,
            dma,
            dma((2,)),
            dma,
            dma,
        ],
        compiler_params=pltpu.CompilerParams(
            collective_id=0, has_side_effects=True, vmem_limit_bytes=60 * 1024 * 1024
        ),
    )(
        phase,
        ratio,
        resident_len,
        raw_keys,
        raw_values,
        beacon_queries,
        beacon_wk,
        beacon_wv,
        resident_keys,
        resident_values,
        decode_queries,
        out_weight,
    )
    keys, values, projected = pl.pallas_call(
        handed_on,
        out_shape=(
            jax.ShapeDtypeStruct(keys.shape, bf16),
            jax.ShapeDtypeStruct(values.shape, bf16),
            jax.ShapeDtypeStruct((steps, requests, out_weight.shape[1]), bf16),
        ),
        in_specs=[vmem] * 3,
        out_specs=(vmem,) * 3,
    )(keys, values, partial_sums)
    return (
        keys.reshape(requests, nb, heads, hd),
        values.reshape(requests, nb, heads, hd),
        projected,
    )


def chosen_body(shard_count, head_count):
    def run(*arrays):
        requests, _, heads, hd = arrays[0].shape
        feature = arrays[6].shape[0]
        fits = (
            head_count == 2
            and shard_count == B * B
            and requests == 2
            and heads == B
            and 2 * feature == G * hd
        )
        return fused_body(shard_count, *arrays) if fits else body(*arrays)

    return run


def solution(mesh):
    return jax.shard_map(
        chosen_body(mesh.shape["seq"], mesh.shape["head"]),
        mesh=mesh,
        in_specs=(
            P(None, "seq", "head", None),
            P(None, "seq", "head", None),
            P(),
            P(),
            P(),
            P(None, "seq", "head", None, None),
            P("seq", "head"),
            P("seq", "head"),
            P(None, "seq", "head", None),
            P(None, "seq", "head", None),
            P(None, None, "head", None, None),
            P("head", "seq"),
        ),
        out_specs=(
            P(None, "seq", "head", None),
            P(None, "seq", "head", None),
            P(None, None, "seq"),
        ),
        check_vma=False,
    )
```
